32 devices in a mesh: row: 4 (over z), col: 8 (over y, x, core).
Axes of the slice: x: 2, y: 2, z: 4, core: 2. Of those that a mesh axis runs over, the one named last changes fastest.
Arguments:
- images: bfloat16 [16384, 2, 4096], P(('row', 'col')), may hold values from -320 to 320
- precision: float32 [16384], P(('row', 'col')), may hold values from 0.001 to 0.01
- templates: bfloat16 [128, 2, 4096], P(('row', 'col')), may hold values from -4 to 4
- template_id: int32 [128], replicated, may hold values from 0 to 127, as said below
- shift_table: int32 [128, 8], replicated, may hold values from 0 to 63, as said below
Outputs:
- updated: float32 [128, 2, 4096], P(('row', 'col'))
The draws below stay inside these ranges and needn't reach their ends.
Inputs may be any that keep to these rules, and one draw needn't show every extreme that they name: `template_id`: A permutation of 0 to 127. `shift_table`: each row holds 8 different shift numbers.
All inputs are finite; a program needn't handle non-finite values.
Results may differ from the reference program's by a relative error of at most 0.00058.
Values may be sent and summed in bfloat16 or wider, within the bound.
No kernel may reach another device: no remote copies, remote signals or barrier semaphores. Data moves between devices by JAX's collectives and lax.ppermute only.
A program may use at most 192 MiB of HBM per device.

```python
import math
import jax
import jax.numpy as jnp
from jax import lax

GRID = 64
HALF = 4096
K = 128
SH = 8
NSHIFT = 64
IMG_DEV = 512
IMAGES = 16384


def phase_tables_drawn(grid_side):
    coefficient = jnp.arange(grid_side * grid_side, dtype=jnp.int32)
    freq_x = coefficient // grid_side - grid_side // 2
    freq_y = coefficient % grid_side - grid_side // 2
    shift_number = jnp.arange(64, dtype=jnp.int32)
    step_x = shift_number // 8 - 4
    step_y = shift_number % 8 - 4
    phase_index = (step_x[:, None] * freq_x[None, :] + step_y[:, None] * freq_y[None, :]) % grid_side
    angle_value = phase_index.astype(jnp.float32) * (2.0 * math.pi / grid_side)
    return (jnp.cos(angle_value), jnp.sin(angle_value))


def shared_truth(key):
    base = jax.random.fold_in(key, 101)
    key_maps, key_order, key_shift = jax.random.split(base, 3)
    noise = jnp.clip(jax.random.normal(key_maps, (K, 2, HALF), jnp.float32), -5.0, 5.0)
    rough = jnp.exp(jax.random.uniform(jax.random.fold_in(key_maps, 3), (K, 2, HALF), jnp.float32, -0.7, 0.7))
    true_maps = noise * rough
    template_ids = jax.random.permutation(key_order, K).astype(jnp.int32)
    ranking = jax.random.randint(key_shift, (K, NSHIFT), 0, 1 << 20) * NSHIFT + jnp.arange(NSHIFT, dtype=jnp.int32)[None, :]
    shift_rows = jnp.argsort(ranking, axis=1)[:, :SH].astype(jnp.int32)
    return (true_maps, template_ids, shift_rows)


def draw_template_id(key, part):
    return shared_truth(key)[1]


def draw_shift_table(key, part):
    return shared_truth(key)[2]


def draw_templates(key, part):
    true_maps, template_ids, shift_rows = shared_truth(key)
    noise_key = jax.random.fold_in(key, 202)
    jitter = 0.15 * jnp.clip(jax.random.normal(noise_key, (K, 2, HALF), jnp.float32), -5.0, 5.0)
    return (0.3 * true_maps[template_ids] + jitter).astype(jnp.bfloat16)


def draw_images(key, part):
    true_maps, template_ids, shift_rows = shared_truth(key)
    cos_table, sin_table = phase_tables_drawn(GRID)

    def make_block(block_index):
        block_key = jax.random.fold_in(jax.random.fold_in(key, 303), block_index)
        key_pick, key_slot, key_noise = jax.random.split(block_key, 3)
        picked = jax.random.randint(key_pick, (IMG_DEV,), 0, K)
        slot_index = jax.random.randint(key_slot, (IMG_DEV,), 0, SH)
        shift_number = shift_rows[picked, slot_index]
        maps = true_maps[picked]
        cosine = cos_table[shift_number]
        sine_table = sin_table[shift_number]
        real_part = maps[:, 0] * cosine + maps[:, 1] * sine_table
        imag_part = maps[:, 1] * cosine - maps[:, 0] * sine_table
        signal = 0.3 * jnp.stack([real_part, imag_part], axis=1)
        noise = jnp.clip(jax.random.normal(key_noise, (IMG_DEV, 2, HALF), jnp.float32), -5.0, 5.0)
        return (signal + noise).astype(jnp.bfloat16)
    blocks = lax.map(make_block, jnp.arange(IMAGES // IMG_DEV, dtype=jnp.int32))
    return blocks.reshape(IMAGES, 2, HALF)


def levels(key, shape, pieces, low, top_value):
    def one(axis_at, parts):
        draws = jax.random.uniform(jax.random.fold_in(jax.random.fold_in(key, 6), axis_at), (parts,), jnp.float32, low / len(pieces), top_value / len(pieces))
        return jnp.repeat(jnp.exp(draws), shape[axis_at] // parts).reshape((-1,) + (1,) * (len(shape) - axis_at - 1))

    loudness = one(*pieces[0])
    for cut in pieces[1:]:
        loudness = loudness * one(*cut)
    return loudness


def setup_inputs(seed: int = 0) -> dict:
    splits = jax.random.split(jax.random.key(seed), 6)
    images = draw_images(jax.random.fold_in(splits[5], 71), 0)
    precision = jnp.clip(jnp.exp(math.log(0.01) - 2.30258502 * jax.random.uniform(splits[1], (IMAGES,), jnp.float32) ** levels(splits[1], (IMAGES,), ((0, 32),), -0.2, 0.2)), 0.001, 0.01)
    templates = draw_templates(jax.random.fold_in(splits[5], 71), 0)
    template_id = draw_template_id(jax.random.fold_in(splits[5], 71), 0)
    shift_table = draw_shift_table(jax.random.fold_in(splits[5], 71), 0)
    return dict(images=images, precision=precision, templates=templates, template_id=template_id, shift_table=shift_table)


PRIOR_WEIGHT = 4.0


def phase_tables(grid_side):
    coefficient = jnp.arange(grid_side * grid_side, dtype=jnp.int32)
    freq_x = coefficient // grid_side - grid_side // 2
    freq_y = coefficient % grid_side - grid_side // 2
    shift_number = jnp.arange(64, dtype=jnp.int32)
    step_x = shift_number // 8 - 4
    step_y = shift_number % 8 - 4
    phase_index = (step_x[:, None] * freq_x[None, :] + step_y[:, None] * freq_y[None, :]) % grid_side
    angle_value = phase_index.astype(jnp.float32) * (2.0 * math.pi / grid_side)
    return jnp.cos(angle_value), jnp.sin(angle_value)


def shift_forward(real_part, imag_part, cosine, sine_table):
    return real_part * cosine + imag_part * sine_table, imag_part * cosine - real_part * sine_table


def shift_back(real_part, imag_part, cosine, sine_table):
    return real_part * cosine - imag_part * sine_table, imag_part * cosine + real_part * sine_table


def reference(images, precision, templates, template_id, shift_table):
    cos_table, sin_table = phase_tables(GRID)
    template_f = templates.astype(jnp.float32)
    shift_rows = shift_table[template_id]
    cosine = cos_table[shift_rows]
    sine_table = sin_table[shift_rows]
    real_part, imag_part = shift_forward(template_f[:, None, 0], template_f[:, None, 1], cosine, sine_table)
    rotated = jnp.stack([real_part, imag_part], axis=2).astype(jnp.bfloat16).reshape(K * SH, 2 * HALF)
    half_norm = jnp.repeat(0.5 * jnp.sum(template_f * template_f, axis=(1, 2)), SH)
    image_blocks = images.reshape(IMAGES // IMG_DEV, IMG_DEV, 2 * HALF)
    precision_blocks = precision.reshape(IMAGES // IMG_DEV, IMG_DEV)

    def scan_step(state_pair, block_pair):
        numerator, denominator = state_pair
        image_rows, block_precision = block_pair
        inner_products = jnp.dot(image_rows, rotated.T, preferred_element_type=jnp.float32)
        scores = block_precision[:, None] * (inner_products - half_norm[None, :])
        highest = jnp.max(scores, axis=1, keepdims=True)
        exponent = jnp.exp(scores - highest)
        weights = (exponent / jnp.sum(exponent, axis=1, keepdims=True)).astype(jnp.bfloat16)
        numerator = numerator + jnp.dot(weights.T, image_rows, preferred_element_type=jnp.float32)
        denominator = denominator + jnp.sum(weights.astype(jnp.float32), axis=0)
        return (numerator, denominator), None

    initial = (jnp.zeros((K * SH, 2 * HALF), jnp.float32), jnp.zeros((K * SH,), jnp.float32))
    (numerator, denominator), _ = lax.scan(scan_step, initial, (image_blocks, precision_blocks))
    numerator = numerator.reshape(K, SH, 2, HALF)
    back_real, back_imag = shift_back(numerator[:, :, 0], numerator[:, :, 1], cosine, sine_table)
    summed = jnp.stack([jnp.sum(back_real, axis=1), jnp.sum(back_imag, axis=1)], axis=1)
    totals = jnp.sum(denominator.reshape(K, SH), axis=1)
    return (summed + PRIOR_WEIGHT * template_f) / (totals + PRIOR_WEIGHT)[:, None, None]
```

```python
import functools
import math

import jax
import jax.numpy as jnp
from jax import lax
from jax.experimental import pallas as pl
from jax.experimental.pallas import tpu as pltpu
from jax.sharding import PartitionSpec as P

GRID = 64
PRIOR_WEIGHT = 4.0
LANES = 128
PAIR = 2 * LANES
AG_CHUNKS = 2
RS_CHUNKS = 4
WIRE = jnp.float32


def relay_kernel(in_ref, out_ref, wide_ref):
    count, width = out_ref.shape
    per = width // LANES
    wide_ref[...] = in_ref[...].astype(jnp.float32)
    for r in range(per):
        rows = wide_ref[pl.ds(r, count, stride=per), :]
        out_ref[:, r * LANES : (r + 1) * LANES] = rows.astype(jnp.bfloat16)


def relay(images):
    count, parts, coeffs = images.shape
    groups = coeffs // LANES
    block = min(count, 64)
    per = parts * groups
    flat = images.reshape(count, parts, groups, LANES)
    flat = flat.transpose(0, 2, 1, 3).reshape(count * per, LANES)
    return pl.pallas_call(
        relay_kernel,
        grid=(count // block,),
        in_specs=[pl.BlockSpec((block * per, LANES), lambda i: (i, 0))],
        out_specs=pl.BlockSpec((block, per * LANES), lambda i: (i, 0)),
        out_shape=jax.ShapeDtypeStruct((count, per * LANES), jnp.bfloat16),
        scratch_shapes=[pltpu.VMEM((block * per, LANES), jnp.float32)],
        cost_estimate=pl.CostEstimate(
            flops=count * per * LANES,
            bytes_accessed=4 * count * per * LANES,
            transcendentals=0,
        ),
    )(flat)


def score_kernel(pieces, groups, has_sum, *refs):
    piece_refs = refs[:pieces]
    cos0, sin0, cos_step, sin_step, x_ref = refs[pieces : pieces + 5]
    rest = refs[pieces + 5 :]
    if has_sum:
        sum_ref, rest = rest[0], rest[1:]
    out_ref, cos_ref, sin_ref, rot_ref = rest
    shifts, held, _ = cos0.shape
    step = pl.program_id(0)

    @pl.when(step == 0)
    def _():
        cos_ref[...] = cos0[...]
        sin_ref[...] = sin0[...]
        if has_sum:
            out_ref[...] = sum_ref[...]
        else:
            out_ref[...] = jnp.zeros_like(out_ref)

    piece_rows = held // pieces
    for g in range(groups):
        at = g * PAIR
        for i in range(pieces):
            here = slice(i * piece_rows, (i + 1) * piece_rows)
            real = piece_refs[i][:, at : at + LANES].astype(jnp.float32)
            imag = piece_refs[i][:, at + LANES : at + PAIR].astype(jnp.float32)
            for j in range(shifts):
                c, s = cos_ref[j, here, :], sin_ref[j, here, :]
                dc, ds = cos_step[j, here, :], sin_step[j, here, :]
                row = slice(j * held + i * piece_rows, j * held + (i + 1) * piece_rows)
                rot_ref[row, at : at + LANES] = (real * c + imag * s).astype(jnp.bfloat16)
                rot_ref[row, at + LANES : at + PAIR] = (imag * c - real * s).astype(
                    jnp.bfloat16
                )
                cos_ref[j, here, :] = c * dc - s * ds
                sin_ref[j, here, :] = s * dc + c * ds
        if (g + 1) % 2 == 0:
            span = slice((g - 1) * PAIR, (g + 1) * PAIR)
            out_ref[...] += lax.dot_general(
                rot_ref[:, span],
                x_ref[:, span],
                (((1,), (1,)), ((), ())),
                preferred_element_type=jnp.float32,
            )


def scores_of(piece_list, phases, steps, half, x, chunk, chunks, so_far, groups=4):
    pieces = len(piece_list)
    rows, width = piece_list[0].shape
    held = pieces * rows
    shifts = phases[0].shape[0]
    images = x.shape[0]
    block = groups * PAIR
    count = width // block
    whole = pl.BlockSpec((shifts, held, LANES), lambda i: (0, half, 0))
    out_spec = pl.BlockSpec((shifts * held, images), lambda i: (0, 0))
    in_specs = [pl.BlockSpec((rows, block), lambda i: (0, i))] * pieces
    in_specs += [whole] * 4
    in_specs += [pl.BlockSpec((images, block), lambda i: (0, chunk * count + i))]
    operands = list(piece_list) + list(phases) + list(steps) + [x]
    if so_far is not None:
        in_specs += [out_spec]
        operands += [so_far]
    return pl.pallas_call(
        functools.partial(score_kernel, pieces, groups, so_far is not None),
        grid=(count,),
        in_specs=in_specs,
        out_specs=out_spec,
        out_shape=jax.ShapeDtypeStruct((shifts * held, images), jnp.float32),
        scratch_shapes=[
            pltpu.VMEM((shifts, held, LANES), jnp.float32),
            pltpu.VMEM((shifts, held, LANES), jnp.float32),
            pltpu.VMEM((shifts * held, block), jnp.bfloat16),
        ],
        cost_estimate=pl.CostEstimate(
            flops=2 * shifts * held * images * width,
            bytes_accessed=2 * images * width + 8 * shifts * held * images,
            transcendentals=0,
        ),
    )(*operands)


def weight_kernel(own_ref, other_ref, norm_ref, prec_ref, *outs):
    shifts = own_ref.shape[0]
    halves = (own_ref, other_ref)
    prec = prec_ref[...][None]
    top = None
    scaled = []
    for h, ref in enumerate(halves):
        held = ref.shape[1]
        value = prec * (ref[...] - norm_ref[h * held : (h + 1) * held, 0:1][None])
        scaled.append(value)
        best = jnp.max(value, axis=(0, 1), keepdims=True)
        top = best if top is None else jnp.maximum(top, best)
    raised = [jnp.exp(value - top) for value in scaled]
    norm = sum(jnp.sum(value, axis=(0, 1), keepdims=True) for value in raised)
    inverse = 1.0 / norm
    for h, value in enumerate(raised):
        weight = (value * inverse).astype(jnp.bfloat16)
        outs[h][...] = weight
        wide = weight.astype(jnp.float32)
        total = jnp.sum(jnp.sum(wide, axis=0), axis=1, keepdims=True)
        outs[2 + h][...] = jnp.broadcast_to(total, outs[2 + h].shape)


def weights_of(own, other, half_norm, precision, shifts):
    rows, images = own.shape
    held = rows // shifts
    norm = jnp.broadcast_to(half_norm[:, None], (2 * held, LANES))
    cube = jax.ShapeDtypeStruct((shifts, held, images), jnp.bfloat16)
    total = jax.ShapeDtypeStruct((held, LANES), jnp.float32)
    own_w, other_w, own_t, other_t = pl.pallas_call(
        weight_kernel,
        out_shape=(cube, cube, total, total),
        cost_estimate=pl.CostEstimate(
            flops=20 * rows * images,
            bytes_accessed=12 * rows * images,
            transcendentals=2 * rows * images,
        ),
    )(
        own.reshape(shifts, held, images),
        other.reshape(shifts, held, images),
        norm,
        precision.reshape(1, images),
    )
    return own_w.reshape(rows, images), other_w.reshape(rows, images), own_t, other_t


def back_kernel(groups, w_ref, x_ref, cos0, sin0, cos_step, sin_step, out_ref, cos_ref, sin_ref):
    shifts, held, _ = cos0.shape
    step = pl.program_id(0)

    @pl.when(step == 0)
    def _():
        cos_ref[...] = cos0[...]
        sin_ref[...] = sin0[...]

    for g in range(groups):
        at = g * PAIR
        mixed = jnp.dot(
            w_ref[...], x_ref[:, at : at + PAIR], preferred_element_type=jnp.float32
        )
        for i in range(held // 8):
            here = slice(i * 8, (i + 1) * 8)
            back_real = jnp.zeros((8, LANES), jnp.float32)
            back_imag = jnp.zeros((8, LANES), jnp.float32)
            for j in range(shifts):
                row = slice(j * held + i * 8, j * held + (i + 1) * 8)
                c, s = cos_ref[j, here, :], sin_ref[j, here, :]
                dc, ds = cos_step[j, here, :], sin_step[j, here, :]
                real, imag = mixed[row, :LANES], mixed[row, LANES:]
                back_real = back_real + (real * c - imag * s)
                back_imag = back_imag + (imag * c + real * s)
                cos_ref[j, here, :] = c * dc - s * ds
                sin_ref[j, here, :] = s * dc + c * ds
            out_ref[here, at : at + LANES] = back_real.astype(out_ref.dtype)
            out_ref[here, at + LANES : at + PAIR] = back_imag.astype(out_ref.dtype)


def back_of(weight, x, phases, steps, half, chunk, chunks, groups=4):
    rows, images = weight.shape
    shifts = phases[0].shape[0]
    held = rows // shifts
    width = x.shape[1] // chunks
    groups = min(groups, width // PAIR)
    block = groups * PAIR
    count = width // block
    whole = pl.BlockSpec((shifts, held, LANES), lambda i: (0, half, 0))
    return pl.pallas_call(
        functools.partial(back_kernel, groups),
        grid=(count,),
        in_specs=[
            pl.BlockSpec((rows, images), lambda i: (0, 0)),
            pl.BlockSpec((images, block), lambda i: (0, chunk * count + i)),
        ]
        + [whole] * 4,
        out_specs=pl.BlockSpec((held, block), lambda i: (0, i)),
        out_shape=jax.ShapeDtypeStruct((held, width), jnp.float32),
        scratch_shapes=[
            pltpu.VMEM((shifts, held, LANES), jnp.float32),
            pltpu.VMEM((shifts, held, LANES), jnp.float32),
        ],
        cost_estimate=pl.CostEstimate(
            flops=2 * rows * images * width,
            bytes_accessed=2 * images * width + 2 * rows * images + 4 * held * width,
            transcendentals=0,
        ),
    )(weight, x, *phases, *steps)


def unit(phase_index):
    angle = phase_index.astype(jnp.float32) * (2.0 * math.pi / GRID)
    return jnp.cos(angle), jnp.sin(angle)


def exchange(value, axis, size, bit):
    return lax.ppermute(value, axis, [(i, i ^ bit) for i in range(size)])


def body(images, precision, templates, template_id, shift_table):
    image_count, parts, coeffs = images.shape
    local = templates.shape[0]
    shifts = shift_table.shape[1]
    rows, cols = lax.axis_size("row"), lax.axis_size("col")
    quads = cols // 2
    groups = coeffs // LANES
    width = parts * coeffs
    held = local * rows * quads

    mine = templates.reshape(local, parts, groups, LANES)
    mine = mine.transpose(0, 2, 1, 3).reshape(local, width)

    own_sets, other_sets = [], []
    for a in range(AG_CHUNKS):
        span = width // AG_CHUNKS
        piece = mine[:, a * span : (a + 1) * span]
        row_set = [piece] + [exchange(piece, "row", rows, d) for d in range(1, rows)]
        row_set = jnp.concatenate(row_set, axis=0)
        own = [row_set]
        own += [exchange(row_set, "col", cols, 2 * d) for d in range(1, quads)]
        own_sets.append(own)
        other_sets.append([exchange(value, "col", cols, 1) for value in own])

    x = relay(images)

    position = jnp.arange(2 * held, dtype=jnp.int32)
    at_local = position % local
    at_row = (position // local % rows) ^ lax.axis_index("row")
    at_quad = position // (local * rows) % quads
    at_col = (2 * at_quad + position // held) ^ lax.axis_index("col")
    slots = (at_row * cols + at_col) * local + at_local
    shift = shift_table[template_id[slots]].T[:, :, None]
    step_x, step_y = shift // 8 - 4, shift % 8 - 4
    lane = jnp.arange(LANES, dtype=jnp.int32)[None, None, :]

    def phases_at(group):
        coefficient = group * LANES + lane
        freq_x = coefficient // GRID - GRID // 2
        freq_y = coefficient % GRID - GRID // 2
        return unit((step_x * freq_x + step_y * freq_y) % GRID)

    per_group = LANES // GRID
    steps = unit(jnp.broadcast_to(step_x * per_group % GRID, (shifts, 2 * held, LANES)))

    own_scores = other_scores = None
    for a in range(AG_CHUNKS):
        start = phases_at(a * groups // AG_CHUNKS)
        own_scores = scores_of(
            own_sets[a], start, steps, 0, x, a, AG_CHUNKS, own_scores
        )
        other_scores = scores_of(
            other_sets[a], start, steps, 1, x, a, AG_CHUNKS, other_scores
        )

    half_norm = 0.0
    for a in range(AG_CHUNKS):
        value = jnp.concatenate(own_sets[a] + other_sets[a], axis=0).astype(jnp.float32)
        half_norm = half_norm + 0.5 * jnp.sum(value * value, axis=1)
    own_w, other_w, own_total, other_total = weights_of(
        own_scores, other_scores, half_norm, precision, shifts
    )

    def reduce_to_owner(own, other, wire):
        def send(value, axis, size, bit):
            return exchange(value.astype(wire), axis, size, bit).astype(jnp.float32)

        total = own + send(other, "col", cols, 1)
        per = local * rows
        part = total[:per]
        for d in range(1, quads):
            part = part + send(total[d * per : (d + 1) * per], "col", cols, 2 * d)
        out = part[:local]
        for d in range(1, rows):
            out = out + send(part[d * local : (d + 1) * local], "row", rows, d)
        return out

    totals = reduce_to_owner(own_total, other_total, jnp.float32)
    scale = 1.0 / (totals[:, :1] + PRIOR_WEIGHT)
    results = []
    for b in range(RS_CHUNKS):
        start = phases_at(b * groups // RS_CHUNKS)
        other = back_of(other_w, x, start, steps, 1, b, RS_CHUNKS)
        own = back_of(own_w, x, start, steps, 0, b, RS_CHUNKS)
        span = width // RS_CHUNKS
        summed = reduce_to_owner(own, other, WIRE)
        prior = mine[:, b * span : (b + 1) * span].astype(jnp.float32)
        results.append((summed + PRIOR_WEIGHT * prior) * scale)
    out = jnp.concatenate(results, axis=1)
    out = out.reshape(local, groups, parts, LANES).transpose(0, 2, 1, 3)
    return out.reshape(local, parts, coeffs)


def solution(mesh):
    return jax.shard_map(
        body,
        mesh=mesh,
        in_specs=(
            P(("row", "col"), None, None),
            P(("row", "col")),
            P(("row", "col"), None, None),
            P(),
            P(),
        ),
        out_specs=P(("row", "col"), None, None),
        check_vma=False,
    )
```

```python
import functools
import math

import jax
import jax.numpy as jnp
from jax import lax
from jax.experimental import pallas as pl
from jax.experimental.pallas import tpu as pltpu
from jax.sharding import PartitionSpec as P


GRID = 64
SHIFT_SIDE = 8
PRIOR_WEIGHT = 4.0
LANES = 128
PAIR = 2 * LANES
RS_CHUNKS = 1
WIRE = jnp.float32
VMEM_LIMIT = 24 << 20

PARAMS = pltpu.CompilerParams(vmem_limit_bytes=VMEM_LIMIT)


def relay_kernel(in_ref, out_ref, wide_ref):
    count, rows, _ = in_ref.shape
    wide_ref[...] = in_ref[...].astype(jnp.float32).reshape(count * rows, LANES)
    for r in range(rows):
        picked = wide_ref[pl.ds(r, count, stride=rows), :]
        out_ref[:, r * LANES : (r + 1) * LANES] = picked.astype(jnp.bfloat16)


def relay(images, rows=8):
    count, parts, coeffs = images.shape
    groups = coeffs // LANES
    per = parts * groups
    flat = images.reshape(count, parts, groups, LANES)
    flat = flat.transpose(0, 2, 1, 3).reshape(count, per, LANES)
    return pl.pallas_call(
        relay_kernel,
        grid=(per // rows,),
        in_specs=[pl.BlockSpec((count, rows, LANES), lambda i: (0, i, 0))],
        out_specs=pl.BlockSpec((count, rows * LANES), lambda i: (0, i)),
        out_shape=jax.ShapeDtypeStruct((count, per * LANES), jnp.bfloat16),
        scratch_shapes=[pltpu.VMEM((count * rows, LANES), jnp.float32)],
        compiler_params=PARAMS,
        cost_estimate=pl.CostEstimate(
            flops=count * per * LANES,
            bytes_accessed=4 * count * per * LANES,
            transcendentals=0,
        ),
    )(flat)


def score_kernel(pieces, groups, *refs):
    piece_refs = refs[:pieces]
    cos0, sin0, cos_step, sin_step, x_ref = refs[pieces : pieces + 5]
    rest = refs[pieces + 5 :]
    out_ref, norm_ref, cos_ref, sin_ref, rot_ref = rest
    shifts, held, _ = cos0.shape
    step = pl.program_id(0)

    @pl.when(step == 0)
    def _():
        cos_ref[...] = cos0[...]
        sin_ref[...] = sin0[...]
        norm_ref[...] = jnp.zeros_like(norm_ref)
        out_ref[...] = jnp.zeros_like(out_ref)

    piece_rows = held // pieces
    for g in range(groups):
        at = g * PAIR
        for i in range(pieces):
            here = slice(i * piece_rows, (i + 1) * piece_rows)
            real = piece_refs[i][:, at : at + LANES].astype(jnp.float32)
            imag = piece_refs[i][:, at + LANES : at + PAIR].astype(jnp.float32)
            norm_ref[here, :] += real * real + imag * imag
            for j in range(shifts):
                c, s = cos_ref[j, here, :], sin_ref[j, here, :]
                dc, ds = cos_step[j, here, :], sin_step[j, here, :]
                row = slice(j * held + i * piece_rows, j * held + (i + 1) * piece_rows)
                rot_ref[row, at : at + LANES] = (real * c + imag * s).astype(jnp.bfloat16)
                rot_ref[row, at + LANES : at + PAIR] = (imag * c - real * s).astype(
                    jnp.bfloat16
                )
                cos_ref[j, here, :] = c * dc - s * ds
                sin_ref[j, here, :] = s * dc + c * ds
        if (g + 1) % 2 == 0:
            span = slice((g - 1) * PAIR, (g + 1) * PAIR)
            out_ref[...] += lax.dot_general(
                rot_ref[:, span],
                x_ref[:, span],
                (((1,), (1,)), ((), ())),
                preferred_element_type=jnp.float32,
            )


def scores_of(piece_list, phases, steps, half, x, groups=4):
    pieces = len(piece_list)
    rows, width = piece_list[0].shape
    held = pieces * rows
    shifts = phases[0].shape[0]
    images = x.shape[0]
    block = groups * PAIR
    count = width // block
    whole = pl.BlockSpec((shifts, held, LANES), lambda i: (0, half, 0))
    out_spec = pl.BlockSpec((shifts * held, images), lambda i: (0, 0))
    in_specs = [pl.BlockSpec((rows, block), lambda i: (0, i))] * pieces
    in_specs += [whole] * 4
    in_specs += [pl.BlockSpec((images, block), lambda i: (0, i))]
    return pl.pallas_call(
        functools.partial(score_kernel, pieces, groups),
        grid=(count,),
        in_specs=in_specs,
        out_specs=(out_spec, pl.BlockSpec((held, LANES), lambda i: (0, 0))),
        out_shape=(
            jax.ShapeDtypeStruct((shifts * held, images), jnp.float32),
            jax.ShapeDtypeStruct((held, LANES), jnp.float32),
        ),
        scratch_shapes=[
            pltpu.VMEM((shifts, held, LANES), jnp.float32),
            pltpu.VMEM((shifts, held, LANES), jnp.float32),
            pltpu.VMEM((shifts * held, block), jnp.bfloat16),
        ],
        compiler_params=PARAMS,
        cost_estimate=pl.CostEstimate(
            flops=2 * shifts * held * images * width,
            bytes_accessed=2 * images * width + 8 * shifts * held * images,
            transcendentals=0,
        ),
    )(*piece_list, *phases, *steps, x)


def weight_kernel(own_ref, other_ref, own_norm, other_norm, prec_ref, *outs):
    outs, raised_refs = outs[:4], outs[4:]
    prec = prec_ref[...][None]
    halves = ((own_ref, own_norm), (other_ref, other_norm))
    bias, tops = [], []
    for ref, norm_ref in halves:
        norm = 0.5 * jnp.sum(norm_ref[...], axis=1, keepdims=True)
        bias.append(norm[None])
        value = prec * (ref[...] - norm[None])
        tops.append(jnp.max(jnp.max(value, axis=0), axis=0, keepdims=True))
    top = jnp.maximum(*tops)[None]
    norm = 0.0
    for (ref, _), offset, raised_ref in zip(halves, bias, raised_refs):
        raised = jnp.exp(prec * (ref[...] - offset) - top)
        raised_ref[...] = raised
        norm = norm + jnp.sum(jnp.sum(raised, axis=0), axis=0, keepdims=True)
    inverse = (1.0 / norm)[None]
    for h, ref in enumerate(raised_refs):
        weight = (ref[...] * inverse).astype(jnp.bfloat16)
        outs[h][...] = weight
        wide = weight.astype(jnp.float32)
        total = jnp.sum(jnp.sum(wide, axis=0), axis=1, keepdims=True)
        outs[2 + h][...] = jnp.broadcast_to(total, outs[2 + h].shape)


def weights_of(own, other, precision, shifts):
    rows, images = own[0].shape
    held = rows // shifts
    cube = jax.ShapeDtypeStruct((shifts, held, images), jnp.bfloat16)
    total = jax.ShapeDtypeStruct((held, LANES), jnp.float32)
    own_w, other_w, own_t, other_t = pl.pallas_call(
        weight_kernel,
        out_shape=(cube, cube, total, total),
        scratch_shapes=[pltpu.VMEM((shifts, held, images), jnp.float32)] * 2,
        compiler_params=PARAMS,
        cost_estimate=pl.CostEstimate(
            flops=20 * rows * images,
            bytes_accessed=12 * rows * images,
            transcendentals=2 * rows * images,
        ),
    )(
        own[0].reshape(shifts, held, images),
        other[0].reshape(shifts, held, images),
        own[1],
        other[1],
        precision.reshape(1, images),
    )
    return own_w.reshape(rows, images), other_w.reshape(rows, images), own_t, other_t


def back_kernel(groups, w_ref, x_ref, cos0, sin0, cos_step, sin_step, out_ref, cos_ref, sin_ref):
    shifts, held, _ = cos0.shape
    step = pl.program_id(0)

    @pl.when(step == 0)
    def _():
        cos_ref[...] = cos0[...]
        sin_ref[...] = sin0[...]

    for g in range(groups):
        at = g * PAIR
        mixed = jnp.dot(
            w_ref[...], x_ref[:, at : at + PAIR], preferred_element_type=jnp.float32
        )
        for i in range(held // 8):
            here = slice(i * 8, (i + 1) * 8)
            back_real = jnp.zeros((8, LANES), jnp.float32)
            back_imag = jnp.zeros((8, LANES), jnp.float32)
            for j in range(shifts):
                row = slice(j * held + i * 8, j * held + (i + 1) * 8)
                c, s = cos_ref[j, here, :], sin_ref[j, here, :]
                dc, ds = cos_step[j, here, :], sin_step[j, here, :]
                real, imag = mixed[row, :LANES], mixed[row, LANES:]
                back_real = back_real + (real * c - imag * s)
                back_imag = back_imag + (imag * c + real * s)
                cos_ref[j, here, :] = c * dc - s * ds
                sin_ref[j, here, :] = s * dc + c * ds
            out_ref[here, at : at + LANES] = back_real.astype(out_ref.dtype)
            out_ref[here, at + LANES : at + PAIR] = back_imag.astype(out_ref.dtype)


def back_of(weight, x, phases, steps, half, chunk, chunks, groups=4):
    rows, images = weight.shape
    shifts = phases[0].shape[0]
    held = rows // shifts
    width = x.shape[1] // chunks
    groups = min(groups, width // PAIR)
    block = groups * PAIR
    count = width // block
    whole = pl.BlockSpec((shifts, held, LANES), lambda i: (0, half, 0))
    return pl.pallas_call(
        functools.partial(back_kernel, groups),
        grid=(count,),
        in_specs=[
            pl.BlockSpec((rows, images), lambda i: (0, 0)),
            pl.BlockSpec((images, block), lambda i: (0, chunk * count + i)),
        ]
        + [whole] * 4,
        out_specs=pl.BlockSpec((held, block), lambda i: (0, i)),
        out_shape=jax.ShapeDtypeStruct((held, width), jnp.float32),
        scratch_shapes=[
            pltpu.VMEM((shifts, held, LANES), jnp.float32),
            pltpu.VMEM((shifts, held, LANES), jnp.float32),
        ],
        compiler_params=PARAMS,
        cost_estimate=pl.CostEstimate(
            flops=2 * rows * images * width,
            bytes_accessed=2 * images * width + 2 * rows * images + 4 * held * width,
            transcendentals=0,
        ),
    )(weight, x, *phases, *steps)


def exchange(value, axis, size, bit):
    return lax.ppermute(value, axis, [(i, i ^ bit) for i in range(size)])


def body(images, precision, templates, template_id, shift_table):
    _, parts, coeffs = images.shape
    local = templates.shape[0]
    shifts = shift_table.shape[1]
    rows, cols = lax.axis_size("row"), lax.axis_size("col")
    quads = cols // 2
    groups = coeffs // LANES
    width = parts * coeffs
    held = local * rows * quads

    mine = templates.reshape(local, parts, groups, LANES)
    mine = mine.transpose(0, 2, 1, 3).reshape(local, width)

    row_set = [mine]
    row_set += [exchange(mine, "row", rows, d) for d in range(1, rows)]
    row_set = jnp.concatenate(row_set, axis=0)
    own_set = [row_set]
    own_set += [exchange(row_set, "col", cols, 2 * d) for d in range(1, quads)]
    other_set = [exchange(value, "col", cols, 1) for value in own_set]

    x = relay(images)

    position = jnp.arange(2 * held, dtype=jnp.int32)
    at_local = position % local
    at_row = (position // local % rows) ^ lax.axis_index("row")
    at_quad = position // (local * rows) % quads
    at_col = (2 * at_quad + position // held) ^ lax.axis_index("col")
    slots = (at_row * cols + at_col) * local + at_local
    shift = shift_table[template_id[slots]].T.reshape(-1, 1)

    number = jnp.arange(SHIFT_SIDE * SHIFT_SIDE, dtype=jnp.int32)[:, None]
    step_x = number // SHIFT_SIDE - SHIFT_SIDE // 2
    step_y = number % SHIFT_SIDE - SHIFT_SIDE // 2
    lane = jnp.arange(LANES, dtype=jnp.int32)[None, :]
    freq_x = lane // GRID - GRID // 2
    freq_y = lane % GRID - GRID // 2
    first = (step_x * freq_x + step_y * freq_y) % GRID
    stride = jnp.broadcast_to(step_x * (LANES // GRID) % GRID, first.shape)
    angle = jnp.concatenate([first, stride], axis=1).astype(jnp.float32)
    angle = angle * (2.0 * math.pi / GRID)
    table = jnp.concatenate([jnp.cos(angle), jnp.sin(angle)], axis=1)
    chosen = (shift == number.T).astype(jnp.float32)
    unit = []
    for at in range(4):
        part = lax.dot(
            chosen, table[:, at * LANES : (at + 1) * LANES], precision=lax.Precision.HIGHEST
        )
        unit.append(part.reshape(shifts, 2 * held, LANES))
    start, steps = (unit[0], unit[2]), (unit[1], unit[3])

    own_scores = scores_of(own_set, start, steps, 0, x)
    other_scores = scores_of(other_set, start, steps, 1, x)
    own_w, other_w, own_total, other_total = weights_of(
        own_scores, other_scores, precision, shifts
    )

    def reduce_to_owner(own, other, wire):
        def send(value, axis, size, bit):
            return exchange(value.astype(wire), axis, size, bit).astype(jnp.float32)

        got = send(other, "col", cols, 1)
        total = own + got
        per = local * rows
        part = total[:per]
        got = [
            send(total[d * per : (d + 1) * per], "col", cols, 2 * d)
            for d in range(1, quads)
        ]
        part = sum(got, part)
        got = [
            send(part[d * local : (d + 1) * local], "row", rows, d)
            for d in range(1, rows)
        ]
        return sum(got, part[:local])

    totals = reduce_to_owner(own_total, other_total, jnp.float32)
    results = []
    for b in range(RS_CHUNKS):
        other = back_of(other_w, x, start, steps, 1, b, RS_CHUNKS)
        own = back_of(own_w, x, start, steps, 0, b, RS_CHUNKS)
        span = width // RS_CHUNKS
        summed = reduce_to_owner(own, other, WIRE)
        prior = mine[:, b * span : (b + 1) * span].astype(jnp.float32)
        results.append((summed + PRIOR_WEIGHT * prior) / (totals[:, :1] + PRIOR_WEIGHT))
    out = results[0] if RS_CHUNKS == 1 else jnp.concatenate(results, axis=1)
    out = out.reshape(local, groups, parts, LANES).transpose(0, 2, 1, 3)
    return out.reshape(local, parts, coeffs)


def solution(mesh):
    return jax.shard_map(
        body,
        mesh=mesh,
        in_specs=(
            P(("row", "col"), None, None),
            P(("row", "col")),
            P(("row", "col"), None, None),
            P(),
            P(),
        ),
        out_specs=P(("row", "col"), None, None),
        check_vma=False,
    )
```

```python
import functools
import math

import jax
import jax.numpy as jnp
from jax import lax
from jax.experimental import pallas as pl
from jax.experimental.pallas import tpu as pltpu
from jax.sharding import PartitionSpec as P


GRID = 64
SHIFT_SIDE = 8
PRIOR_WEIGHT = 4.0
LANES = 128
PAIR = 2 * LANES
RS_CHUNKS = 1
WIRE = jnp.float16
VMEM_LIMIT = 24 << 20

PARAMS = pltpu.CompilerParams(vmem_limit_bytes=VMEM_LIMIT)


def relay_kernel(in_ref, out_ref, peak_ref, wide_ref):
    count, rows, _ = in_ref.shape
    wide = in_ref[...].astype(jnp.float32)
    wide_ref[...] = wide.reshape(count * rows, LANES)
    peak = jnp.max(jnp.abs(wide), axis=0)

    @pl.when(pl.program_id(0) == 0)
    def _():
        peak_ref[...] = jnp.zeros_like(peak_ref)

    peak_ref[...] = jnp.maximum(peak_ref[...], peak)
    for r in range(rows):
        picked = wide_ref[pl.ds(r, count, stride=rows), :]
        out_ref[:, r * LANES : (r + 1) * LANES] = picked.astype(jnp.bfloat16)


def relay(images, rows=8):
    count, parts, coeffs = images.shape
    groups = coeffs // LANES
    per = parts * groups
    flat = images.reshape(count, parts, groups, LANES)
    flat = flat.transpose(0, 2, 1, 3).reshape(count, per, LANES)
    return pl.pallas_call(
        relay_kernel,
        grid=(per // rows,),
        in_specs=[pl.BlockSpec((count, rows, LANES), lambda i: (0, i, 0))],
        out_specs=(
            pl.BlockSpec((count, rows * LANES), lambda i: (0, i)),
            pl.BlockSpec((rows, LANES), lambda i: (0, 0)),
        ),
        out_shape=(
            jax.ShapeDtypeStruct((count, per * LANES), jnp.bfloat16),
            jax.ShapeDtypeStruct((rows, LANES), jnp.float32),
        ),
        scratch_shapes=[pltpu.VMEM((count * rows, LANES), jnp.float32)],
        compiler_params=PARAMS,
        cost_estimate=pl.CostEstimate(
            flops=count * per * LANES,
            bytes_accessed=4 * count * per * LANES,
            transcendentals=0,
        ),
    )(flat)


def score_kernel(pieces, groups, *refs):
    piece_refs = refs[:pieces]
    cos0, sin0, cos_step, sin_step, x_ref = refs[pieces : pieces + 5]
    rest = refs[pieces + 5 :]
    out_ref, norm_ref, cos_ref, sin_ref, rot_ref = rest
    shifts, held, _ = cos0.shape
    step = pl.program_id(0)

    @pl.when(step == 0)
    def _():
        cos_ref[...] = cos0[...]
        sin_ref[...] = sin0[...]
        norm_ref[...] = jnp.zeros_like(norm_ref)
        out_ref[...] = jnp.zeros_like(out_ref)

    piece_rows = held // pieces
    for g in range(groups):
        at = g * PAIR
        for i in range(pieces):
            here = slice(i * piece_rows, (i + 1) * piece_rows)
            real = piece_refs[i][:, at : at + LANES].astype(jnp.float32)
            imag = piece_refs[i][:, at + LANES : at + PAIR].astype(jnp.float32)
            norm_ref[here, :] += real * real + imag * imag
            for j in range(shifts):
                c, s = cos_ref[j, here, :], sin_ref[j, here, :]
                dc, ds = cos_step[j, here, :], sin_step[j, here, :]
                row = slice(j * held + i * piece_rows, j * held + (i + 1) * piece_rows)
                rot_ref[row, at : at + LANES] = (real * c + imag * s).astype(jnp.bfloat16)
                rot_ref[row, at + LANES : at + PAIR] = (imag * c - real * s).astype(
                    jnp.bfloat16
                )
                cos_ref[j, here, :] = c * dc - s * ds
                sin_ref[j, here, :] = s * dc + c * ds
        if (g + 1) % 2 == 0:
            span = slice((g - 1) * PAIR, (g + 1) * PAIR)
            out_ref[...] += lax.dot_general(
                rot_ref[:, span],
                x_ref[:, span],
                (((1,), (1,)), ((), ())),
                preferred_element_type=jnp.float32,
            )


def scores_of(piece_list, phases, steps, half, x, groups=4):
    pieces = len(piece_list)
    rows, width = piece_list[0].shape
    held = pieces * rows
    shifts = phases[0].shape[0]
    images = x.shape[0]
    block = groups * PAIR
    count = width // block
    whole = pl.BlockSpec((shifts, held, LANES), lambda i: (0, half, 0))
    out_spec = pl.BlockSpec((shifts * held, images), lambda i: (0, 0))
    in_specs = [pl.BlockSpec((rows, block), lambda i: (0, i))] * pieces
    in_specs += [whole] * 4
    in_specs += [pl.BlockSpec((images, block), lambda i: (0, i))]
    return pl.pallas_call(
        functools.partial(score_kernel, pieces, groups),
        grid=(count,),
        in_specs=in_specs,
        out_specs=(out_spec, pl.BlockSpec((held, LANES), lambda i: (0, 0))),
        out_shape=(
            jax.ShapeDtypeStruct((shifts * held, images), jnp.float32),
            jax.ShapeDtypeStruct((held, LANES), jnp.float32),
        ),
        scratch_shapes=[
            pltpu.VMEM((shifts, held, LANES), jnp.float32),
            pltpu.VMEM((shifts, held, LANES), jnp.float32),
            pltpu.VMEM((shifts * held, block), jnp.bfloat16),
        ],
        compiler_params=PARAMS,
        cost_estimate=pl.CostEstimate(
            flops=2 * shifts * held * images * width,
            bytes_accessed=2 * images * width + 8 * shifts * held * images,
            transcendentals=0,
        ),
    )(*piece_list, *phases, *steps, x)


def weight_kernel(own_ref, other_ref, own_norm, other_norm, prec_ref, *outs):
    outs, raised_refs = outs[:4], outs[4:]
    prec = prec_ref[...][None]
    halves = ((own_ref, own_norm), (other_ref, other_norm))
    bias, tops = [], []
    for ref, norm_ref in halves:
        norm = 0.5 * jnp.sum(norm_ref[...], axis=1, keepdims=True)
        bias.append(norm[None])
        value = prec * (ref[...] - norm[None])
        tops.append(jnp.max(jnp.max(value, axis=0), axis=0, keepdims=True))
    top = jnp.maximum(*tops)[None]
    norm = 0.0
    for (ref, _), offset, raised_ref in zip(halves, bias, raised_refs):
        raised = jnp.exp(prec * (ref[...] - offset) - top)
        raised_ref[...] = raised
        norm = norm + jnp.sum(jnp.sum(raised, axis=0), axis=0, keepdims=True)
    inverse = (1.0 / norm)[None]
    for h, ref in enumerate(raised_refs):
        weight = (ref[...] * inverse).astype(jnp.bfloat16)
        outs[h][...] = weight
        wide = weight.astype(jnp.float32)
        total = jnp.sum(jnp.sum(wide, axis=0), axis=1, keepdims=True)
        outs[2 + h][...] = jnp.broadcast_to(total, outs[2 + h].shape)


def weights_of(own, other, precision, shifts):
    rows, images = own[0].shape
    held = rows // shifts
    cube = jax.ShapeDtypeStruct((shifts, held, images), jnp.bfloat16)
    total = jax.ShapeDtypeStruct((held, LANES), jnp.float32)
    own_w, other_w, own_t, other_t = pl.pallas_call(
        weight_kernel,
        out_shape=(cube, cube, total, total),
        scratch_shapes=[pltpu.VMEM((shifts, held, images), jnp.float32)] * 2,
        compiler_params=PARAMS,
        cost_estimate=pl.CostEstimate(
            flops=20 * rows * images,
            bytes_accessed=12 * rows * images,
            transcendentals=2 * rows * images,
        ),
    )(
        own[0].reshape(shifts, held, images),
        other[0].reshape(shifts, held, images),
        own[1],
        other[1],
        precision.reshape(1, images),
    )
    return own_w.reshape(rows, images), other_w.reshape(rows, images), own_t, other_t


def back_kernel(groups, w_ref, x_ref, cos0, sin0, cos_step, sin_step, out_ref, cos_ref, sin_ref):
    shifts, held, _ = cos0.shape
    step = pl.program_id(0)

    @pl.when(step == 0)
    def _():
        cos_ref[...] = cos0[...]
        sin_ref[...] = sin0[...]

    for g in range(groups):
        at = g * PAIR
        mixed = jnp.dot(
            w_ref[...], x_ref[:, at : at + PAIR], preferred_element_type=jnp.float32
        )
        for i in range(held // 8):
            here = slice(i * 8, (i + 1) * 8)
            back_real = jnp.zeros((8, LANES), jnp.float32)
            back_imag = jnp.zeros((8, LANES), jnp.float32)
            for j in range(shifts):
                row = slice(j * held + i * 8, j * held + (i + 1) * 8)
                c, s = cos_ref[j, here, :], sin_ref[j, here, :]
                dc, ds = cos_step[j, here, :], sin_step[j, here, :]
                real, imag = mixed[row, :LANES], mixed[row, LANES:]
                back_real = back_real + (real * c - imag * s)
                back_imag = back_imag + (imag * c + real * s)
                cos_ref[j, here, :] = c * dc - s * ds
                sin_ref[j, here, :] = s * dc + c * ds
            out_ref[here, at : at + LANES] = back_real.astype(out_ref.dtype)
            out_ref[here, at + LANES : at + PAIR] = back_imag.astype(out_ref.dtype)


def back_of(weight, x, phases, steps, half, chunk, chunks, groups=4):
    rows, images = weight.shape
    shifts = phases[0].shape[0]
    held = rows // shifts
    width = x.shape[1] // chunks
    groups = min(groups, width // PAIR)
    block = groups * PAIR
    count = width // block
    whole = pl.BlockSpec((shifts, held, LANES), lambda i: (0, half, 0))
    return pl.pallas_call(
        functools.partial(back_kernel, groups),
        grid=(count,),
        in_specs=[
            pl.BlockSpec((rows, images), lambda i: (0, 0)),
            pl.BlockSpec((images, block), lambda i: (0, chunk * count + i)),
        ]
        + [whole] * 4,
        out_specs=pl.BlockSpec((held, block), lambda i: (0, i)),
        out_shape=jax.ShapeDtypeStruct((held, width), jnp.float32),
        scratch_shapes=[
            pltpu.VMEM((shifts, held, LANES), jnp.float32),
            pltpu.VMEM((shifts, held, LANES), jnp.float32),
        ],
        compiler_params=PARAMS,
        cost_estimate=pl.CostEstimate(
            flops=2 * rows * images * width,
            bytes_accessed=2 * images * width + 2 * rows * images + 4 * held * width,
            transcendentals=0,
        ),
    )(weight, x, *phases, *steps)


def exchange(value, axis, size, bit):
    return lax.ppermute(value, axis, [(i, i ^ bit) for i in range(size)])


def body(images, precision, templates, template_id, shift_table):
    _, parts, coeffs = images.shape
    local = templates.shape[0]
    shifts = shift_table.shape[1]
    rows, cols = lax.axis_size("row"), lax.axis_size("col")
    quads = cols // 2
    groups = coeffs // LANES
    width = parts * coeffs
    held = local * rows * quads

    mine = templates.reshape(local, parts, groups, LANES)
    mine = mine.transpose(0, 2, 1, 3).reshape(local, width)

    row_set = [mine]
    row_set += [exchange(mine, "row", rows, d) for d in range(1, rows)]
    row_set = jnp.concatenate(row_set, axis=0)
    own_set = [row_set]
    own_set += [exchange(row_set, "col", cols, 2 * d) for d in range(1, quads)]
    other_set = [exchange(value, "col", cols, 1) for value in own_set]

    x, peaks = relay(images)

    position = jnp.arange(2 * held, dtype=jnp.int32)
    at_local = position % local
    at_row = (position // local % rows) ^ lax.axis_index("row")
    at_quad = position // (local * rows) % quads
    at_col = (2 * at_quad + position // held) ^ lax.axis_index("col")
    slots = (at_row * cols + at_col) * local + at_local
    shift = shift_table[template_id[slots]].T.reshape(-1, 1)

    number = jnp.arange(SHIFT_SIDE * SHIFT_SIDE, dtype=jnp.int32)[:, None]
    step_x = number // SHIFT_SIDE - SHIFT_SIDE // 2
    step_y = number % SHIFT_SIDE - SHIFT_SIDE // 2
    lane = jnp.arange(LANES, dtype=jnp.int32)[None, :]
    freq_x = lane // GRID - GRID // 2
    freq_y = lane % GRID - GRID // 2
    first = (step_x * freq_x + step_y * freq_y) % GRID
    stride = jnp.broadcast_to(step_x * (LANES // GRID) % GRID, first.shape)
    angle = jnp.concatenate([first, stride], axis=1).astype(jnp.float32)
    angle = angle * (2.0 * math.pi / GRID)
    table = jnp.concatenate([jnp.cos(angle), jnp.sin(angle)], axis=1)
    chosen = (shift == number.T).astype(jnp.float32)
    unit = []
    for at in range(4):
        part = lax.dot(
            chosen, table[:, at * LANES : (at + 1) * LANES], precision=lax.Precision.HIGHEST
        )
        unit.append(part.reshape(shifts, 2 * held, LANES))
    start, steps = (unit[0], unit[2]), (unit[1], unit[3])

    own_scores = scores_of(own_set, start, steps, 0, x)
    other_scores = scores_of(other_set, start, steps, 1, x)
    own_w, other_w, own_total, other_total = weights_of(
        own_scores, other_scores, precision, shifts
    )

    peak = math.sqrt(2.0) * jnp.max(peaks)

    def send(held_rows, axis, size, bit):
        value, total, bound = held_rows
        power = jnp.ceil(jnp.log2(jnp.maximum(bound, 1e-30))) - 15.0
        at = jnp.arange(LANES, dtype=jnp.int32)[None, :]
        extra = jnp.where(at == 0, total, jnp.where(at == 1, power, 0.0))
        payload = jnp.concatenate([value * jnp.exp2(-power), extra], axis=1)
        got = exchange(payload.astype(WIRE), axis, size, bit).astype(jnp.float32)
        span = value.shape[1]
        total, power = got[:, span : span + 1], got[:, span + 1 : span + 2]
        return got[:, :span] * jnp.exp2(power), total, jnp.exp2(power + 15.0)

    def add(first, *others):
        for other in others:
            first = tuple(a + b for a, b in zip(first, other))
        return first

    def cut(held_rows, at, count):
        return tuple(value[at * count : (at + 1) * count] for value in held_rows)

    def reduce_to_owner(own, other):
        got = send(other, "col", cols, 1)
        whole = add(own, got)
        per = local * rows
        got = [send(cut(whole, d, per), "col", cols, 2 * d) for d in range(1, quads)]
        whole = add(cut(whole, 0, per), *got)
        got = [
            send(cut(whole, d, local), "row", rows, d) for d in range(1, rows)
        ]
        return add(cut(whole, 0, local), *got)

    results = []
    for b in range(RS_CHUNKS):
        other = back_of(other_w, x, start, steps, 1, b, RS_CHUNKS)
        own = back_of(own_w, x, start, steps, 0, b, RS_CHUNKS)
        span = width // RS_CHUNKS
        own_sum, other_sum = own_total[:, :1], other_total[:, :1]
        summed, totals, _ = reduce_to_owner(
            (own, own_sum, own_sum * peak), (other, other_sum, other_sum * peak)
        )
        prior = mine[:, b * span : (b + 1) * span].astype(jnp.float32)
        results.append((summed + PRIOR_WEIGHT * prior) / (totals + PRIOR_WEIGHT))
    out = results[0] if RS_CHUNKS == 1 else jnp.concatenate(results, axis=1)
    out = out.reshape(local, groups, parts, LANES).transpose(0, 2, 1, 3)
    return out.reshape(local, parts, coeffs)


def solution(mesh):
    return jax.shard_map(
        body,
        mesh=mesh,
        in_specs=(
            P(("row", "col"), None, None),
            P(("row", "col")),
            P(("row", "col"), None, None),
            P(),
            P(),
        ),
        out_specs=P(("row", "col"), None, None),
        check_vma=False,
    )
```

```python
import functools
import math

import jax
import jax.numpy as jnp
from jax import lax
from jax.experimental import pallas as pl
from jax.experimental.pallas import tpu as pltpu
from jax.sharding import PartitionSpec as P


GRID = 64
SHIFT_SIDE = 8
PRIOR_WEIGHT = 4.0
LANES = 128
PAIR = 2 * LANES
UNROLL = 4
WIRE = jnp.float16
VMEM_LIMIT = 16 << 20

PARAMS = pltpu.CompilerParams(vmem_limit_bytes=VMEM_LIMIT)


def whole_in_vmem(count):
    return [pl.BlockSpec(memory_space=pltpu.VMEM)] * count


def relay_kernel(rows, in_ref, out_ref, taken_ref, wide_ref, peak_ref, sems):
    count, per, _ = in_ref.shape
    blocks = per // rows
    last = out_ref.shape[0]

    def fetch(block, slot):
        return pltpu.make_async_copy(
            in_ref.at[:, pl.ds(block * rows, rows), :], taken_ref.at[slot], sems.at[slot]
        )

    fetch(0, 0).start()
    peak_ref[...] = jnp.zeros_like(peak_ref)

    def step(block, carry):
        slot = lax.rem(block, 2)

        @pl.when(block + 1 < blocks)
        def _():
            fetch(block + 1, 1 - slot).start()

        fetch(block, slot).wait()
        base = pl.multiple_of(block * rows * LANES, rows * LANES)
        peak = peak_ref[...]
        for n in range(0, count, 16):
            wide = taken_ref[slot, n : n + 16].astype(jnp.float32)
            wide_ref[n * rows : (n + 16) * rows, :] = wide.reshape(16 * rows, LANES)
            peak = jnp.maximum(peak, jnp.max(jnp.abs(wide), axis=0))
            for r in range(rows):
                picked = wide_ref[pl.ds(n * rows + r, 16, stride=rows), :]
                at = pl.ds(base + r * LANES, LANES)
                out_ref[n : n + 16, at] = picked.astype(jnp.bfloat16)
        peak_ref[...] = peak
        return carry

    lax.fori_loop(0, blocks, step, 0)
    peak = jnp.max(peak_ref[...], axis=0, keepdims=True)
    out_ref[count:last, :LANES] = jnp.broadcast_to(peak, (last - count, LANES)).astype(
        jnp.bfloat16
    )


def relay(images, rows=8, spare=16):
    count, parts, coeffs = images.shape
    groups = coeffs // LANES
    per = parts * groups
    flat = images.reshape(count, parts, groups, LANES)
    flat = flat.transpose(0, 2, 1, 3).reshape(count, per, LANES)
    return pl.pallas_call(
        functools.partial(relay_kernel, rows),
        in_specs=[pl.BlockSpec(memory_space=pltpu.HBM)],
        out_specs=pl.BlockSpec(memory_space=pltpu.VMEM),
        out_shape=jax.ShapeDtypeStruct((count + spare, per * LANES), jnp.bfloat16),
        scratch_shapes=[
            pltpu.VMEM((2, count, rows, LANES), jnp.bfloat16),
            pltpu.VMEM((count * rows, LANES), jnp.float32),
            pltpu.VMEM((rows, LANES), jnp.float32),
            pltpu.SemaphoreType.DMA((2,)),
        ],
        compiler_params=pltpu.CompilerParams(vmem_limit_bytes=2 * VMEM_LIMIT),
        cost_estimate=pl.CostEstimate(
            flops=count * per * LANES,
            bytes_accessed=4 * count * per * LANES,
            transcendentals=0,
        ),
    )(flat)


def phase_kernel(shift_ref, table_ref, *refs):
    outs, first_ref = refs[:6], refs[6]
    count, rows, _ = outs[0].shape
    number = table_ref.shape[0]
    rest, parts = table_ref[...], []
    for _ in range(3):
        part = rest.astype(jnp.bfloat16)
        parts.append(part)
        rest = rest - part.astype(jnp.float32)
    parts = jnp.concatenate(parts, axis=0)
    numbers = lax.rem(lax.broadcasted_iota(jnp.int32, (rows, 3 * number), 1), number)
    for half in range(2):
        cos_ref, sin_ref, sign_ref = outs[3 * half : 3 * half + 3]
        chosen = shift_ref[half * rows : (half + 1) * rows, :] == numbers
        first_ref[...] = jnp.dot(
            jnp.where(chosen, 1.0, 0.0).astype(jnp.bfloat16),
            parts,
            preferred_element_type=jnp.float32,
        )

        def step(i, carry, cos_ref=cos_ref, sin_ref=sin_ref, sign_ref=sign_ref):
            here = pl.ds(pl.multiple_of(i * 32, 32), 32)
            c, s = first_ref[here, :LANES], first_ref[here, LANES:PAIR]
            dc, ds = first_ref[here, PAIR : PAIR + LANES], first_ref[here, PAIR + LANES :]
            cos_ref[0, here, :] = c
            sin_ref[0, here, :] = s
            for k in range(1, count):
                c, s = c * dc - s * ds, s * dc + c * ds
                cos_ref[k, here, :] = c
                sin_ref[k, here, :] = s
            c, s = c * dc - s * ds, s * dc + c * ds
            same = c * first_ref[here, :LANES] + s * first_ref[here, LANES:PAIR]
            sign_ref[here, :] = jnp.where(same > 0.0, 1.0, -1.0)
            return carry

        lax.fori_loop(0, rows // 32, step, 0)


def phases_of(shift, table, count, rows):
    held = jax.ShapeDtypeStruct((count, rows, LANES), jnp.float32)
    sign = jax.ShapeDtypeStruct((rows, LANES), jnp.float32)
    out = pl.pallas_call(
        phase_kernel,
        in_specs=whole_in_vmem(2),
        out_specs=tuple(whole_in_vmem(6)),
        out_shape=(held, held, sign) * 2,
        scratch_shapes=[pltpu.VMEM((rows, table.shape[1]), jnp.float32)],
        compiler_params=PARAMS,
        cost_estimate=pl.CostEstimate(
            flops=12 * count * rows * LANES,
            bytes_accessed=16 * count * rows * LANES,
            transcendentals=0,
        ),
    )(shift, table)
    return out[:3], out[3:]


def whole_in_vmem(count):
    return [pl.BlockSpec(memory_space=pltpu.VMEM)] * count


def score_kernel(pieces, shifts, *refs):
    piece_refs = refs[:pieces]
    cos_ref, sin_ref, sign_ref, x_ref = refs[pieces : pieces + 4]
    out_ref, norm_ref, rot_a, rot_b = refs[pieces + 4 :]
    images = out_ref.shape[1]
    piece_rows = piece_refs[0].shape[0]
    held = pieces * piece_rows
    block = rot_a.shape[1]
    per = block // PAIR
    half = cos_ref.shape[0] // per

    norm_ref[...] = jnp.zeros_like(norm_ref)
    out_ref[...] = jnp.zeros_like(out_ref)

    def rotate(index, rot_ref):
        live = index < 2 * half
        index = jnp.minimum(index, 2 * half - 1)
        base = pl.multiple_of(index * block, block)
        phase = lax.rem(index, half) * per
        for g in range(per):
            at = g * PAIR
            for i in range(pieces):
                here = slice(i * piece_rows, (i + 1) * piece_rows)
                real = piece_refs[i][:, pl.ds(base + at, LANES)].astype(jnp.float32)
                imag = piece_refs[i][:, pl.ds(base + at + LANES, LANES)].astype(jnp.float32)
                power = real * real + imag * imag
                norm_ref[here, :] += jnp.where(live, power, 0.0)
                for j in range(shifts):
                    start = j * held + i * piece_rows
                    row = slice(start, start + piece_rows)
                    c, s = cos_ref[phase + g, row, :], sin_ref[phase + g, row, :]
                    rot_ref[row, at : at + LANES] = (real * c + imag * s).astype(jnp.bfloat16)
                    rot_ref[row, at + LANES : at + PAIR] = (imag * c - real * s).astype(
                        jnp.bfloat16
                    )

    def gather_scores(index, rot_ref):
        base = pl.multiple_of(index * block, block)
        out_ref[...] += lax.dot_general(
            rot_ref[...],
            x_ref[0:images, pl.ds(base, block)],
            (((1,), (1,)), ((), ())),
            preferred_element_type=jnp.float32,
        )

    def turn_sign():
        for n in range(images // LANES):
            lanes = slice(n * LANES, (n + 1) * LANES)
            out_ref[:, lanes] = out_ref[:, lanes] * sign_ref[...]

    rotate(jnp.int32(0), rot_a)

    def step(i, carry):
        for at in range(0, UNROLL, 2):
            index = i * UNROLL + at
            gather_scores(index, rot_a)
            rotate(index + 1, rot_b)
            gather_scores(index + 1, rot_b)
            rotate(index + 2, rot_a)
        return carry

    lax.fori_loop(0, half // UNROLL, step, 0)
    turn_sign()
    lax.fori_loop(half // UNROLL, 2 * half // UNROLL, step, 0)
    turn_sign()


def scores_of(piece_list, phases, shifts, x, images, groups=2):
    pieces = len(piece_list)
    rows, width = piece_list[0].shape
    held = pieces * rows
    rotated = pltpu.VMEM((shifts * held, groups * PAIR), jnp.bfloat16)
    return pl.pallas_call(
        functools.partial(score_kernel, pieces, shifts),
        in_specs=whole_in_vmem(pieces + 4),
        out_specs=tuple(whole_in_vmem(2)),
        out_shape=(
            jax.ShapeDtypeStruct((shifts * held, images), jnp.float32),
            jax.ShapeDtypeStruct((held, LANES), jnp.float32),
        ),
        scratch_shapes=[rotated, rotated],
        compiler_params=PARAMS,
        cost_estimate=pl.CostEstimate(
            flops=2 * shifts * held * images * width,
            bytes_accessed=2 * images * width + 8 * shifts * held * images,
            transcendentals=0,
        ),
    )(*piece_list, *phases, x)


def weight_kernel(own_ref, other_ref, own_norm, other_norm, prec_ref, x_ref, *outs):
    outs, raised_refs = outs[:6], outs[6:]
    images = prec_ref.shape[1]
    peak = jnp.max(x_ref[images:, :LANES].astype(jnp.float32)) * math.sqrt(2.0)
    prec = prec_ref[...][None]
    halves = ((own_ref, own_norm), (other_ref, other_norm))
    bias, tops = [], []
    for ref, norm_ref in halves:
        norm = 0.5 * jnp.sum(norm_ref[...], axis=1, keepdims=True)
        bias.append(norm[None])
        value = prec * (ref[...] - norm[None])
        tops.append(jnp.max(jnp.max(value, axis=0), axis=0, keepdims=True))
    top = jnp.maximum(*tops)[None]
    norm = 0.0
    for (ref, _), offset, raised_ref in zip(halves, bias, raised_refs):
        raised = jnp.exp(prec * (ref[...] - offset) - top)
        raised_ref[...] = raised
        norm = norm + jnp.sum(jnp.sum(raised, axis=0), axis=0, keepdims=True)
    inverse = (1.0 / norm)[None]
    for h, ref in enumerate(raised_refs):
        weight = (ref[...] * inverse).astype(jnp.bfloat16)
        outs[h][...] = weight
        wide = weight.astype(jnp.float32)
        total = jnp.sum(jnp.sum(wide, axis=0), axis=1, keepdims=True)
        total = jnp.broadcast_to(total, outs[2 + h].shape)
        outs[2 + h][...] = total
        outs[4 + h][...] = total * peak


def weights_of(own, other, precision, x, shifts):
    rows, images = own[0].shape
    held = rows // shifts
    cube = jax.ShapeDtypeStruct((shifts, held, images), jnp.bfloat16)
    total = jax.ShapeDtypeStruct((held, LANES), jnp.float32)
    own_w, other_w, own_t, other_t, own_b, other_b = pl.pallas_call(
        weight_kernel,
        in_specs=whole_in_vmem(6),
        out_specs=tuple(whole_in_vmem(6)),
        out_shape=(cube, cube, total, total, total, total),
        scratch_shapes=[pltpu.VMEM((shifts, held, images), jnp.float32)] * 2,
        compiler_params=PARAMS,
        cost_estimate=pl.CostEstimate(
            flops=20 * rows * images,
            bytes_accessed=12 * rows * images,
            transcendentals=2 * rows * images,
        ),
    )(
        own[0].reshape(shifts, held, images),
        other[0].reshape(shifts, held, images),
        own[1],
        other[1],
        precision.reshape(1, images),
        x,
    )
    own_w, other_w = own_w.reshape(rows, images), other_w.reshape(rows, images)
    own_sum, other_sum = own_t[:, :1], other_t[:, :1]
    return (own_w, own_sum, own_b[:, :1]), (other_w, other_sum, other_b[:, :1])


def back_kernel(shifts, w_ref, cos_ref, sin_ref, sign_ref, x_ref, out_ref, *scratch):
    turned_ref, mix_a, mix_b = scratch
    rows, images = w_ref.shape
    held = rows // shifts
    count = cos_ref.shape[0]
    for n in range(images // LANES):
        lanes = slice(n * LANES, (n + 1) * LANES)
        wide = w_ref[:, lanes].astype(jnp.float32) * sign_ref[...]
        turned_ref[:, lanes] = wide.astype(jnp.bfloat16)

    def mix(index, mix_ref):
        index = jnp.minimum(index, count - 1)
        for second, ref in enumerate((w_ref, turned_ref)):
            base = pl.multiple_of((second * count + index) * PAIR, PAIR)
            mix_ref[:, second * PAIR : (second + 1) * PAIR] = jnp.dot(
                ref[...], x_ref[0:images, pl.ds(base, PAIR)], preferred_element_type=jnp.float32
            )

    def turn(index, mix_ref):
        for i in range(held // 8):
            here = slice(i * 8, (i + 1) * 8)
            total = [None] * 4
            for j in range(shifts):
                row = slice(j * held + i * 8, j * held + (i + 1) * 8)
                c, s = cos_ref[index, row, :], sin_ref[index, row, :]
                terms = []
                for second in range(2):
                    at = second * PAIR
                    real = mix_ref[row, at : at + LANES]
                    imag = mix_ref[row, at + LANES : at + PAIR]
                    terms += [real * c - imag * s, imag * c + real * s]
                total = [b if a is None else a + b for a, b in zip(total, terms)]
            for part in range(4):
                base = (part // 2 * count + index) * PAIR + part % 2 * LANES
                out_ref[here, pl.ds(pl.multiple_of(base, LANES), LANES)] = total[part]

    mix(jnp.int32(0), mix_a)

    def step(i, carry):
        for at in range(0, UNROLL, 2):
            index = i * UNROLL + at
            mix(index + 1, mix_b)
            turn(index, mix_a)
            mix(index + 2, mix_a)
            turn(index + 1, mix_b)
        return carry

    lax.fori_loop(0, count // UNROLL, step, 0)


def back_of(weight, x, phases, shifts):
    rows, images = weight.shape
    held = rows // shifts
    width = x.shape[1]
    mixed = pltpu.VMEM((rows, 2 * PAIR), jnp.float32)
    return pl.pallas_call(
        functools.partial(back_kernel, shifts),
        in_specs=whole_in_vmem(5),
        out_specs=whole_in_vmem(1)[0],
        out_shape=jax.ShapeDtypeStruct((held, width), jnp.float32),
        scratch_shapes=[pltpu.VMEM((rows, images), jnp.bfloat16), mixed, mixed],
        compiler_params=PARAMS,
        cost_estimate=pl.CostEstimate(
            flops=2 * rows * images * width,
            bytes_accessed=2 * images * width + 2 * rows * images + 4 * held * width,
            transcendentals=0,
        ),
    )(weight, *phases, x)


def exchange(value, axis, size, bit):
    return lax.ppermute(value, axis, [(i, i ^ bit) for i in range(size)])


def body(images, precision, templates, template_id, shift_table):
    image_count, parts, coeffs = images.shape
    local = templates.shape[0]
    shifts = shift_table.shape[1]
    rows, cols = lax.axis_size("row"), lax.axis_size("col")
    quads = cols // 2
    groups = coeffs // LANES
    width = parts * coeffs
    held = local * rows * quads

    mine = templates.reshape(local, parts, groups, LANES)
    mine = mine.transpose(0, 2, 1, 3).reshape(local, width)

    row_set = [mine]
    row_set += [exchange(mine, "row", rows, d) for d in range(1, rows)]
    row_set = jnp.concatenate(row_set, axis=0)
    own_set = [row_set]
    own_set += [exchange(row_set, "col", cols, 2 * d) for d in range(1, quads)]
    other_set = [exchange(value, "col", cols, 1) for value in own_set]

    x = relay(images)

    position = jnp.arange(2 * held, dtype=jnp.int32)
    at_local = position % local
    at_row = (position // local % rows) ^ lax.axis_index("row")
    at_quad = position // (local * rows) % quads
    at_col = (2 * at_quad + position // held) ^ lax.axis_index("col")
    slots = (at_row * cols + at_col) * local + at_local
    shift = shift_table[template_id[slots]].reshape(2, held, shifts)
    shift = shift.transpose(0, 2, 1).reshape(-1, 1)

    number = jnp.arange(SHIFT_SIDE * SHIFT_SIDE, dtype=jnp.int32)[:, None]
    step_x = number // SHIFT_SIDE - SHIFT_SIDE // 2
    step_y = number % SHIFT_SIDE - SHIFT_SIDE // 2
    lane = jnp.arange(LANES, dtype=jnp.int32)[None, :]
    freq_x = lane // GRID - GRID // 2
    freq_y = lane % GRID - GRID // 2
    first = (step_x * freq_x + step_y * freq_y) % GRID
    stride = jnp.broadcast_to(step_x * (LANES // GRID) % GRID, first.shape)
    angle = jnp.concatenate([first, stride], axis=1).astype(jnp.float32)
    angle = angle * (2.0 * math.pi / GRID)
    table = [jnp.cos(angle), jnp.sin(angle)]
    table = [part[:, at : at + LANES] for at in (0, LANES) for part in table]
    table = jnp.concatenate(table, axis=1)
    own_phases, other_phases = phases_of(shift, table, groups // 2, shifts * held)

    own_scores = scores_of(own_set, own_phases, shifts, x, image_count)
    other_scores = scores_of(other_set, other_phases, shifts, x, image_count)
    own, other = weights_of(own_scores, other_scores, precision, x, shifts)

    def send(held_rows, axis, size, bit):
        value, total, bound = held_rows
        power = jnp.ceil(jnp.log2(jnp.maximum(bound, 1e-30))) - 15.0
        at = jnp.arange(LANES, dtype=jnp.int32)[None, :]
        extra = jnp.where(at == 0, total, jnp.where(at == 1, power, 0.0))
        payload = jnp.concatenate([value * jnp.exp2(-power), extra], axis=1)
        got = exchange(payload.astype(WIRE), axis, size, bit).astype(jnp.float32)
        span = value.shape[1]
        total, power = got[:, span : span + 1], got[:, span + 1 : span + 2]
        return got[:, :span] * jnp.exp2(power), total, jnp.exp2(power + 15.0)

    def add(first, *others):
        for other in others:
            first = tuple(a + b for a, b in zip(first, other))
        return first

    def cut(held_rows, at, count):
        return tuple(value[at * count : (at + 1) * count] for value in held_rows)

    def reduce_to_owner(own, other):
        got = send(other, "col", cols, 1)
        whole = add(own, got)
        per = local * rows
        got = [send(cut(whole, d, per), "col", cols, 2 * d) for d in range(1, quads)]
        whole = add(cut(whole, 0, per), *got)
        got = [
            send(cut(whole, d, local), "row", rows, d) for d in range(1, rows)
        ]
        return add(cut(whole, 0, local), *got)

    other_back = back_of(other[0], x, other_phases, shifts)
    own_back = back_of(own[0], x, own_phases, shifts)
    summed, totals, _ = reduce_to_owner(
        (own_back,) + own[1:], (other_back,) + other[1:]
    )
    prior = mine.astype(jnp.float32)
    out = (summed + PRIOR_WEIGHT * prior) / (totals + PRIOR_WEIGHT)
    out = out.reshape(local, groups, parts, LANES).transpose(0, 2, 1, 3)
    return out.reshape(local, parts, coeffs)


def solution(mesh):
    return jax.shard_map(
        body,
        mesh=mesh,
        in_specs=(
            P(("row", "col"), None, None),
            P(("row", "col")),
            P(("row", "col"), None, None),
            P(),
            P(),
        ),
        out_specs=P(("row", "col"), None, None),
        check_vma=False,
    )
```

```python
import functools
import math

import jax
import jax.numpy as jnp
from jax import lax
from jax.experimental import pallas as pl
from jax.experimental.pallas import tpu as pltpu
from jax.sharding import PartitionSpec as P


GRID = 64
SHIFT_SIDE = 8
PRIOR_WEIGHT = 4.0
LANES = 128
PAIR = 2 * LANES
UNROLL = 4
WIRE = jnp.float16
VMEM_LIMIT = 8 << 20
RELAY_LIMIT = 12 << 20

PARAMS = pltpu.CompilerParams(vmem_limit_bytes=VMEM_LIMIT)


def whole_in_vmem(count):
    return [pl.BlockSpec(memory_space=pltpu.VMEM)] * count


def relay_kernel(rows, in_ref, out_ref, taken_ref, wide_ref, peak_ref, sems):
    count, per, _ = in_ref.shape
    blocks = per // rows
    last = out_ref.shape[0]

    def fetch(block, slot):
        return pltpu.make_async_copy(
            in_ref.at[:, pl.ds(block * rows, rows), :], taken_ref.at[slot], sems.at[slot]
        )

    fetch(0, 0).start()
    peak_ref[...] = jnp.zeros_like(peak_ref)

    def step(block, carry):
        slot = lax.rem(block, 2)

        @pl.when(block + 1 < blocks)
        def _():
            fetch(block + 1, 1 - slot).start()

        fetch(block, slot).wait()
        base = pl.multiple_of(block * rows * LANES, rows * LANES)
        peak = peak_ref[...]
        for n in range(0, count, 16):
            wide = taken_ref[slot, n : n + 16].astype(jnp.float32)
            wide_ref[n * rows : (n + 16) * rows, :] = wide.reshape(16 * rows, LANES)
            peak = jnp.maximum(peak, jnp.max(jnp.abs(wide), axis=0))
            for r in range(rows):
                picked = wide_ref[pl.ds(n * rows + r, 16, stride=rows), :]
                at = pl.ds(base + r * LANES, LANES)
                out_ref[n : n + 16, at] = picked.astype(jnp.bfloat16)
        peak_ref[...] = peak
        return carry

    lax.fori_loop(0, blocks, step, 0)
    peak = jnp.max(peak_ref[...], axis=0, keepdims=True)
    out_ref[count:last, :LANES] = jnp.broadcast_to(peak, (last - count, LANES)).astype(
        jnp.bfloat16
    )


def relay(images, rows=8, spare=16):
    count, parts, coeffs = images.shape
    groups = coeffs // LANES
    per = parts * groups
    flat = images.reshape(count, parts, groups, LANES)
    flat = flat.transpose(0, 2, 1, 3).reshape(count, per, LANES)
    flat = pltpu.with_memory_space_constraint(flat, pltpu.HBM)
    return pl.pallas_call(
        functools.partial(relay_kernel, rows),
        in_specs=[pl.BlockSpec(memory_space=pltpu.HBM)],
        out_specs=pl.BlockSpec(memory_space=pltpu.VMEM),
        out_shape=jax.ShapeDtypeStruct((count + spare, per * LANES), jnp.bfloat16),
        scratch_shapes=[
            pltpu.VMEM((2, count, rows, LANES), jnp.bfloat16),
            pltpu.VMEM((count * rows, LANES), jnp.float32),
            pltpu.VMEM((rows, LANES), jnp.float32),
            pltpu.SemaphoreType.DMA((2,)),
        ],
        compiler_params=pltpu.CompilerParams(vmem_limit_bytes=RELAY_LIMIT),
        cost_estimate=pl.CostEstimate(
            flops=count * per * LANES,
            bytes_accessed=4 * count * per * LANES,
            transcendentals=0,
        ),
    )(flat)


def phase_kernel(shift_ref, table_ref, *refs):
    outs, first_ref = refs[:6], refs[6]
    count, rows, _ = outs[0].shape
    number = table_ref.shape[0]
    rest, parts = table_ref[...], []
    for _ in range(3):
        part = rest.astype(jnp.bfloat16)
        parts.append(part)
        rest = rest - part.astype(jnp.float32)
    parts = jnp.concatenate(parts, axis=0)
    numbers = lax.rem(lax.broadcasted_iota(jnp.int32, (rows, 3 * number), 1), number)
    for half in range(2):
        cos_ref, sin_ref, sign_ref = outs[3 * half : 3 * half + 3]
        chosen = shift_ref[half * rows : (half + 1) * rows, :] == numbers
        first_ref[...] = jnp.dot(
            jnp.where(chosen, 1.0, 0.0).astype(jnp.bfloat16),
            parts,
            preferred_element_type=jnp.float32,
        )

        def step(i, carry, cos_ref=cos_ref, sin_ref=sin_ref, sign_ref=sign_ref):
            here = pl.ds(pl.multiple_of(i * 32, 32), 32)
            c, s = first_ref[here, :LANES], first_ref[here, LANES:PAIR]
            dc, ds = first_ref[here, PAIR : PAIR + LANES], first_ref[here, PAIR + LANES :]
            cos_ref[0, here, :] = c
            sin_ref[0, here, :] = s
            for k in range(1, count):
                c, s = c * dc - s * ds, s * dc + c * ds
                cos_ref[k, here, :] = c
                sin_ref[k, here, :] = s
            c, s = c * dc - s * ds, s * dc + c * ds
            same = c * first_ref[here, :LANES] + s * first_ref[here, LANES:PAIR]
            sign_ref[here, :] = jnp.where(same > 0.0, 1.0, -1.0)
            return carry

        lax.fori_loop(0, rows // 32, step, 0)


def phases_of(shift, table, count, rows):
    held = jax.ShapeDtypeStruct((count, rows, LANES), jnp.float32)
    sign = jax.ShapeDtypeStruct((rows, LANES), jnp.float32)
    out = pl.pallas_call(
        phase_kernel,
        in_specs=whole_in_vmem(2),
        out_specs=tuple(whole_in_vmem(6)),
        out_shape=(held, held, sign) * 2,
        scratch_shapes=[pltpu.VMEM((rows, table.shape[1]), jnp.float32)],
        compiler_params=PARAMS,
        cost_estimate=pl.CostEstimate(
            flops=12 * count * rows * LANES,
            bytes_accessed=16 * count * rows * LANES,
            transcendentals=0,
        ),
    )(shift, table)
    return out[:3], out[3:]


def whole_in_vmem(count):
    return [pl.BlockSpec(memory_space=pltpu.VMEM)] * count


def score_kernel(places, shifts, *refs):
    pieces = len(places)
    piece_refs = refs[:pieces]
    tables = (refs[pieces : pieces + 3], refs[pieces + 3 : pieces + 6])
    x_ref, out_ref, norm_ref, rot_a, rot_b = refs[pieces + 6 :]
    images = out_ref.shape[1]
    piece_rows = piece_refs[0].shape[0]
    span = shifts * piece_rows
    block = rot_a.shape[1]
    per = block // PAIR
    half = tables[0][0].shape[0] // per

    norm_ref[...] = jnp.zeros_like(norm_ref)
    out_ref[...] = jnp.zeros_like(out_ref)

    def rotate(index, rot_ref):
        live = index < 2 * half
        index = jnp.minimum(index, 2 * half - 1)
        base = pl.multiple_of(index * block, block)
        phase = lax.rem(index, half) * per
        for g in range(per):
            at = g * PAIR
            for i, (side, place) in enumerate(places):
                cos_ref, sin_ref, _ = tables[side]
                here = slice(i * piece_rows, (i + 1) * piece_rows)
                real = piece_refs[i][:, pl.ds(base + at, LANES)].astype(jnp.float32)
                imag = piece_refs[i][:, pl.ds(base + at + LANES, LANES)].astype(jnp.float32)
                power = real * real + imag * imag
                norm_ref[here, :] += jnp.where(live, power, 0.0)
                for j in range(shifts):
                    start = place * span + j * piece_rows
                    row = slice(start, start + piece_rows)
                    c, s = cos_ref[phase + g, row, :], sin_ref[phase + g, row, :]
                    start = i * span + j * piece_rows
                    row = slice(start, start + piece_rows)
                    rot_ref[row, at : at + LANES] = (real * c + imag * s).astype(jnp.bfloat16)
                    rot_ref[row, at + LANES : at + PAIR] = (imag * c - real * s).astype(
                        jnp.bfloat16
                    )

    def gather_scores(index, rot_ref):
        base = pl.multiple_of(index * block, block)
        out_ref[...] += lax.dot_general(
            rot_ref[...],
            x_ref[0:images, pl.ds(base, block)],
            (((1,), (1,)), ((), ())),
            preferred_element_type=jnp.float32,
        )

    def turn_sign():
        for n in range(images // LANES):
            lanes = slice(n * LANES, (n + 1) * LANES)
            for i, (side, place) in enumerate(places):
                sign = tables[side][2][place * span : (place + 1) * span, :]
                row = slice(i * span, (i + 1) * span)
                out_ref[row, lanes] = out_ref[row, lanes] * sign

    rotate(jnp.int32(0), rot_a)

    def step(i, carry):
        for at in range(0, UNROLL, 2):
            index = i * UNROLL + at
            gather_scores(index, rot_a)
            rotate(index + 1, rot_b)
            gather_scores(index + 1, rot_b)
            rotate(index + 2, rot_a)
        return carry

    lax.fori_loop(0, half // UNROLL, step, 0)
    turn_sign()
    lax.fori_loop(half // UNROLL, 2 * half // UNROLL, step, 0)
    turn_sign()


def scores_of(piece_list, places, tables, shifts, x, images, groups=2):
    pieces = len(piece_list)
    rows, width = piece_list[0].shape
    held = pieces * rows
    rotated = pltpu.VMEM((shifts * held, groups * PAIR), jnp.bfloat16)
    return pl.pallas_call(
        functools.partial(score_kernel, places, shifts),
        in_specs=whole_in_vmem(pieces + 7),
        out_specs=tuple(whole_in_vmem(2)),
        out_shape=(
            jax.ShapeDtypeStruct((shifts * held, images), jnp.float32),
            jax.ShapeDtypeStruct((held, LANES), jnp.float32),
        ),
        scratch_shapes=[rotated, rotated],
        compiler_params=PARAMS,
        cost_estimate=pl.CostEstimate(
            flops=2 * shifts * held * images * width,
            bytes_accessed=2 * images * width + 8 * shifts * held * images,
            transcendentals=0,
        ),
    )(*piece_list, *tables[0], *tables[1], x)


def weight_kernel(layout, shifts, piece_rows, *refs):
    blocks = len(layout)
    score_refs, norm_refs = refs[:blocks], refs[blocks : 2 * blocks]
    prec_ref, x_ref = refs[2 * blocks : 2 * blocks + 2]
    outs, raised_refs = refs[2 * blocks + 2 : 2 * blocks + 8], refs[2 * blocks + 8 :]
    images = prec_ref.shape[1]
    span = shifts * piece_rows
    peak = jnp.max(x_ref[images:, :LANES].astype(jnp.float32)) * math.sqrt(2.0)
    prec = prec_ref[...][None]

    def cube(value):
        return value.reshape(-1, piece_rows, value.shape[-1])

    top = None
    for places, score_ref, norm_ref, raised_ref in zip(
        layout, score_refs, norm_refs, raised_refs
    ):
        norm = 0.5 * jnp.sum(norm_ref[...], axis=1, keepdims=True)
        for i in range(len(places)):
            row = slice(i * span, (i + 1) * span)
            bias = norm[i * piece_rows : (i + 1) * piece_rows][None]
            value = prec * (cube(score_ref[row, :]) - bias)
            raised_ref[row, :] = value.reshape(span, images)
            best = jnp.max(jnp.max(value, axis=0), axis=0, keepdims=True)
            top = best if top is None else jnp.maximum(top, best)
    norm = None
    for places, raised_ref in zip(layout, raised_refs):
        for i in range(len(places)):
            row = slice(i * span, (i + 1) * span)
            raised = jnp.exp(raised_ref[row, :] - top)
            raised_ref[row, :] = raised
            part = jnp.sum(jnp.sum(cube(raised), axis=0), axis=0, keepdims=True)
            norm = part if norm is None else norm + part
    inverse = 1.0 / norm
    for places, raised_ref in zip(layout, raised_refs):
        for i, (side, place) in enumerate(places):
            weight = (raised_ref[i * span : (i + 1) * span, :] * inverse).astype(jnp.bfloat16)
            outs[side][place * span : (place + 1) * span, :] = weight
            total = jnp.sum(cube(weight.astype(jnp.float32)), axis=0)
            total = jnp.sum(total, axis=1, keepdims=True)
            total = jnp.broadcast_to(total, (piece_rows, LANES))
            here = slice(place * piece_rows, (place + 1) * piece_rows)
            outs[2 + side][here, :] = total
            outs[4 + side][here, :] = total * peak


def weights_of(scores, layout, precision, x, shifts, held, piece_rows):
    images = precision.shape[0]
    weight = jax.ShapeDtypeStruct((shifts * held, images), jnp.bfloat16)
    total = jax.ShapeDtypeStruct((held, LANES), jnp.float32)
    rows = 2 * shifts * held
    own_w, other_w, own_t, other_t, own_b, other_b = pl.pallas_call(
        functools.partial(weight_kernel, layout, shifts, piece_rows),
        in_specs=whole_in_vmem(2 * len(layout) + 2),
        out_specs=tuple(whole_in_vmem(6)),
        out_shape=(weight, weight, total, total, total, total),
        scratch_shapes=[pltpu.VMEM(value.shape, jnp.float32) for value, _ in scores],
        compiler_params=PARAMS,
        cost_estimate=pl.CostEstimate(
            flops=20 * rows * images,
            bytes_accessed=12 * rows * images,
            transcendentals=2 * rows * images,
        ),
    )(
        *[value for value, _ in scores],
        *[value for _, value in scores],
        precision.reshape(1, images),
        x,
    )
    return (own_w, own_t[:, :1], own_b[:, :1]), (other_w, other_t[:, :1], other_b[:, :1])


def back_kernel(first, pieces, shifts, w_ref, cos_ref, sin_ref, sign_ref, x_ref, *refs):
    out_ref, turned_ref, mix_a, mix_b = refs
    rows, images = turned_ref.shape
    span = rows // pieces
    piece_rows = span // shifts
    count = cos_ref.shape[0]
    first = first * span
    used = slice(first, first + rows)
    for n in range(images // LANES):
        lanes = slice(n * LANES, (n + 1) * LANES)
        wide = w_ref[used, lanes].astype(jnp.float32) * sign_ref[used, :]
        turned_ref[:, lanes] = wide.astype(jnp.bfloat16)

    def mix(index, mix_ref):
        index = jnp.minimum(index, count - 1)
        for second in range(2):
            weight = turned_ref[...] if second else w_ref[used, :]
            base = pl.multiple_of((second * count + index) * PAIR, PAIR)
            mix_ref[:, second * PAIR : (second + 1) * PAIR] = jnp.dot(
                weight, x_ref[0:images, pl.ds(base, PAIR)], preferred_element_type=jnp.float32
            )

    def turn(index, mix_ref):
        for i in range(pieces):
            for t in range(0, piece_rows, 8):
                total = [None] * 4
                for j in range(shifts):
                    start = i * span + j * piece_rows + t
                    row = slice(start, start + 8)
                    at_row = slice(first + start, first + start + 8)
                    c, s = cos_ref[index, at_row, :], sin_ref[index, at_row, :]
                    terms = []
                    for second in range(2):
                        at = second * PAIR
                        real = mix_ref[row, at : at + LANES]
                        imag = mix_ref[row, at + LANES : at + PAIR]
                        terms += [real * c - imag * s, imag * c + real * s]
                    total = [b if a is None else a + b for a, b in zip(total, terms)]
                here = slice(i * piece_rows + t, i * piece_rows + t + 8)
                for part in range(4):
                    base = (part // 2 * count + index) * PAIR + part % 2 * LANES
                    out_ref[here, pl.ds(pl.multiple_of(base, LANES), LANES)] = total[part]

    mix(jnp.int32(0), mix_a)

    def step(i, carry):
        for at in range(0, UNROLL, 2):
            index = i * UNROLL + at
            mix(index + 1, mix_b)
            turn(index, mix_a)
            mix(index + 2, mix_a)
            turn(index + 1, mix_b)
        return carry

    lax.fori_loop(0, count // UNROLL, step, 0)


def back_of(weight, x, phases, shifts, first, pieces, piece_rows):
    images = weight.shape[1]
    rows = pieces * shifts * piece_rows
    width = x.shape[1]
    mixed = pltpu.VMEM((rows, 2 * PAIR), jnp.float32)
    return pl.pallas_call(
        functools.partial(back_kernel, first, pieces, shifts),
        in_specs=whole_in_vmem(5),
        out_specs=whole_in_vmem(1)[0],
        out_shape=jax.ShapeDtypeStruct((pieces * piece_rows, width), jnp.float32),
        scratch_shapes=[pltpu.VMEM((rows, images), jnp.bfloat16), mixed, mixed],
        compiler_params=PARAMS,
        cost_estimate=pl.CostEstimate(
            flops=2 * rows * images * width,
            bytes_accessed=2 * images * width + 2 * rows * images + 4 * pieces * width,
            transcendentals=0,
        ),
    )(weight, *phases, x)


def exchange(value, axis, size, bit):
    return lax.ppermute(value, axis, [(i, i ^ bit) for i in range(size)])


def body(images, precision, templates, template_id, shift_table):
    image_count, parts, coeffs = images.shape
    local = templates.shape[0]
    shifts = shift_table.shape[1]
    rows, cols = lax.axis_size("row"), lax.axis_size("col")
    quads = cols // 2
    groups = coeffs // LANES
    width = parts * coeffs
    held = local * rows * quads

    mine = templates.reshape(local, parts, groups, LANES)
    mine = mine.transpose(0, 2, 1, 3).reshape(local, width)

    row_set = [mine]
    row_set += [exchange(mine, "row", rows, d) for d in range(1, rows)]
    own_set = [jnp.concatenate(row_set, axis=0)]
    for d in range(1, quads):
        own_set.append(exchange(own_set[0], "col", cols, 2 * d))
    other_set = []
    for d in range(quads):
        other_set.append(exchange(own_set[d], "col", cols, 1))

    x = relay(images)

    piece_rows = local * rows
    position = jnp.arange(2 * held, dtype=jnp.int32)
    at_local = position % local
    at_row = (position // local % rows) ^ lax.axis_index("row")
    at_quad = (position // piece_rows + 1) % quads
    at_col = (2 * at_quad + position // held) ^ lax.axis_index("col")
    slots = (at_row * cols + at_col) * local + at_local
    shift = shift_table[template_id[slots]].reshape(2 * quads, piece_rows, shifts)
    shift = shift.transpose(0, 2, 1).reshape(-1, 1)

    number = jnp.arange(SHIFT_SIDE * SHIFT_SIDE, dtype=jnp.int32)[:, None]
    step_x = number // SHIFT_SIDE - SHIFT_SIDE // 2
    step_y = number % SHIFT_SIDE - SHIFT_SIDE // 2
    lane = jnp.arange(LANES, dtype=jnp.int32)[None, :]
    freq_x = lane // GRID - GRID // 2
    freq_y = lane % GRID - GRID // 2
    first = (step_x * freq_x + step_y * freq_y) % GRID
    stride = jnp.broadcast_to(step_x * (LANES // GRID) % GRID, first.shape)
    angle = jnp.concatenate([first, stride], axis=1).astype(jnp.float32)
    angle = angle * (2.0 * math.pi / GRID)
    table = [jnp.cos(angle), jnp.sin(angle)]
    table = [part[:, at : at + LANES] for at in (0, LANES) for part in table]
    table = jnp.concatenate(table, axis=1)
    tables = phases_of(shift, table, groups // 2, shifts * held)

    layout = [
        tuple((0, (d - 1) % quads) for d in range(quads - 1)),
        tuple((1, (d - 1) % quads) for d in range(quads - 1)),
        ((0, quads - 2), (1, quads - 2)),
    ]
    piece_lists = [own_set[:-1], other_set[:-1], [own_set[-1], other_set[-1]]]
    scores = []
    for number, (piece_list, places) in enumerate(zip(piece_lists, layout)):
        scores.append(scores_of(piece_list, places, tables, shifts, x, image_count))
    own, other = weights_of(scores, layout, precision, x, shifts, held, piece_rows)

    def pack(held_rows):
        value, total, bound = held_rows
        power = jnp.ceil(jnp.log2(jnp.maximum(bound, 1e-30))) - 15.0
        at = jnp.arange(LANES, dtype=jnp.int32)[None, :]
        extra = jnp.where(at == 0, total, jnp.where(at == 1, power, 0.0))
        return jnp.concatenate([value * jnp.exp2(-power), extra], axis=1).astype(WIRE)

    def unpack(payload):
        got = payload.astype(jnp.float32)
        total, power = got[:, width : width + 1], got[:, width + 1 : width + 2]
        return got[:, :width] * jnp.exp2(power), total, jnp.exp2(power + 15.0)

    def send(held_rows, axis, size, bit):
        return unpack(exchange(pack(held_rows), axis, size, bit))

    def add(first, *others):
        for other in others:
            first = tuple(a + b for a, b in zip(first, other))
        return first

    def cut(held_rows, at, count):
        return tuple(value[at * count : (at + 1) * count] for value in held_rows)

    other_back = back_of(other[0], x, tables[1], shifts, 0, quads, piece_rows)
    got = send((other_back,) + other[1:], "col", cols, 1)
    per_set = quads // 2
    set_rows = per_set * piece_rows
    own_weight = own[0]
    sums, received = [], []
    for number in range(2):
        back = back_of(
            own_weight, x, tables[0], shifts, number * per_set, per_set, piece_rows
        )
        whole = add((back,) + cut(own[1:], number, set_rows), cut(got, number, set_rows))
        pieces = [cut(whole, place, piece_rows) for place in range(per_set)]
        if number:
            sums.append(pieces.pop())
        pieces = [pack(piece) for piece in pieces]
        if not number:
            *pieces, own_weight = lax.optimization_barrier((*pieces, own_weight))
        for place, piece in enumerate(pieces):
            d = number * per_set + place + 1
            received.append(unpack(exchange(piece, "col", cols, 2 * d)))
    whole = add(sums[0], *received)
    got = [send(cut(whole, d, local), "row", rows, d) for d in range(1, rows)]
    summed, totals, _ = add(cut(whole, 0, local), *got)
    prior = mine.astype(jnp.float32)
    out = (summed + PRIOR_WEIGHT * prior) / (totals + PRIOR_WEIGHT)
    out = out.reshape(local, groups, parts, LANES).transpose(0, 2, 1, 3)
    return out.reshape(local, parts, coeffs)


def solution(mesh):
    return jax.shard_map(
        body,
        mesh=mesh,
        in_specs=(
            P(("row", "col"), None, None),
            P(("row", "col")),
            P(("row", "col"), None, None),
            P(),
            P(),
        ),
        out_specs=P(("row", "col"), None, None),
        check_vma=False,
    )
```

```python
import functools
import math

import jax
import jax.numpy as jnp
from jax import lax
from jax.experimental import pallas as pl
from jax.experimental.pallas import tpu as pltpu
from jax.sharding import PartitionSpec as P


GRID = 64
SHIFT_SIDE = 8
PRIOR_WEIGHT = 4.0
LANES = 128
PAIR = 2 * LANES
UNROLL = 4
WIRE = jnp.float16
VMEM_LIMIT = 8 << 20
RELAY_LIMIT = 12 << 20

PARAMS = pltpu.CompilerParams(vmem_limit_bytes=VMEM_LIMIT)


def whole_in_vmem(count):
    return [pl.BlockSpec(memory_space=pltpu.VMEM)] * count


def relay_kernel(in_ref, out_ref, taken_ref, wide_ref, peak_ref, sems):
    count, per, _ = in_ref.shape
    some = taken_ref.shape[1]
    rows = peak_ref.shape[0]
    blocks = count // some
    last = out_ref.shape[0]

    def fetch(block, slot):
        return pltpu.make_async_copy(
            in_ref.at[pl.ds(block * some, some)], taken_ref.at[slot], sems.at[slot]
        )

    fetch(0, 0).start()
    peak_ref[...] = jnp.zeros_like(peak_ref)

    def step(block, carry):
        slot = lax.rem(block, 2)

        @pl.when(block + 1 < blocks)
        def _():
            fetch(block + 1, 1 - slot).start()

        fetch(block, slot).wait()
        base = pl.multiple_of(block * some, some)
        peak = peak_ref[...]
        for n in range(0, some, 16):
            for r in range(0, per, rows):
                wide = taken_ref[slot, n : n + 16, r : r + rows, :].astype(jnp.float32)
                start = (n * per) + 16 * r
                wide_ref[start : start + 16 * rows, :] = wide.reshape(16 * rows, LANES)
                peak = jnp.maximum(peak, jnp.max(jnp.abs(wide), axis=0))
                for k in range(rows):
                    picked = wide_ref[pl.ds(start + k, 16, stride=rows), :]
                    at = (r + k) * LANES
                    out_ref[pl.ds(base + n, 16), at : at + LANES] = picked.astype(jnp.bfloat16)
        peak_ref[...] = peak
        return carry

    lax.fori_loop(0, blocks, step, 0)
    peak = jnp.max(peak_ref[...], axis=0, keepdims=True)
    out_ref[count:last, :LANES] = jnp.broadcast_to(peak, (last - count, LANES)).astype(
        jnp.bfloat16
    )


def relay(images, rows=8, spare=16):
    count, parts, coeffs = images.shape
    groups = coeffs // LANES
    per = parts * groups
    some = min(count, 64)
    flat = images.reshape(count, parts, groups, LANES)
    flat = flat.transpose(0, 2, 1, 3).reshape(count, per, LANES)
    flat = pltpu.with_memory_space_constraint(flat, pltpu.HBM)
    return pl.pallas_call(
        relay_kernel,
        in_specs=[pl.BlockSpec(memory_space=pltpu.HBM)],
        out_specs=pl.BlockSpec(memory_space=pltpu.VMEM),
        out_shape=jax.ShapeDtypeStruct((count + spare, per * LANES), jnp.bfloat16),
        scratch_shapes=[
            pltpu.VMEM((2, some, per, LANES), jnp.bfloat16),
            pltpu.VMEM((some * per, LANES), jnp.float32),
            pltpu.VMEM((rows, LANES), jnp.float32),
            pltpu.SemaphoreType.DMA((2,)),
        ],
        compiler_params=pltpu.CompilerParams(vmem_limit_bytes=RELAY_LIMIT),
        cost_estimate=pl.CostEstimate(
            flops=count * per * LANES,
            bytes_accessed=4 * count * per * LANES,
            transcendentals=0,
        ),
    )(flat)


def phase_kernel(shift_ref, table_ref, *refs):
    outs, first_ref = refs[:6], refs[6]
    count, rows, _ = outs[0].shape
    number = table_ref.shape[0]
    rest, parts = table_ref[...], []
    for _ in range(3):
        part = rest.astype(jnp.bfloat16)
        parts.append(part)
        rest = rest - part.astype(jnp.float32)
    parts = jnp.concatenate(parts, axis=0)
    numbers = lax.rem(lax.broadcasted_iota(jnp.int32, (rows, 3 * number), 1), number)
    for half in range(2):
        cos_ref, sin_ref, sign_ref = outs[3 * half : 3 * half + 3]
        chosen = shift_ref[half * rows : (half + 1) * rows, :] == numbers
        first_ref[...] = jnp.dot(
            jnp.where(chosen, 1.0, 0.0).astype(jnp.bfloat16),
            parts,
            preferred_element_type=jnp.float32,
        )

        def step(i, carry, cos_ref=cos_ref, sin_ref=sin_ref, sign_ref=sign_ref):
            here = pl.ds(pl.multiple_of(i * 32, 32), 32)
            c, s = first_ref[here, :LANES], first_ref[here, LANES:PAIR]
            dc, ds = first_ref[here, PAIR : PAIR + LANES], first_ref[here, PAIR + LANES :]
            cos_ref[0, here, :] = c
            sin_ref[0, here, :] = s
            for k in range(1, count):
                c, s = c * dc - s * ds, s * dc + c * ds
                cos_ref[k, here, :] = c
                sin_ref[k, here, :] = s
            c, s = c * dc - s * ds, s * dc + c * ds
            same = c * first_ref[here, :LANES] + s * first_ref[here, LANES:PAIR]
            sign_ref[here, :] = jnp.where(same > 0.0, 1.0, -1.0)
            return carry

        lax.fori_loop(0, rows // 32, step, 0)


def phases_of(shift, table, count, rows):
    held = jax.ShapeDtypeStruct((count, rows, LANES), jnp.float32)
    sign = jax.ShapeDtypeStruct((rows, LANES), jnp.float32)
    out = pl.pallas_call(
        phase_kernel,
        in_specs=whole_in_vmem(2),
        out_specs=tuple(whole_in_vmem(6)),
        out_shape=(held, held, sign) * 2,
        scratch_shapes=[pltpu.VMEM((rows, table.shape[1]), jnp.float32)],
        compiler_params=PARAMS,
        cost_estimate=pl.CostEstimate(
            flops=12 * count * rows * LANES,
            bytes_accessed=16 * count * rows * LANES,
            transcendentals=0,
        ),
    )(shift, table)
    return out[:3], out[3:]


def whole_in_vmem(count):
    return [pl.BlockSpec(memory_space=pltpu.VMEM)] * count


def score_kernel(places, shifts, *refs):
    pieces = len(places)
    piece_refs = refs[:pieces]
    tables = (refs[pieces : pieces + 3], refs[pieces + 3 : pieces + 6])
    x_ref, out_ref, norm_ref, rot_a, rot_b = refs[pieces + 6 :]
    images = out_ref.shape[1]
    piece_rows = piece_refs[0].shape[0]
    span = shifts * piece_rows
    block = rot_a.shape[1]
    per = block // PAIR
    half = tables[0][0].shape[0] // per

    norm_ref[...] = jnp.zeros_like(norm_ref)
    out_ref[...] = jnp.zeros_like(out_ref)

    def rotate(index, rot_ref):
        live = index < 2 * half
        index = jnp.minimum(index, 2 * half - 1)
        base = pl.multiple_of(index * block, block)
        phase = lax.rem(index, half) * per
        for g in range(per):
            at = g * PAIR
            for i, (side, place) in enumerate(places):
                cos_ref, sin_ref, _ = tables[side]
                here = slice(i * piece_rows, (i + 1) * piece_rows)
                real = piece_refs[i][:, pl.ds(base + at, LANES)].astype(jnp.float32)
                imag = piece_refs[i][:, pl.ds(base + at + LANES, LANES)].astype(jnp.float32)
                power = real * real + imag * imag
                norm_ref[here, :] += jnp.where(live, power, 0.0)
                for j in range(shifts):
                    start = place * span + j * piece_rows
                    row = slice(start, start + piece_rows)
                    c, s = cos_ref[phase + g, row, :], sin_ref[phase + g, row, :]
                    start = i * span + j * piece_rows
                    row = slice(start, start + piece_rows)
                    rot_ref[row, at : at + LANES] = (real * c + imag * s).astype(jnp.bfloat16)
                    rot_ref[row, at + LANES : at + PAIR] = (imag * c - real * s).astype(
                        jnp.bfloat16
                    )

    def gather_scores(index, rot_ref):
        base = pl.multiple_of(index * block, block)
        out_ref[...] += lax.dot_general(
            rot_ref[...],
            x_ref[0:images, pl.ds(base, block)],
            (((1,), (1,)), ((), ())),
            preferred_element_type=jnp.float32,
        )

    def turn_sign():
        for n in range(images // LANES):
            lanes = slice(n * LANES, (n + 1) * LANES)
            for i, (side, place) in enumerate(places):
                sign = tables[side][2][place * span : (place + 1) * span, :]
                row = slice(i * span, (i + 1) * span)
                out_ref[row, lanes] = out_ref[row, lanes] * sign

    rotate(jnp.int32(0), rot_a)

    def step(i, carry):
        for at in range(0, UNROLL, 2):
            index = i * UNROLL + at
            gather_scores(index, rot_a)
            rotate(index + 1, rot_b)
            gather_scores(index + 1, rot_b)
            rotate(index + 2, rot_a)
        return carry

    lax.fori_loop(0, half // UNROLL, step, 0)
    turn_sign()
    lax.fori_loop(half // UNROLL, 2 * half // UNROLL, step, 0)
    turn_sign()


def scores_of(piece_list, places, tables, shifts, x, images, groups=2):
    pieces = len(piece_list)
    rows, width = piece_list[0].shape
    held = pieces * rows
    rotated = pltpu.VMEM((shifts * held, groups * PAIR), jnp.bfloat16)
    return pl.pallas_call(
        functools.partial(score_kernel, places, shifts),
        in_specs=whole_in_vmem(pieces + 7),
        out_specs=tuple(whole_in_vmem(2)),
        out_shape=(
            jax.ShapeDtypeStruct((shifts * held, images), jnp.float32),
            jax.ShapeDtypeStruct((held, LANES), jnp.float32),
        ),
        scratch_shapes=[rotated, rotated],
        compiler_params=PARAMS,
        cost_estimate=pl.CostEstimate(
            flops=2 * shifts * held * images * width,
            bytes_accessed=2 * images * width + 8 * shifts * held * images,
            transcendentals=0,
        ),
    )(*piece_list, *tables[0], *tables[1], x)


def weight_kernel(layout, shifts, piece_rows, *refs):
    blocks = len(layout)
    score_refs, norm_refs = refs[:blocks], refs[blocks : 2 * blocks]
    prec_ref, x_ref = refs[2 * blocks : 2 * blocks + 2]
    outs, raised_refs = refs[2 * blocks + 2 : 2 * blocks + 8], refs[2 * blocks + 8 :]
    images = prec_ref.shape[1]
    span = shifts * piece_rows
    peak = jnp.max(x_ref[images:, :LANES].astype(jnp.float32)) * math.sqrt(2.0)
    prec = prec_ref[...][None]

    def cube(value):
        return value.reshape(-1, piece_rows, value.shape[-1])

    top = None
    for places, score_ref, norm_ref, raised_ref in zip(
        layout, score_refs, norm_refs, raised_refs
    ):
        norm = 0.5 * jnp.sum(norm_ref[...], axis=1, keepdims=True)
        for i in range(len(places)):
            row = slice(i * span, (i + 1) * span)
            bias = norm[i * piece_rows : (i + 1) * piece_rows][None]
            value = prec * (cube(score_ref[row, :]) - bias)
            raised_ref[row, :] = value.reshape(span, images)
            best = jnp.max(jnp.max(value, axis=0), axis=0, keepdims=True)
            top = best if top is None else jnp.maximum(top, best)
    norm = None
    for places, raised_ref in zip(layout, raised_refs):
        for i in range(len(places)):
            row = slice(i * span, (i + 1) * span)
            raised = jnp.exp(raised_ref[row, :] - top)
            raised_ref[row, :] = raised
            part = jnp.sum(jnp.sum(cube(raised), axis=0), axis=0, keepdims=True)
            norm = part if norm is None else norm + part
    inverse = 1.0 / norm
    for places, raised_ref in zip(layout, raised_refs):
        for i, (side, place) in enumerate(places):
            weight = (raised_ref[i * span : (i + 1) * span, :] * inverse).astype(jnp.bfloat16)
            outs[side][place * span : (place + 1) * span, :] = weight
            total = jnp.sum(cube(weight.astype(jnp.float32)), axis=0)
            total = jnp.sum(total, axis=1, keepdims=True)
            total = jnp.broadcast_to(total, (piece_rows, LANES))
            here = slice(place * piece_rows, (place + 1) * piece_rows)
            outs[2 + side][here, :] = total
            outs[4 + side][here, :] = total * peak


def weights_of(scores, layout, precision, x, shifts, held, piece_rows):
    images = precision.shape[0]
    weight = jax.ShapeDtypeStruct((shifts * held, images), jnp.bfloat16)
    total = jax.ShapeDtypeStruct((held, LANES), jnp.float32)
    rows = 2 * shifts * held
    own_w, other_w, own_t, other_t, own_b, other_b = pl.pallas_call(
        functools.partial(weight_kernel, layout, shifts, piece_rows),
        in_specs=whole_in_vmem(2 * len(layout) + 2),
        out_specs=tuple(whole_in_vmem(6)),
        out_shape=(weight, weight, total, total, total, total),
        scratch_shapes=[pltpu.VMEM(value.shape, jnp.float32) for value, _ in scores],
        compiler_params=PARAMS,
        cost_estimate=pl.CostEstimate(
            flops=20 * rows * images,
            bytes_accessed=12 * rows * images,
            transcendentals=2 * rows * images,
        ),
    )(
        *[value for value, _ in scores],
        *[value for _, value in scores],
        precision.reshape(1, images),
        x,
    )
    return (own_w, own_t[:, :1], own_b[:, :1]), (other_w, other_t[:, :1], other_b[:, :1])


def back_kernel(first, pieces, shifts, w_ref, cos_ref, sin_ref, sign_ref, x_ref, *refs):
    out_ref, turned_ref, mix_a, mix_b = refs
    rows, images = turned_ref.shape
    span = rows // pieces
    piece_rows = span // shifts
    count = cos_ref.shape[0]
    first = first * span
    used = slice(first, first + rows)
    for n in range(images // LANES):
        lanes = slice(n * LANES, (n + 1) * LANES)
        wide = w_ref[used, lanes].astype(jnp.float32) * sign_ref[used, :]
        turned_ref[:, lanes] = wide.astype(jnp.bfloat16)

    def mix(index, mix_ref):
        index = jnp.minimum(index, count - 1)
        for second in range(2):
            weight = turned_ref[...] if second else w_ref[used, :]
            base = pl.multiple_of((second * count + index) * PAIR, PAIR)
            mix_ref[:, second * PAIR : (second + 1) * PAIR] = jnp.dot(
                weight, x_ref[0:images, pl.ds(base, PAIR)], preferred_element_type=jnp.float32
            )

    def turn(index, mix_ref):
        for i in range(pieces):
            for t in range(0, piece_rows, 8):
                total = [None] * 4
                for j in range(shifts):
                    start = i * span + j * piece_rows + t
                    row = slice(start, start + 8)
                    at_row = slice(first + start, first + start + 8)
                    c, s = cos_ref[index, at_row, :], sin_ref[index, at_row, :]
                    terms = []
                    for second in range(2):
                        at = second * PAIR
                        real = mix_ref[row, at : at + LANES]
                        imag = mix_ref[row, at + LANES : at + PAIR]
                        terms += [real * c - imag * s, imag * c + real * s]
                    total = [b if a is None else a + b for a, b in zip(total, terms)]
                here = slice(i * piece_rows + t, i * piece_rows + t + 8)
                for part in range(4):
                    base = (part // 2 * count + index) * PAIR + part % 2 * LANES
                    out_ref[here, pl.ds(pl.multiple_of(base, LANES), LANES)] = total[part]

    mix(jnp.int32(0), mix_a)

    def step(i, carry):
        for at in range(0, UNROLL, 2):
            index = i * UNROLL + at
            mix(index + 1, mix_b)
            turn(index, mix_a)
            mix(index + 2, mix_a)
            turn(index + 1, mix_b)
        return carry

    lax.fori_loop(0, count // UNROLL, step, 0)


def back_of(weight, x, phases, shifts, first, pieces, piece_rows):
    images = weight.shape[1]
    rows = pieces * shifts * piece_rows
    width = x.shape[1]
    mixed = pltpu.VMEM((rows, 2 * PAIR), jnp.float32)
    return pl.pallas_call(
        functools.partial(back_kernel, first, pieces, shifts),
        in_specs=whole_in_vmem(5),
        out_specs=whole_in_vmem(1)[0],
        out_shape=jax.ShapeDtypeStruct((pieces * piece_rows, width), jnp.float32),
        scratch_shapes=[pltpu.VMEM((rows, images), jnp.bfloat16), mixed, mixed],
        compiler_params=PARAMS,
        cost_estimate=pl.CostEstimate(
            flops=2 * rows * images * width,
            bytes_accessed=2 * images * width + 2 * rows * images + 4 * pieces * width,
            transcendentals=0,
        ),
    )(weight, *phases, x)


def exchange(value, axis, size, bit):
    return lax.ppermute(value, axis, [(i, i ^ bit) for i in range(size)])


def body(images, precision, templates, template_id, shift_table):
    image_count, parts, coeffs = images.shape
    local = templates.shape[0]
    shifts = shift_table.shape[1]
    rows, cols = lax.axis_size("row"), lax.axis_size("col")
    quads = cols // 2
    groups = coeffs // LANES
    width = parts * coeffs
    held = local * rows * quads

    mine = templates.reshape(local, parts, groups, LANES)
    mine = mine.transpose(0, 2, 1, 3).reshape(local, width)

    row_set = [mine]
    row_set += [exchange(mine, "row", rows, d) for d in range(1, rows)]
    own_set = [jnp.concatenate(row_set, axis=0)]
    for d in range(1, quads):
        own_set.append(exchange(own_set[0], "col", cols, 2 * d))
    other_set = []
    for d in range(quads):
        other_set.append(exchange(own_set[d], "col", cols, 1))

    x = relay(images)

    piece_rows = local * rows
    position = jnp.arange(2 * held, dtype=jnp.int32)
    at_local = position % local
    at_row = (position // local % rows) ^ lax.axis_index("row")
    at_quad = (position // piece_rows + 1) % quads
    at_col = (2 * at_quad + position // held) ^ lax.axis_index("col")
    slots = (at_row * cols + at_col) * local + at_local
    shift = shift_table[template_id[slots]].reshape(2 * quads, piece_rows, shifts)
    shift = shift.transpose(0, 2, 1).reshape(-1, 1)

    number = jnp.arange(SHIFT_SIDE * SHIFT_SIDE, dtype=jnp.int32)[:, None]
    step_x = number // SHIFT_SIDE - SHIFT_SIDE // 2
    step_y = number % SHIFT_SIDE - SHIFT_SIDE // 2
    lane = jnp.arange(LANES, dtype=jnp.int32)[None, :]
    freq_x = lane // GRID - GRID // 2
    freq_y = lane % GRID - GRID // 2
    first = (step_x * freq_x + step_y * freq_y) % GRID
    stride = jnp.broadcast_to(step_x * (LANES // GRID) % GRID, first.shape)
    angle = jnp.concatenate([first, stride], axis=1).astype(jnp.float32)
    angle = angle * (2.0 * math.pi / GRID)
    table = [jnp.cos(angle), jnp.sin(angle)]
    table = [part[:, at : at + LANES] for at in (0, LANES) for part in table]
    table = jnp.concatenate(table, axis=1)
    tables = phases_of(shift, table, groups // 2, shifts * held)

    layout = [
        tuple((0, (d - 1) % quads) for d in range(quads - 1)),
        tuple((1, (d - 1) % quads) for d in range(quads - 1)),
        ((0, quads - 2), (1, quads - 2)),
    ]
    piece_lists = [own_set[:-1], other_set[:-1], [own_set[-1], other_set[-1]]]
    scores = []
    for number, (piece_list, places) in enumerate(zip(piece_lists, layout)):
        scores.append(scores_of(piece_list, places, tables, shifts, x, image_count))
    own, other = weights_of(scores, layout, precision, x, shifts, held, piece_rows)

    def pack(held_rows):
        value, total, bound = held_rows
        power = jnp.ceil(jnp.log2(jnp.maximum(bound, 1e-30))) - 15.0
        at = jnp.arange(LANES, dtype=jnp.int32)[None, :]
        extra = jnp.where(at == 0, total, jnp.where(at == 1, power, 0.0))
        return jnp.concatenate([value * jnp.exp2(-power), extra], axis=1).astype(WIRE)

    def unpack(payload):
        got = payload.astype(jnp.float32)
        total, power = got[:, width : width + 1], got[:, width + 1 : width + 2]
        return got[:, :width] * jnp.exp2(power), total, jnp.exp2(power + 15.0)

    def send(held_rows, axis, size, bit):
        return unpack(exchange(pack(held_rows), axis, size, bit))

    def add(first, *others):
        for other in others:
            first = tuple(a + b for a, b in zip(first, other))
        return first

    def cut(held_rows, at, count):
        return tuple(value[at * count : (at + 1) * count] for value in held_rows)

    other_back = back_of(other[0], x, tables[1], shifts, 0, quads, piece_rows)
    got = send((other_back,) + other[1:], "col", cols, 1)
    per_set = quads // 2
    set_rows = per_set * piece_rows
    own_weight = own[0]
    sums, received = [], []
    for number in range(2):
        back = back_of(
            own_weight, x, tables[0], shifts, number * per_set, per_set, piece_rows
        )
        whole = add((back,) + cut(own[1:], number, set_rows), cut(got, number, set_rows))
        pieces = [cut(whole, place, piece_rows) for place in range(per_set)]
        if number:
            sums.append(pieces.pop())
        pieces = [pack(piece) for piece in pieces]
        if not number:
            *pieces, own_weight = lax.optimization_barrier((*pieces, own_weight))
        for place, piece in enumerate(pieces):
            d = number * per_set + place + 1
            received.append(unpack(exchange(piece, "col", cols, 2 * d)))
    whole = add(sums[0], *received)
    got = [send(cut(whole, d, local), "row", rows, d) for d in range(1, rows)]
    summed, totals, _ = add(cut(whole, 0, local), *got)
    prior = mine.astype(jnp.float32)
    out = (summed + PRIOR_WEIGHT * prior) / (totals + PRIOR_WEIGHT)
    out = out.reshape(local, groups, parts, LANES).transpose(0, 2, 1, 3)
    return out.reshape(local, parts, coeffs)


def solution(mesh):
    return jax.shard_map(
        body,
        mesh=mesh,
        in_specs=(
            P(("row", "col"), None, None),
            P(("row", "col")),
            P(("row", "col"), None, None),
            P(),
            P(),
        ),
        out_specs=P(("row", "col"), None, None),
        check_vma=False,
    )
```

```python
import functools
import math

import jax
import jax.numpy as jnp
from jax import lax
from jax.experimental import pallas as pl
from jax.experimental.pallas import tpu as pltpu
from jax.sharding import PartitionSpec as P


GRID = 64
SHIFT_SIDE = 8
PRIOR_WEIGHT = 4.0
LANES = 128
PAIR = 2 * LANES
UNROLL = 8
WIRE = jnp.float16
VMEM_LIMIT = 8 << 20
RELAY_LIMIT = 12 << 20

PARAMS = pltpu.CompilerParams(vmem_limit_bytes=VMEM_LIMIT)


def whole_in_vmem(count):
    return [pl.BlockSpec(memory_space=pltpu.VMEM)] * count


def relay_kernel(in_ref, out_ref, taken_ref, wide_ref, peak_ref, sems):
    count, per, _ = in_ref.shape
    some = taken_ref.shape[1]
    rows = peak_ref.shape[0]
    blocks = count // some
    last = out_ref.shape[0]

    def fetch(block, slot):
        return pltpu.make_async_copy(
            in_ref.at[pl.ds(block * some, some)], taken_ref.at[slot], sems.at[slot]
        )

    fetch(0, 0).start()
    peak_ref[...] = jnp.zeros_like(peak_ref)

    def step(block, carry):
        slot = lax.rem(block, 2)

        @pl.when(block + 1 < blocks)
        def _():
            fetch(block + 1, 1 - slot).start()

        fetch(block, slot).wait()
        base = pl.multiple_of(block * some, some)
        peak = peak_ref[...]
        for n in range(0, some, 16):
            for r in range(0, per, rows):
                wide = taken_ref[slot, n : n + 16, r : r + rows, :].astype(jnp.float32)
                start = (n * per) + 16 * r
                wide_ref[start : start + 16 * rows, :] = wide.reshape(16 * rows, LANES)
                peak = jnp.maximum(peak, jnp.max(jnp.abs(wide), axis=0))
                for k in range(rows):
                    picked = wide_ref[pl.ds(start + k, 16, stride=rows), :]
                    at = (r + k) * LANES
                    out_ref[pl.ds(base + n, 16), at : at + LANES] = picked.astype(jnp.bfloat16)
        peak_ref[...] = peak
        return carry

    lax.fori_loop(0, blocks, step, 0)
    peak = jnp.max(peak_ref[...], axis=0, keepdims=True)
    out_ref[count:last, :LANES] = jnp.broadcast_to(peak, (last - count, LANES)).astype(
        jnp.bfloat16
    )


def relay(images, rows=8, spare=16):
    count, parts, coeffs = images.shape
    groups = coeffs // LANES
    per = parts * groups
    some = min(count, 64)
    flat = images.reshape(count, parts, groups, LANES)
    flat = flat.transpose(0, 2, 1, 3).reshape(count, per, LANES)
    flat = pltpu.with_memory_space_constraint(flat, pltpu.HBM)
    return pl.pallas_call(
        relay_kernel,
        in_specs=[pl.BlockSpec(memory_space=pltpu.HBM)],
        out_specs=pl.BlockSpec(memory_space=pltpu.VMEM),
        out_shape=jax.ShapeDtypeStruct((count + spare, per * LANES), jnp.bfloat16),
        scratch_shapes=[
            pltpu.VMEM((2, some, per, LANES), jnp.bfloat16),
            pltpu.VMEM((some * per, LANES), jnp.float32),
            pltpu.VMEM((rows, LANES), jnp.float32),
            pltpu.SemaphoreType.DMA((2,)),
        ],
        compiler_params=pltpu.CompilerParams(vmem_limit_bytes=RELAY_LIMIT),
        cost_estimate=pl.CostEstimate(
            flops=count * per * LANES,
            bytes_accessed=4 * count * per * LANES,
            transcendentals=0,
        ),
    )(flat)


def phase_kernel(local, quads, id_ref, shifts_ref, table_ref, *refs):
    outs, first_ref, chosen_ref = refs[:6], refs[6], refs[7]
    count, rows, _ = outs[0].shape
    number = table_ref.shape[0]
    shifts, templates = shifts_ref.shape
    held = templates // 2
    piece_rows = held // quads
    in_row = piece_rows // local

    position = lax.broadcasted_iota(jnp.int32, (templates, templates), 0)
    lane = lax.broadcasted_iota(jnp.int32, (templates, templates), 1)
    at_local = lax.rem(position, local)
    at_row = lax.rem(lax.div(position, local), in_row) ^ lax.axis_index("row")
    at_quad = lax.rem(lax.div(position, piece_rows) + 1, quads)
    at_col = (2 * at_quad + lax.div(position, held)) ^ lax.axis_index("col")
    slots = (at_row * (2 * quads) + at_col) * local + at_local
    names = jnp.where(slots == lane, id_ref[...].astype(jnp.float32), 0.0)
    names = jnp.sum(names, axis=1, keepdims=True)
    named = jnp.where(names == lane.astype(jnp.float32), 1.0, 0.0).astype(jnp.bfloat16)
    shift = lax.dot_general(
        named,
        shifts_ref[...].astype(jnp.float32).astype(jnp.bfloat16),
        (((1,), (1,)), ((), ())),
        preferred_element_type=jnp.float32,
    )

    rest, parts = table_ref[...], []
    for _ in range(3):
        part = rest.astype(jnp.bfloat16)
        parts.append(part)
        rest = rest - part.astype(jnp.float32)
    parts = jnp.concatenate(parts, axis=0)
    numbers = lax.broadcasted_iota(jnp.int32, (piece_rows, 3 * number), 1)
    numbers = lax.rem(numbers, number).astype(jnp.float32)
    for half in range(2):
        cos_ref, sin_ref, sign_ref = outs[3 * half : 3 * half + 3]
        for place in range(quads):
            at = half * held + place * piece_rows
            for j in range(shifts):
                hit = shift[at : at + piece_rows, j : j + 1] == numbers
                to = (place * shifts + j) * piece_rows
                chosen_ref[to : to + piece_rows, :] = jnp.where(hit, 1.0, 0.0).astype(
                    jnp.bfloat16
                )
        first_ref[...] = jnp.dot(
            chosen_ref[...], parts, preferred_element_type=jnp.float32
        )

        def step(i, carry, cos_ref=cos_ref, sin_ref=sin_ref, sign_ref=sign_ref):
            here = pl.ds(pl.multiple_of(i * 32, 32), 32)
            c, s = first_ref[here, :LANES], first_ref[here, LANES:PAIR]
            dc, ds = first_ref[here, PAIR : PAIR + LANES], first_ref[here, PAIR + LANES :]
            cos_ref[0, here, :] = c
            sin_ref[0, here, :] = s
            for k in range(1, count):
                c, s = c * dc - s * ds, s * dc + c * ds
                cos_ref[k, here, :] = c
                sin_ref[k, here, :] = s
            c, s = c * dc - s * ds, s * dc + c * ds
            same = c * first_ref[here, :LANES] + s * first_ref[here, LANES:PAIR]
            sign_ref[here, :] = jnp.where(same > 0.0, 1.0, -1.0)
            return carry

        lax.fori_loop(0, rows // 32, step, 0)


def phases_of(template_id, shift_table, table, count, local, quads):
    templates, shifts = shift_table.shape
    rows = templates // 2 * shifts
    held = jax.ShapeDtypeStruct((count, rows, LANES), jnp.float32)
    sign = jax.ShapeDtypeStruct((rows, LANES), jnp.float32)
    out = pl.pallas_call(
        functools.partial(phase_kernel, local, quads),
        in_specs=whole_in_vmem(3),
        out_specs=tuple(whole_in_vmem(6)),
        out_shape=(held, held, sign) * 2,
        scratch_shapes=[
            pltpu.VMEM((rows, table.shape[1]), jnp.float32),
            pltpu.VMEM((rows, 3 * table.shape[0]), jnp.bfloat16),
        ],
        compiler_params=PARAMS,
        cost_estimate=pl.CostEstimate(
            flops=12 * count * rows * LANES,
            bytes_accessed=16 * count * rows * LANES,
            transcendentals=0,
        ),
    )(template_id.reshape(1, templates), shift_table.T, table)
    return out[:3], out[3:]


def score_kernel(places, shifts, *refs):
    pieces = len(places)
    piece_refs = refs[:pieces]
    tables = (refs[pieces : pieces + 3], refs[pieces + 3 : pieces + 6])
    x_ref, out_ref, norm_ref, rot_a, rot_b = refs[pieces + 6 :]
    images = out_ref.shape[1]
    piece_rows = piece_refs[0].shape[0]
    span = shifts * piece_rows
    block = rot_a.shape[1]
    per = block // PAIR
    half = tables[0][0].shape[0] // per

    norm_ref[...] = jnp.zeros_like(norm_ref)
    out_ref[...] = jnp.zeros_like(out_ref)

    def rotate(index, rot_ref):
        live = index < 2 * half
        index = jnp.minimum(index, 2 * half - 1)
        base = pl.multiple_of(index * block, block)
        phase = lax.rem(index, half) * per
        for g in range(per):
            at = g * PAIR
            for i, (side, place) in enumerate(places):
                cos_ref, sin_ref, _ = tables[side]
                here = slice(i * piece_rows, (i + 1) * piece_rows)
                real = piece_refs[i][:, pl.ds(base + at, LANES)].astype(jnp.float32)
                imag = piece_refs[i][:, pl.ds(base + at + LANES, LANES)].astype(jnp.float32)
                power = real * real + imag * imag
                norm_ref[here, :] += jnp.where(live, power, 0.0)
                for j in range(shifts):
                    start = place * span + j * piece_rows
                    row = slice(start, start + piece_rows)
                    c, s = cos_ref[phase + g, row, :], sin_ref[phase + g, row, :]
                    start = i * span + j * piece_rows
                    row = slice(start, start + piece_rows)
                    rot_ref[row, at : at + LANES] = (real * c + imag * s).astype(jnp.bfloat16)
                    rot_ref[row, at + LANES : at + PAIR] = (imag * c - real * s).astype(
                        jnp.bfloat16
                    )

    def gather_scores(index, rot_ref):
        base = pl.multiple_of(index * block, block)
        out_ref[...] += lax.dot_general(
            rot_ref[...],
            x_ref[0:images, pl.ds(base, block)],
            (((1,), (1,)), ((), ())),
            preferred_element_type=jnp.float32,
        )

    def turn_sign():
        for n in range(images // LANES):
            lanes = slice(n * LANES, (n + 1) * LANES)
            for i, (side, place) in enumerate(places):
                sign = tables[side][2][place * span : (place + 1) * span, :]
                row = slice(i * span, (i + 1) * span)
                out_ref[row, lanes] = out_ref[row, lanes] * sign

    rotate(jnp.int32(0), rot_a)

    def step(i, carry):
        for at in range(0, UNROLL, 2):
            index = i * UNROLL + at
            gather_scores(index, rot_a)
            rotate(index + 1, rot_b)
            gather_scores(index + 1, rot_b)
            rotate(index + 2, rot_a)
        return carry

    lax.fori_loop(0, half // UNROLL, step, 0)
    turn_sign()
    lax.fori_loop(half // UNROLL, 2 * half // UNROLL, step, 0)
    turn_sign()


def scores_of(piece_list, places, tables, shifts, x, images, groups=2):
    pieces = len(piece_list)
    rows, width = piece_list[0].shape
    held = pieces * rows
    rotated = pltpu.VMEM((shifts * held, groups * PAIR), jnp.bfloat16)
    return pl.pallas_call(
        functools.partial(score_kernel, places, shifts),
        in_specs=whole_in_vmem(pieces + 7),
        out_specs=tuple(whole_in_vmem(2)),
        out_shape=(
            jax.ShapeDtypeStruct((shifts * held, images), jnp.float32),
            jax.ShapeDtypeStruct((held, LANES), jnp.float32),
        ),
        scratch_shapes=[rotated, rotated],
        compiler_params=PARAMS,
        cost_estimate=pl.CostEstimate(
            flops=2 * shifts * held * images * width,
            bytes_accessed=2 * images * width + 8 * shifts * held * images,
            transcendentals=0,
        ),
    )(*piece_list, *tables[0], *tables[1], x)


def weight_kernel(layout, shifts, piece_rows, *refs):
    blocks = len(layout)
    score_refs, norm_refs = refs[:blocks], refs[blocks : 2 * blocks]
    prec_ref, x_ref = refs[2 * blocks : 2 * blocks + 2]
    outs, raised_refs = refs[2 * blocks + 2 : 2 * blocks + 8], refs[2 * blocks + 8 :]
    images = prec_ref.shape[1]
    span = shifts * piece_rows
    peak = jnp.max(x_ref[images:, :LANES].astype(jnp.float32)) * math.sqrt(2.0)
    prec = prec_ref[...][None]

    def cube(value):
        return value.reshape(-1, piece_rows, value.shape[-1])

    top = None
    for places, score_ref, norm_ref, raised_ref in zip(
        layout, score_refs, norm_refs, raised_refs
    ):
        norm = 0.5 * jnp.sum(norm_ref[...], axis=1, keepdims=True)
        for i in range(len(places)):
            row = slice(i * span, (i + 1) * span)
            bias = norm[i * piece_rows : (i + 1) * piece_rows][None]
            value = prec * (cube(score_ref[row, :]) - bias)
            raised_ref[row, :] = value.reshape(span, images)
            best = jnp.max(jnp.max(value, axis=0), axis=0, keepdims=True)
            top = best if top is None else jnp.maximum(top, best)
    norm = None
    for places, raised_ref in zip(layout, raised_refs):
        for i in range(len(places)):
            row = slice(i * span, (i + 1) * span)
            raised = jnp.exp(raised_ref[row, :] - top)
            raised_ref[row, :] = raised
            part = jnp.sum(jnp.sum(cube(raised), axis=0), axis=0, keepdims=True)
            norm = part if norm is None else norm + part
    inverse = 1.0 / norm
    for places, raised_ref in zip(layout, raised_refs):
        for i, (side, place) in enumerate(places):
            weight = (raised_ref[i * span : (i + 1) * span, :] * inverse).astype(jnp.bfloat16)
            outs[side][place * span : (place + 1) * span, :] = weight
            total = jnp.sum(cube(weight.astype(jnp.float32)), axis=0)
            total = jnp.sum(total, axis=1, keepdims=True)
            total = jnp.broadcast_to(total, (piece_rows, LANES))
            here = slice(place * piece_rows, (place + 1) * piece_rows)
            outs[2 + side][here, :] = total
            outs[4 + side][here, :] = total * peak


def weights_of(scores, layout, precision, x, shifts, held, piece_rows):
    images = precision.shape[0]
    weight = jax.ShapeDtypeStruct((shifts * held, images), jnp.bfloat16)
    total = jax.ShapeDtypeStruct((held, LANES), jnp.float32)
    rows = 2 * shifts * held
    own_w, other_w, own_t, other_t, own_b, other_b = pl.pallas_call(
        functools.partial(weight_kernel, layout, shifts, piece_rows),
        in_specs=whole_in_vmem(2 * len(layout) + 2),
        out_specs=tuple(whole_in_vmem(6)),
        out_shape=(weight, weight, total, total, total, total),
        scratch_shapes=[pltpu.VMEM(value.shape, jnp.float32) for value, _ in scores],
        compiler_params=PARAMS,
        cost_estimate=pl.CostEstimate(
            flops=20 * rows * images,
            bytes_accessed=12 * rows * images,
            transcendentals=2 * rows * images,
        ),
    )(
        *[value for value, _ in scores],
        *[value for _, value in scores],
        precision.reshape(1, images),
        x,
    )
    return (own_w, own_t[:, :1], own_b[:, :1]), (other_w, other_t[:, :1], other_b[:, :1])


def back_kernel(first, pieces, shifts, w_ref, cos_ref, sin_ref, sign_ref, x_ref, *refs):
    out_ref, turned_ref, mix_a, mix_b = refs
    rows, images = turned_ref.shape
    span = rows // pieces
    piece_rows = span // shifts
    count = cos_ref.shape[0]
    first = first * span
    used = slice(first, first + rows)
    for n in range(images // LANES):
        lanes = slice(n * LANES, (n + 1) * LANES)
        wide = w_ref[used, lanes].astype(jnp.float32) * sign_ref[used, :]
        turned_ref[:, lanes] = wide.astype(jnp.bfloat16)

    def mix(index, mix_ref):
        index = jnp.minimum(index, count - 1)
        for second in range(2):
            weight = turned_ref[...] if second else w_ref[used, :]
            base = pl.multiple_of((second * count + index) * PAIR, PAIR)
            mix_ref[:, second * PAIR : (second + 1) * PAIR] = jnp.dot(
                weight, x_ref[0:images, pl.ds(base, PAIR)], preferred_element_type=jnp.float32
            )

    def turn(index, mix_ref):
        for i in range(pieces):
            for t in range(0, piece_rows, 8):
                total = [None] * 4
                for j in range(shifts):
                    start = i * span + j * piece_rows + t
                    row = slice(start, start + 8)
                    at_row = slice(first + start, first + start + 8)
                    c, s = cos_ref[index, at_row, :], sin_ref[index, at_row, :]
                    terms = []
                    for second in range(2):
                        at = second * PAIR
                        real = mix_ref[row, at : at + LANES]
                        imag = mix_ref[row, at + LANES : at + PAIR]
                        terms += [real * c - imag * s, imag * c + real * s]
                    total = [b if a is None else a + b for a, b in zip(total, terms)]
                here = slice(i * piece_rows + t, i * piece_rows + t + 8)
                for part in range(4):
                    base = (part // 2 * count + index) * PAIR + part % 2 * LANES
                    out_ref[here, pl.ds(pl.multiple_of(base, LANES), LANES)] = total[part]

    mix(jnp.int32(0), mix_a)

    def step(i, carry):
        for at in range(0, UNROLL, 2):
            index = i * UNROLL + at
            mix(index + 1, mix_b)
            turn(index, mix_a)
            mix(index + 2, mix_a)
            turn(index + 1, mix_b)
        return carry

    lax.fori_loop(0, count // UNROLL, step, 0)


def back_of(weight, x, phases, shifts, first, pieces, piece_rows):
    images = weight.shape[1]
    rows = pieces * shifts * piece_rows
    width = x.shape[1]
    mixed = pltpu.VMEM((rows, 2 * PAIR), jnp.float32)
    return pl.pallas_call(
        functools.partial(back_kernel, first, pieces, shifts),
        in_specs=whole_in_vmem(5),
        out_specs=whole_in_vmem(1)[0],
        out_shape=jax.ShapeDtypeStruct((pieces * piece_rows, width), jnp.float32),
        scratch_shapes=[pltpu.VMEM((rows, images), jnp.bfloat16), mixed, mixed],
        compiler_params=PARAMS,
        cost_estimate=pl.CostEstimate(
            flops=2 * rows * images * width,
            bytes_accessed=2 * images * width + 2 * rows * images + 4 * pieces * width,
            transcendentals=0,
        ),
    )(weight, *phases, x)


def exchange(value, axis, size, bit):
    return lax.ppermute(value, axis, [(i, i ^ bit) for i in range(size)])


def body(images, precision, templates, template_id, shift_table):
    image_count, parts, coeffs = images.shape
    local = templates.shape[0]
    shifts = shift_table.shape[1]
    rows, cols = lax.axis_size("row"), lax.axis_size("col")
    quads = cols // 2
    groups = coeffs // LANES
    width = parts * coeffs
    held = local * rows * quads

    mine = templates.reshape(local, parts, groups, LANES)
    mine = mine.transpose(0, 2, 1, 3).reshape(local, width)

    row_set = [mine]
    row_set += [exchange(mine, "row", rows, d) for d in range(1, rows)]
    own_set = [jnp.concatenate(row_set, axis=0)]
    for d in range(1, quads):
        own_set.append(exchange(own_set[0], "col", cols, 2 * d))
    other_set = []
    for d in range(quads):
        other_set.append(exchange(own_set[d], "col", cols, 1))

    x = relay(images)

    piece_rows = local * rows

    number = jnp.arange(SHIFT_SIDE * SHIFT_SIDE, dtype=jnp.int32)[:, None]
    step_x = number // SHIFT_SIDE - SHIFT_SIDE // 2
    step_y = number % SHIFT_SIDE - SHIFT_SIDE // 2
    lane = jnp.arange(LANES, dtype=jnp.int32)[None, :]
    freq_x = lane // GRID - GRID // 2
    freq_y = lane % GRID - GRID // 2
    first = (step_x * freq_x + step_y * freq_y) % GRID
    stride = jnp.broadcast_to(step_x * (LANES // GRID) % GRID, first.shape)
    angle = jnp.concatenate([first, stride], axis=1).astype(jnp.float32)
    angle = angle * (2.0 * math.pi / GRID)
    table = [jnp.cos(angle), jnp.sin(angle)]
    table = [part[:, at : at + LANES] for at in (0, LANES) for part in table]
    table = jnp.concatenate(table, axis=1)
    tables = phases_of(template_id, shift_table, table, groups // 2, local, quads)

    layout = [
        tuple((0, (d - 1) % quads) for d in range(quads - 1)),
        tuple((1, (d - 1) % quads) for d in range(quads - 1)),
        ((0, quads - 2), (1, quads - 2)),
    ]
    piece_lists = [own_set[:-1], other_set[:-1], [own_set[-1], other_set[-1]]]
    scores = []
    for number, (piece_list, places) in enumerate(zip(piece_lists, layout)):
        scores.append(scores_of(piece_list, places, tables, shifts, x, image_count))
    own, other = weights_of(scores, layout, precision, x, shifts, held, piece_rows)

    def pack(held_rows):
        value, total, bound = held_rows
        power = jnp.ceil(jnp.log2(jnp.maximum(bound, 1e-30))) - 15.0
        at = jnp.arange(LANES, dtype=jnp.int32)[None, :]
        extra = jnp.where(at == 0, total, jnp.where(at == 1, power, 0.0))
        return jnp.concatenate([value * jnp.exp2(-power), extra], axis=1).astype(WIRE)

    def unpack(payload):
        got = payload.astype(jnp.float32)
        total, power = got[:, width : width + 1], got[:, width + 1 : width + 2]
        return got[:, :width] * jnp.exp2(power), total, jnp.exp2(power + 15.0)

    def send(held_rows, axis, size, bit):
        return unpack(exchange(pack(held_rows), axis, size, bit))

    def add(first, *others):
        for other in others:
            first = tuple(a + b for a, b in zip(first, other))
        return first

    def cut(held_rows, at, count):
        return tuple(value[at * count : (at + 1) * count] for value in held_rows)

    other_back = back_of(other[0], x, tables[1], shifts, 0, quads, piece_rows)
    got = send((other_back,) + other[1:], "col", cols, 1)
    per_set = quads // 2
    set_rows = per_set * piece_rows
    own_weight = own[0]
    sums, received = [], []
    for number in range(2):
        back = back_of(
            own_weight, x, tables[0], shifts, number * per_set, per_set, piece_rows
        )
        whole = add((back,) + cut(own[1:], number, set_rows), cut(got, number, set_rows))
        pieces = [cut(whole, place, piece_rows) for place in range(per_set)]
        if number:
            sums.append(pieces.pop())
        pieces = [pack(piece) for piece in pieces]
        if not number:
            *pieces, own_weight = lax.optimization_barrier((*pieces, own_weight))
        for place, piece in enumerate(pieces):
            d = number * per_set + place + 1
            received.append(unpack(exchange(piece, "col", cols, 2 * d)))
    whole = add(sums[0], *received)
    got = [send(cut(whole, d, local), "row", rows, d) for d in range(1, rows)]
    summed, totals, _ = add(cut(whole, 0, local), *got)
    prior = mine.astype(jnp.float32)
    out = (summed + PRIOR_WEIGHT * prior) / (totals + PRIOR_WEIGHT)
    out = out.reshape(local, groups, parts, LANES).transpose(0, 2, 1, 3)
    return out.reshape(local, parts, coeffs)


def solution(mesh):
    return jax.shard_map(
        body,
        mesh=mesh,
        in_specs=(
            P(("row", "col"), None, None),
            P(("row", "col")),
            P(("row", "col"), None, None),
            P(),
            P(),
        ),
        out_specs=P(("row", "col"), None, None),
        check_vma=False,
    )
```

```python
import functools
import math

import jax
import jax.numpy as jnp
from jax import lax
from jax.experimental import pallas as pl
from jax.experimental.pallas import tpu as pltpu
from jax.sharding import PartitionSpec as P


GRID = 64
SHIFT_SIDE = 8
PRIOR_WEIGHT = 4.0
LANES = 128
PAIR = 2 * LANES
UNROLL = 8
WIRE = jnp.float16
VMEM_LIMIT = 8 << 20
RELAY_LIMIT = 14 << 20

PARAMS = pltpu.CompilerParams(vmem_limit_bytes=VMEM_LIMIT)


def whole_in_vmem(count):
    return [pl.BlockSpec(memory_space=pltpu.VMEM)] * count


def relay_kernel(in_ref, out_ref, taken_ref, wide_ref, peak_ref, sems):
    blocks, some, per, _ = taken_ref.shape
    rows = peak_ref.shape[0]
    count = blocks * some
    last = out_ref.shape[0]
    pitch = rows + 1

    def fetch(block):
        return pltpu.make_async_copy(
            in_ref.at[pl.ds(block * some, some)], taken_ref.at[block], sems.at[block]
        )

    for block in range(blocks):
        fetch(block).start()
    peak_ref[...] = jnp.zeros_like(peak_ref)

    def step(block, carry):
        fetch(block).wait()
        base = pl.multiple_of(block * some, some)
        peak = peak_ref[...]
        for n in range(0, some, 16):
            for r in range(0, per, rows):
                start = (n // 16 * (per // rows) + r // rows) * 16 * pitch
                for m in range(16):
                    wide = taken_ref[block, n + m, r : r + rows, :].astype(jnp.float32)
                    peak = jnp.maximum(peak, jnp.abs(wide))
                    at = start + m * pitch
                    wide_ref[at : at + rows, :] = wide
                for k in range(rows):
                    picked = wide_ref[pl.ds(start + k, 16, stride=pitch), :]
                    at = (r + k) * LANES
                    out_ref[pl.ds(base + n, 16), at : at + LANES] = picked.astype(jnp.bfloat16)
        peak_ref[...] = peak
        return carry

    lax.fori_loop(0, blocks, step, 0)
    peak = jnp.max(peak_ref[...], axis=0, keepdims=True)
    out_ref[count:last, :LANES] = jnp.broadcast_to(peak, (last - count, LANES)).astype(
        jnp.bfloat16
    )


def flat_rows(value, lead):
    count, parts, coeffs = value.shape
    groups = coeffs // LANES
    value = value.reshape(count, parts, groups, LANES)
    return value.transpose(0, 2, 1, 3).reshape(lead + (LANES,))


def relay(images, rows=8, spare=16):
    count, parts, coeffs = images.shape
    per = parts * (coeffs // LANES)
    some = min(count, 64)
    flat = pltpu.with_memory_space_constraint(flat_rows(images, (count, per)), pltpu.HBM)
    return pl.pallas_call(
        relay_kernel,
        in_specs=[pl.BlockSpec(memory_space=pltpu.HBM)],
        out_specs=pl.BlockSpec(memory_space=pltpu.VMEM),
        out_shape=jax.ShapeDtypeStruct((count + spare, per * LANES), jnp.bfloat16),
        scratch_shapes=[
            pltpu.VMEM((count // some, some, per, LANES), jnp.bfloat16),
            pltpu.VMEM((some * per // rows * (rows + 1), LANES), jnp.float32),
            pltpu.VMEM((rows, LANES), jnp.float32),
            pltpu.SemaphoreType.DMA((count // some,)),
        ],
        compiler_params=pltpu.CompilerParams(vmem_limit_bytes=RELAY_LIMIT),
        cost_estimate=pl.CostEstimate(
            flops=count * per * LANES,
            bytes_accessed=4 * count * per * LANES,
            transcendentals=0,
        ),
    )(flat)


def lay_kernel(in_ref, out_ref, wide_ref):
    local, width = out_ref.shape
    per = width // LANES
    wide_ref[...] = in_ref[...].astype(jnp.float32)
    for r in range(per):
        picked = wide_ref[pl.ds(r, local, stride=per), :]
        out_ref[:, r * LANES : (r + 1) * LANES] = picked.astype(out_ref.dtype)


def unlay_kernel(in_ref, out_ref):
    local, width = in_ref.shape
    per = width // LANES
    for r in range(per):
        out_ref[pl.ds(r, local, stride=per), :] = in_ref[:, r * LANES : (r + 1) * LANES]


def lay(templates):
    local, parts, coeffs = templates.shape
    width = parts * coeffs
    rows = local * width // LANES
    return pl.pallas_call(
        lay_kernel,
        in_specs=whole_in_vmem(1),
        out_specs=whole_in_vmem(1)[0],
        out_shape=jax.ShapeDtypeStruct((local, width), templates.dtype),
        scratch_shapes=[pltpu.VMEM((rows, LANES), jnp.float32)],
        compiler_params=PARAMS,
    )(flat_rows(templates, (rows,)))


def unlay(value, parts):
    local, width = value.shape
    groups = width // parts // LANES
    flat = pl.pallas_call(
        unlay_kernel,
        in_specs=whole_in_vmem(1),
        out_specs=whole_in_vmem(1)[0],
        out_shape=jax.ShapeDtypeStruct((local * width // LANES, LANES), value.dtype),
        compiler_params=PARAMS,
    )(value)
    flat = flat.reshape(local, groups, parts, LANES).transpose(0, 2, 1, 3)
    return flat.reshape(local, parts, width // parts)


def phase_kernel(local, quads, id_ref, shifts_ref, table_ref, *refs):
    outs, first_ref, chosen_ref = refs[:6], refs[6], refs[7]
    count, rows, _ = outs[0].shape
    number = table_ref.shape[0]
    shifts, templates = shifts_ref.shape
    held = templates // 2
    piece_rows = held // quads
    in_row = piece_rows // local

    position = lax.broadcasted_iota(jnp.int32, (templates, templates), 0)
    lane = lax.broadcasted_iota(jnp.int32, (templates, templates), 1)
    at_local = lax.rem(position, local)
    at_row = lax.rem(lax.div(position, local), in_row) ^ lax.axis_index("row")
    at_quad = lax.rem(lax.div(position, piece_rows) + 1, quads)
    at_col = (2 * at_quad + lax.div(position, held)) ^ lax.axis_index("col")
    slots = (at_row * (2 * quads) + at_col) * local + at_local
    names = jnp.where(slots == lane, id_ref[...].astype(jnp.float32), 0.0)
    names = jnp.sum(names, axis=1, keepdims=True)
    named = jnp.where(names == lane.astype(jnp.float32), 1.0, 0.0).astype(jnp.bfloat16)
    shift = lax.dot_general(
        named,
        shifts_ref[...].astype(jnp.float32).astype(jnp.bfloat16),
        (((1,), (1,)), ((), ())),
        preferred_element_type=jnp.float32,
    )

    rest, parts = table_ref[...], []
    for _ in range(3):
        part = rest.astype(jnp.bfloat16)
        parts.append(part)
        rest = rest - part.astype(jnp.float32)
    parts = jnp.concatenate(parts, axis=0)
    numbers = lax.broadcasted_iota(jnp.int32, (piece_rows, 3 * number), 1)
    numbers = lax.rem(numbers, number).astype(jnp.float32)
    for half in range(2):
        cos_ref, sin_ref, sign_ref = outs[3 * half : 3 * half + 3]
        for place in range(quads):
            at = half * held + place * piece_rows
            for j in range(shifts):
                hit = shift[at : at + piece_rows, j : j + 1] == numbers
                to = (place * shifts + j) * piece_rows
                chosen_ref[to : to + piece_rows, :] = jnp.where(hit, 1.0, 0.0).astype(
                    jnp.bfloat16
                )
        first_ref[...] = jnp.dot(
            chosen_ref[...], parts, preferred_element_type=jnp.float32
        )

        def step(i, carry, cos_ref=cos_ref, sin_ref=sin_ref, sign_ref=sign_ref):
            here = pl.ds(pl.multiple_of(i * 32, 32), 32)
            c, s = first_ref[here, :LANES], first_ref[here, LANES:PAIR]
            dc, ds = first_ref[here, PAIR : PAIR + LANES], first_ref[here, PAIR + LANES :]
            cos_ref[0, here, :] = c
            sin_ref[0, here, :] = s
            for k in range(1, count):
                c, s = c * dc - s * ds, s * dc + c * ds
                cos_ref[k, here, :] = c
                sin_ref[k, here, :] = s
            c, s = c * dc - s * ds, s * dc + c * ds
            same = c * first_ref[here, :LANES] + s * first_ref[here, LANES:PAIR]
            sign_ref[here, :] = jnp.where(same > 0.0, 1.0, -1.0)
            return carry

        lax.fori_loop(0, rows // 32, step, 0)


def phases_of(template_id, shift_table, table, count, local, quads):
    templates, shifts = shift_table.shape
    rows = templates // 2 * shifts
    held = jax.ShapeDtypeStruct((count, rows, LANES), jnp.float32)
    sign = jax.ShapeDtypeStruct((rows, LANES), jnp.float32)
    out = pl.pallas_call(
        functools.partial(phase_kernel, local, quads),
        in_specs=whole_in_vmem(3),
        out_specs=tuple(whole_in_vmem(6)),
        out_shape=(held, held, sign) * 2,
        scratch_shapes=[
            pltpu.VMEM((rows, table.shape[1]), jnp.float32),
            pltpu.VMEM((rows, 3 * table.shape[0]), jnp.bfloat16),
        ],
        compiler_params=PARAMS,
        cost_estimate=pl.CostEstimate(
            flops=12 * count * rows * LANES,
            bytes_accessed=16 * count * rows * LANES,
            transcendentals=0,
        ),
    )(template_id.reshape(1, templates), shift_table.T, table)
    return out[:3], out[3:]


def score_kernel(places, shifts, *refs):
    pieces = len(places)
    piece_refs = refs[:pieces]
    tables = (refs[pieces : pieces + 3], refs[pieces + 3 : pieces + 6])
    x_ref, out_ref, norm_ref, rot_a, rot_b = refs[pieces + 6 :]
    images = out_ref.shape[1]
    piece_rows = piece_refs[0].shape[0]
    span = shifts * piece_rows
    block = rot_a.shape[1]
    per = block // PAIR
    half = tables[0][0].shape[0] // per

    norm_ref[...] = jnp.zeros_like(norm_ref)
    out_ref[...] = jnp.zeros_like(out_ref)

    def rotate(index, rot_ref):
        live = index < 2 * half
        index = jnp.minimum(index, 2 * half - 1)
        base = pl.multiple_of(index * block, block)
        phase = lax.rem(index, half) * per
        for g in range(per):
            at = g * PAIR
            for i, (side, place) in enumerate(places):
                cos_ref, sin_ref, _ = tables[side]
                here = slice(i * piece_rows, (i + 1) * piece_rows)
                real = piece_refs[i][:, pl.ds(base + at, LANES)].astype(jnp.float32)
                imag = piece_refs[i][:, pl.ds(base + at + LANES, LANES)].astype(jnp.float32)
                power = real * real + imag * imag
                norm_ref[here, :] += jnp.where(live, power, 0.0)
                for j in range(shifts):
                    start = place * span + j * piece_rows
                    row = slice(start, start + piece_rows)
                    c, s = cos_ref[phase + g, row, :], sin_ref[phase + g, row, :]
                    start = i * span + j * piece_rows
                    row = slice(start, start + piece_rows)
                    rot_ref[row, at : at + LANES] = (real * c + imag * s).astype(jnp.bfloat16)
                    rot_ref[row, at + LANES : at + PAIR] = (imag * c - real * s).astype(
                        jnp.bfloat16
                    )

    def gather_scores(index, rot_ref):
        base = pl.multiple_of(index * block, block)
        out_ref[...] += lax.dot_general(
            rot_ref[...],
            x_ref[0:images, pl.ds(base, block)],
            (((1,), (1,)), ((), ())),
            preferred_element_type=jnp.float32,
        )

    def turn_sign():
        for n in range(images // LANES):
            lanes = slice(n * LANES, (n + 1) * LANES)
            for i, (side, place) in enumerate(places):
                sign = tables[side][2][place * span : (place + 1) * span, :]
                row = slice(i * span, (i + 1) * span)
                out_ref[row, lanes] = out_ref[row, lanes] * sign

    rotate(jnp.int32(0), rot_a)

    def step(i, carry):
        for at in range(0, UNROLL, 2):
            index = i * UNROLL + at
            gather_scores(index, rot_a)
            rotate(index + 1, rot_b)
            gather_scores(index + 1, rot_b)
            rotate(index + 2, rot_a)
        return carry

    lax.fori_loop(0, half // UNROLL, step, 0)
    turn_sign()
    lax.fori_loop(half // UNROLL, 2 * half // UNROLL, step, 0)
    turn_sign()


def scores_of(piece_list, places, tables, shifts, x, images, groups=2):
    pieces = len(piece_list)
    rows, width = piece_list[0].shape
    held = pieces * rows
    rotated = pltpu.VMEM((shifts * held, groups * PAIR), jnp.bfloat16)
    return pl.pallas_call(
        functools.partial(score_kernel, places, shifts),
        in_specs=whole_in_vmem(pieces + 7),
        out_specs=tuple(whole_in_vmem(2)),
        out_shape=(
            jax.ShapeDtypeStruct((shifts * held, images), jnp.float32),
            jax.ShapeDtypeStruct((held, LANES), jnp.float32),
        ),
        scratch_shapes=[rotated, rotated],
        compiler_params=PARAMS,
        cost_estimate=pl.CostEstimate(
            flops=2 * shifts * held * images * width,
            bytes_accessed=2 * images * width + 8 * shifts * held * images,
            transcendentals=0,
        ),
    )(*piece_list, *tables[0], *tables[1], x)


def weight_kernel(layout, shifts, piece_rows, *refs):
    blocks = len(layout)
    score_refs, norm_refs = refs[:blocks], refs[blocks : 2 * blocks]
    prec_ref, x_ref = refs[2 * blocks : 2 * blocks + 2]
    outs, raised_refs = refs[2 * blocks + 2 : 2 * blocks + 8], refs[2 * blocks + 8 :]
    images = prec_ref.shape[1]
    span = shifts * piece_rows
    peak = jnp.max(x_ref[images:, :LANES].astype(jnp.float32)) * math.sqrt(2.0)
    prec = prec_ref[...][None]

    def cube(value):
        return value.reshape(-1, piece_rows, value.shape[-1])

    top = None
    for places, score_ref, norm_ref, raised_ref in zip(
        layout, score_refs, norm_refs, raised_refs
    ):
        norm = 0.5 * jnp.sum(norm_ref[...], axis=1, keepdims=True)
        for i in range(len(places)):
            row = slice(i * span, (i + 1) * span)
            bias = norm[i * piece_rows : (i + 1) * piece_rows][None]
            value = prec * (cube(score_ref[row, :]) - bias)
            raised_ref[row, :] = value.reshape(span, images)
            best = jnp.max(jnp.max(value, axis=0), axis=0, keepdims=True)
            top = best if top is None else jnp.maximum(top, best)
    norm = None
    for places, raised_ref in zip(layout, raised_refs):
        for i in range(len(places)):
            row = slice(i * span, (i + 1) * span)
            raised = jnp.exp(raised_ref[row, :] - top)
            raised_ref[row, :] = raised
            part = jnp.sum(jnp.sum(cube(raised), axis=0), axis=0, keepdims=True)
            norm = part if norm is None else norm + part
    inverse = 1.0 / norm
    for places, raised_ref in zip(layout, raised_refs):
        for i, (side, place) in enumerate(places):
            weight = (raised_ref[i * span : (i + 1) * span, :] * inverse).astype(jnp.bfloat16)
            outs[side][place * span : (place + 1) * span, :] = weight
            total = jnp.sum(cube(weight.astype(jnp.float32)), axis=0)
            total = jnp.sum(total, axis=1, keepdims=True)
            total = jnp.broadcast_to(total, (piece_rows, LANES))
            here = slice(place * piece_rows, (place + 1) * piece_rows)
            outs[2 + side][here, :] = total
            outs[4 + side][here, :] = total * peak


def weights_of(scores, layout, precision, x, shifts, held, piece_rows):
    images = precision.shape[0]
    weight = jax.ShapeDtypeStruct((shifts * held, images), jnp.bfloat16)
    total = jax.ShapeDtypeStruct((held, LANES), jnp.float32)
    rows = 2 * shifts * held
    own_w, other_w, own_t, other_t, own_b, other_b = pl.pallas_call(
        functools.partial(weight_kernel, layout, shifts, piece_rows),
        in_specs=whole_in_vmem(2 * len(layout) + 2),
        out_specs=tuple(whole_in_vmem(6)),
        out_shape=(weight, weight, total, total, total, total),
        scratch_shapes=[pltpu.VMEM(value.shape, jnp.float32) for value, _ in scores],
        compiler_params=PARAMS,
        cost_estimate=pl.CostEstimate(
            flops=20 * rows * images,
            bytes_accessed=12 * rows * images,
            transcendentals=2 * rows * images,
        ),
    )(
        *[value for value, _ in scores],
        *[value for _, value in scores],
        precision.reshape(1, images),
        x,
    )
    return (own_w, own_t[:, :1], own_b[:, :1]), (other_w, other_t[:, :1], other_b[:, :1])


def back_kernel(first, pieces, shifts, w_ref, cos_ref, sin_ref, sign_ref, x_ref, *refs):
    out_ref, turned_ref, mix_a, mix_b = refs
    rows, images = turned_ref.shape
    span = rows // pieces
    piece_rows = span // shifts
    count = cos_ref.shape[0]
    first = first * span
    used = slice(first, first + rows)
    for n in range(images // LANES):
        lanes = slice(n * LANES, (n + 1) * LANES)
        wide = w_ref[used, lanes].astype(jnp.float32) * sign_ref[used, :]
        turned_ref[:, lanes] = wide.astype(jnp.bfloat16)

    def mix(index, mix_ref):
        index = jnp.minimum(index, count - 1)
        for second in range(2):
            weight = turned_ref[...] if second else w_ref[used, :]
            base = pl.multiple_of((second * count + index) * PAIR, PAIR)
            mix_ref[:, second * PAIR : (second + 1) * PAIR] = jnp.dot(
                weight, x_ref[0:images, pl.ds(base, PAIR)], preferred_element_type=jnp.float32
            )

    def turn(index, mix_ref):
        for i in range(pieces):
            for t in range(0, piece_rows, 8):
                total = [None] * 4
                for j in range(shifts):
                    start = i * span + j * piece_rows + t
                    row = slice(start, start + 8)
                    at_row = slice(first + start, first + start + 8)
                    c, s = cos_ref[index, at_row, :], sin_ref[index, at_row, :]
                    terms = []
                    for second in range(2):
                        at = second * PAIR
                        real = mix_ref[row, at : at + LANES]
                        imag = mix_ref[row, at + LANES : at + PAIR]
                        terms += [real * c - imag * s, imag * c + real * s]
                    total = [b if a is None else a + b for a, b in zip(total, terms)]
                here = slice(i * piece_rows + t, i * piece_rows + t + 8)
                for part in range(4):
                    base = (part // 2 * count + index) * PAIR + part % 2 * LANES
                    out_ref[here, pl.ds(pl.multiple_of(base, LANES), LANES)] = total[part]

    mix(jnp.int32(0), mix_a)

    def step(i, carry):
        for at in range(0, UNROLL, 2):
            index = i * UNROLL + at
            mix(index + 1, mix_b)
            turn(index, mix_a)
            mix(index + 2, mix_a)
            turn(index + 1, mix_b)
        return carry

    lax.fori_loop(0, count // UNROLL, step, 0)


def back_of(weight, x, phases, shifts, first, pieces, piece_rows):
    images = weight.shape[1]
    rows = pieces * shifts * piece_rows
    width = x.shape[1]
    mixed = pltpu.VMEM((rows, 2 * PAIR), jnp.float32)
    return pl.pallas_call(
        functools.partial(back_kernel, first, pieces, shifts),
        in_specs=whole_in_vmem(5),
        out_specs=whole_in_vmem(1)[0],
        out_shape=jax.ShapeDtypeStruct((pieces * piece_rows, width), jnp.float32),
        scratch_shapes=[pltpu.VMEM((rows, images), jnp.bfloat16), mixed, mixed],
        compiler_params=PARAMS,
        cost_estimate=pl.CostEstimate(
            flops=2 * rows * images * width,
            bytes_accessed=2 * images * width + 2 * rows * images + 4 * pieces * width,
            transcendentals=0,
        ),
    )(weight, *phases, x)


def exchange(value, axis, size, bit):
    return lax.ppermute(value, axis, [(i, i ^ bit) for i in range(size)])


def body(images, precision, templates, template_id, shift_table):
    image_count, parts, coeffs = images.shape
    local = templates.shape[0]
    shifts = shift_table.shape[1]
    rows, cols = lax.axis_size("row"), lax.axis_size("col")
    quads = cols // 2
    groups = coeffs // LANES
    width = parts * coeffs
    held = local * rows * quads

    mine = lay(templates)
    row_set = [mine]
    row_set += [exchange(mine, "row", rows, d) for d in range(1, rows)]
    own_set = [jnp.concatenate(row_set, axis=0)]
    for d in range(1, quads):
        own_set.append(exchange(own_set[0], "col", cols, 2 * d))
    other_set = []
    for d in range(quads):
        other_set.append(exchange(own_set[d], "col", cols, 1))

    x = relay(images)

    piece_rows = local * rows

    number = jnp.arange(SHIFT_SIDE * SHIFT_SIDE, dtype=jnp.int32)[:, None]
    step_x = number // SHIFT_SIDE - SHIFT_SIDE // 2
    step_y = number % SHIFT_SIDE - SHIFT_SIDE // 2
    lane = jnp.arange(LANES, dtype=jnp.int32)[None, :]
    freq_x = lane // GRID - GRID // 2
    freq_y = lane % GRID - GRID // 2
    first = (step_x * freq_x + step_y * freq_y) % GRID
    stride = jnp.broadcast_to(step_x * (LANES // GRID) % GRID, first.shape)
    angle = jnp.concatenate([first, stride], axis=1).astype(jnp.float32)
    angle = angle * (2.0 * math.pi / GRID)
    table = [jnp.cos(angle), jnp.sin(angle)]
    table = [part[:, at : at + LANES] for at in (0, LANES) for part in table]
    table = jnp.concatenate(table, axis=1)
    tables = phases_of(template_id, shift_table, table, groups // 2, local, quads)

    layout = [
        tuple((0, (d - 1) % quads) for d in range(quads - 1)),
        tuple((1, (d - 1) % quads) for d in range(quads - 1)),
        ((0, quads - 2), (1, quads - 2)),
    ]
    piece_lists = [own_set[:-1], other_set[:-1], [own_set[-1], other_set[-1]]]
    scores = []
    for number, (piece_list, places) in enumerate(zip(piece_lists, layout)):
        scores.append(scores_of(piece_list, places, tables, shifts, x, image_count))
    own, other = weights_of(scores, layout, precision, x, shifts, held, piece_rows)

    def pack(held_rows):
        value, total, bound = held_rows
        power = jnp.ceil(jnp.log2(jnp.maximum(bound, 1e-30))) - 15.0
        at = jnp.arange(LANES, dtype=jnp.int32)[None, :]
        extra = jnp.where(at == 0, total, jnp.where(at == 1, power, 0.0))
        return jnp.concatenate([value * jnp.exp2(-power), extra], axis=1).astype(WIRE)

    def unpack(payload):
        got = payload.astype(jnp.float32)
        total, power = got[:, width : width + 1], got[:, width + 1 : width + 2]
        return got[:, :width] * jnp.exp2(power), total, jnp.exp2(power + 15.0)

    def send(held_rows, axis, size, bit):
        return unpack(exchange(pack(held_rows), axis, size, bit))

    def add(first, *others):
        for other in others:
            first = tuple(a + b for a, b in zip(first, other))
        return first

    def cut(held_rows, at, count):
        return tuple(value[at * count : (at + 1) * count] for value in held_rows)

    other_back = back_of(other[0], x, tables[1], shifts, 0, quads, piece_rows)
    got = send((other_back,) + other[1:], "col", cols, 1)
    per_set = quads // 2
    set_rows = per_set * piece_rows
    own_weight = own[0]
    sums, received = [], []
    for number in range(2):
        back = back_of(
            own_weight, x, tables[0], shifts, number * per_set, per_set, piece_rows
        )
        whole = add((back,) + cut(own[1:], number, set_rows), cut(got, number, set_rows))
        pieces = [cut(whole, place, piece_rows) for place in range(per_set)]
        if number:
            sums.append(pieces.pop())
        pieces = [pack(piece) for piece in pieces]
        if not number:
            *pieces, own_weight = lax.optimization_barrier((*pieces, own_weight))
        for place, piece in enumerate(pieces):
            d = number * per_set + place + 1
            received.append(unpack(exchange(piece, "col", cols, 2 * d)))
    whole = add(sums[0], *received)
    got = []
    for d in range(1, rows):
        got.append(send(cut(whole, d, local), "row", rows, d))
    summed, totals, _ = add(cut(whole, 0, local), *got)
    prior = mine.astype(jnp.float32)
    out = (summed + PRIOR_WEIGHT * prior) / (totals + PRIOR_WEIGHT)
    return unlay(out, parts)


def solution(mesh):
    return jax.shard_map(
        body,
        mesh=mesh,
        in_specs=(
            P(("row", "col"), None, None),
            P(("row", "col")),
            P(("row", "col"), None, None),
            P(),
            P(),
        ),
        out_specs=P(("row", "col"), None, None),
        check_vma=False,
    )
```

```python
import functools
import math

import jax
import jax.numpy as jnp
from jax import lax
from jax.experimental import pallas as pl
from jax.experimental.pallas import tpu as pltpu
from jax.sharding import PartitionSpec as P


GRID = 64
SHIFT_SIDE = 8
PRIOR_WEIGHT = 4.0
LANES = 128
PAIR = 2 * LANES
UNROLL = 8
WIRE = jnp.float16
VMEM_LIMIT = 8 << 20
RELAY_LIMIT = 14 << 20

PARAMS = pltpu.CompilerParams(vmem_limit_bytes=VMEM_LIMIT)


def whole_in_vmem(count):
    return [pl.BlockSpec(memory_space=pltpu.VMEM)] * count


def relay_kernel(in_ref, out_ref, taken_ref, wide_ref, peak_ref, sems):
    blocks, some, per, _ = taken_ref.shape
    rows = peak_ref.shape[0]
    count = blocks * some
    last = out_ref.shape[0]
    pitch = rows + 1

    def fetch(block):
        return pltpu.make_async_copy(
            in_ref.at[pl.ds(block * some, some)], taken_ref.at[block], sems.at[block]
        )

    for block in range(blocks):
        fetch(block).start()
    peak_ref[...] = jnp.zeros_like(peak_ref)

    def step(block, carry):
        fetch(block).wait()
        base = pl.multiple_of(block * some, some)
        peak = peak_ref[...]
        for n in range(0, some, 16):
            for r in range(0, per, rows):
                start = (n // 16 * (per // rows) + r // rows) * 16 * pitch
                for m in range(16):
                    wide = taken_ref[block, n + m, r : r + rows, :].astype(jnp.float32)
                    peak = jnp.maximum(peak, jnp.abs(wide))
                    at = start + m * pitch
                    wide_ref[at : at + rows, :] = wide
                for k in range(rows):
                    picked = wide_ref[pl.ds(start + k, 16, stride=pitch), :]
                    at = (r + k) * LANES
                    out_ref[pl.ds(base + n, 16), at : at + LANES] = picked.astype(jnp.bfloat16)
        peak_ref[...] = peak
        return carry

    lax.fori_loop(0, blocks, step, 0)
    peak = jnp.max(peak_ref[...], axis=0, keepdims=True)
    out_ref[count:last, :LANES] = jnp.broadcast_to(peak, (last - count, LANES)).astype(
        jnp.bfloat16
    )


def flat_rows(value, lead):
    count, parts, coeffs = value.shape
    groups = coeffs // LANES
    value = value.reshape(count, parts, groups, LANES)
    return value.transpose(0, 2, 1, 3).reshape(lead + (LANES,))


def relay(images, rows=8, spare=16):
    count, parts, coeffs = images.shape
    per = parts * (coeffs // LANES)
    some = min(count, 64)
    flat = pltpu.with_memory_space_constraint(flat_rows(images, (count, per)), pltpu.HBM)
    return pl.pallas_call(
        relay_kernel,
        in_specs=[pl.BlockSpec(memory_space=pltpu.HBM)],
        out_specs=pl.BlockSpec(memory_space=pltpu.VMEM),
        out_shape=jax.ShapeDtypeStruct((count + spare, per * LANES), jnp.bfloat16),
        scratch_shapes=[
            pltpu.VMEM((count // some, some, per, LANES), jnp.bfloat16),
            pltpu.VMEM((some * per // rows * (rows + 1), LANES), jnp.float32),
            pltpu.VMEM((rows, LANES), jnp.float32),
            pltpu.SemaphoreType.DMA((count // some,)),
        ],
        compiler_params=pltpu.CompilerParams(vmem_limit_bytes=RELAY_LIMIT),
        cost_estimate=pl.CostEstimate(
            flops=count * per * LANES,
            bytes_accessed=4 * count * per * LANES,
            transcendentals=0,
        ),
    )(flat)


def lay_kernel(in_ref, out_ref, wide_ref):
    local, width = out_ref.shape
    per = width // LANES
    wide_ref[...] = in_ref[...].astype(jnp.float32)
    for r in range(per):
        picked = wide_ref[pl.ds(r, local, stride=per), :]
        out_ref[:, r * LANES : (r + 1) * LANES] = picked.astype(out_ref.dtype)


def unlay_kernel(in_ref, out_ref):
    local, width = in_ref.shape
    per = width // LANES
    for r in range(per):
        out_ref[pl.ds(r, local, stride=per), :] = in_ref[:, r * LANES : (r + 1) * LANES]


def lay(templates):
    local, parts, coeffs = templates.shape
    width = parts * coeffs
    rows = local * width // LANES
    return pl.pallas_call(
        lay_kernel,
        in_specs=whole_in_vmem(1),
        out_specs=whole_in_vmem(1)[0],
        out_shape=jax.ShapeDtypeStruct((local, width), templates.dtype),
        scratch_shapes=[pltpu.VMEM((rows, LANES), jnp.float32)],
        compiler_params=PARAMS,
    )(flat_rows(templates, (rows,)))


def unlay(value, parts):
    local, width = value.shape
    groups = width // parts // LANES
    flat = pl.pallas_call(
        unlay_kernel,
        in_specs=whole_in_vmem(1),
        out_specs=whole_in_vmem(1)[0],
        out_shape=jax.ShapeDtypeStruct((local * width // LANES, LANES), value.dtype),
        compiler_params=PARAMS,
    )(value)
    flat = flat.reshape(local, groups, parts, LANES).transpose(0, 2, 1, 3)
    return flat.reshape(local, parts, width // parts)


def phase_kernel(local, quads, id_ref, shifts_ref, table_ref, *refs):
    outs, first_ref, chosen_ref = refs[:6], refs[6], refs[7]
    count, rows, _ = outs[0].shape
    number = table_ref.shape[0]
    shifts, templates = shifts_ref.shape
    held = templates // 2
    piece_rows = held // quads
    in_row = piece_rows // local

    position = lax.broadcasted_iota(jnp.int32, (templates, templates), 0)
    lane = lax.broadcasted_iota(jnp.int32, (templates, templates), 1)
    at_local = lax.rem(position, local)
    at_row = lax.rem(lax.div(position, local), in_row) ^ lax.axis_index("row")
    at_quad = lax.rem(lax.div(position, piece_rows) + 1, quads)
    at_col = (2 * at_quad + lax.div(position, held)) ^ lax.axis_index("col")
    slots = (at_row * (2 * quads) + at_col) * local + at_local
    names = jnp.where(slots == lane, id_ref[...].astype(jnp.float32), 0.0)
    names = jnp.sum(names, axis=1, keepdims=True)
    named = jnp.where(names == lane.astype(jnp.float32), 1.0, 0.0).astype(jnp.bfloat16)
    shift = lax.dot_general(
        named,
        shifts_ref[...].astype(jnp.float32).astype(jnp.bfloat16),
        (((1,), (1,)), ((), ())),
        preferred_element_type=jnp.float32,
    )

    rest, parts = table_ref[...], []
    for _ in range(3):
        part = rest.astype(jnp.bfloat16)
        parts.append(part)
        rest = rest - part.astype(jnp.float32)
    parts = jnp.concatenate(parts, axis=0)
    numbers = lax.broadcasted_iota(jnp.int32, (piece_rows, 3 * number), 1)
    numbers = lax.rem(numbers, number).astype(jnp.float32)
    for half in range(2):
        cos_ref, sin_ref, sign_ref = outs[3 * half : 3 * half + 3]
        for place in range(quads):
            at = half * held + place * piece_rows
            for j in range(shifts):
                hit = shift[at : at + piece_rows, j : j + 1] == numbers
                to = (place * shifts + j) * piece_rows
                chosen_ref[to : to + piece_rows, :] = jnp.where(hit, 1.0, 0.0).astype(
                    jnp.bfloat16
                )
        first_ref[...] = jnp.dot(
            chosen_ref[...], parts, preferred_element_type=jnp.float32
        )

        def step(i, carry, cos_ref=cos_ref, sin_ref=sin_ref, sign_ref=sign_ref):
            here = pl.ds(pl.multiple_of(i * 32, 32), 32)
            c, s = first_ref[here, :LANES], first_ref[here, LANES:PAIR]
            dc, ds = first_ref[here, PAIR : PAIR + LANES], first_ref[here, PAIR + LANES :]
            cos_ref[0, here, :] = c
            sin_ref[0, here, :] = s
            for k in range(1, count):
                c, s = c * dc - s * ds, s * dc + c * ds
                cos_ref[k, here, :] = c
                sin_ref[k, here, :] = s
            c, s = c * dc - s * ds, s * dc + c * ds
            same = c * first_ref[here, :LANES] + s * first_ref[here, LANES:PAIR]
            sign_ref[here, :] = jnp.where(same > 0.0, 1.0, -1.0)
            return carry

        lax.fori_loop(0, rows // 32, step, 0)


def phases_of(template_id, shift_table, table, count, local, quads):
    templates, shifts = shift_table.shape
    rows = templates // 2 * shifts
    held = jax.ShapeDtypeStruct((count, rows, LANES), jnp.float32)
    sign = jax.ShapeDtypeStruct((rows, LANES), jnp.float32)
    out = pl.pallas_call(
        functools.partial(phase_kernel, local, quads),
        in_specs=whole_in_vmem(3),
        out_specs=tuple(whole_in_vmem(6)),
        out_shape=(held, held, sign) * 2,
        scratch_shapes=[
            pltpu.VMEM((rows, table.shape[1]), jnp.float32),
            pltpu.VMEM((rows, 3 * table.shape[0]), jnp.bfloat16),
        ],
        compiler_params=PARAMS,
        cost_estimate=pl.CostEstimate(
            flops=12 * count * rows * LANES,
            bytes_accessed=16 * count * rows * LANES,
            transcendentals=0,
        ),
    )(template_id.reshape(1, templates), shift_table.T, table)
    return out[:3], out[3:]


def score_kernel(places, shifts, *refs):
    pieces = len(places)
    piece_refs = refs[:pieces]
    tables = (refs[pieces : pieces + 3], refs[pieces + 3 : pieces + 6])
    x_ref, out_ref, norm_ref, rot_a, rot_b = refs[pieces + 6 :]
    images = out_ref.shape[1]
    piece_rows = piece_refs[0].shape[0]
    span = shifts * piece_rows
    block = rot_a.shape[1]
    per = block // PAIR
    half = tables[0][0].shape[0] // per

    norm_ref[...] = jnp.zeros_like(norm_ref)
    out_ref[...] = jnp.zeros_like(out_ref)

    def rotate(index, rot_ref):
        live = index < 2 * half
        index = jnp.minimum(index, 2 * half - 1)
        base = pl.multiple_of(index * block, block)
        phase = lax.rem(index, half) * per
        for g in range(per):
            at = g * PAIR
            for i, (side, place) in enumerate(places):
                cos_ref, sin_ref, _ = tables[side]
                here = slice(i * piece_rows, (i + 1) * piece_rows)
                real = piece_refs[i][:, pl.ds(base + at, LANES)].astype(jnp.float32)
                imag = piece_refs[i][:, pl.ds(base + at + LANES, LANES)].astype(jnp.float32)
                power = real * real + imag * imag
                norm_ref[here, :] += jnp.where(live, power, 0.0)
                for j in range(shifts):
                    start = place * span + j * piece_rows
                    row = slice(start, start + piece_rows)
                    c, s = cos_ref[phase + g, row, :], sin_ref[phase + g, row, :]
                    start = i * span + j * piece_rows
                    row = slice(start, start + piece_rows)
                    rot_ref[row, at : at + LANES] = (real * c + imag * s).astype(jnp.bfloat16)
                    rot_ref[row, at + LANES : at + PAIR] = (imag * c - real * s).astype(
                        jnp.bfloat16
                    )

    def gather_scores(index, rot_ref):
        base = pl.multiple_of(index * block, block)
        out_ref[...] += lax.dot_general(
            rot_ref[...],
            x_ref[0:images, pl.ds(base, block)],
            (((1,), (1,)), ((), ())),
            preferred_element_type=jnp.float32,
        )

    def turn_sign():
        for n in range(images // LANES):
            lanes = slice(n * LANES, (n + 1) * LANES)
            for i, (side, place) in enumerate(places):
                sign = tables[side][2][place * span : (place + 1) * span, :]
                row = slice(i * span, (i + 1) * span)
                out_ref[row, lanes] = out_ref[row, lanes] * sign

    rotate(jnp.int32(0), rot_a)

    def step(i, carry):
        for at in range(0, UNROLL, 2):
            index = i * UNROLL + at
            gather_scores(index, rot_a)
            rotate(index + 1, rot_b)
            gather_scores(index + 1, rot_b)
            rotate(index + 2, rot_a)
        return carry

    lax.fori_loop(0, half // UNROLL, step, 0)
    turn_sign()
    lax.fori_loop(half // UNROLL, 2 * half // UNROLL, step, 0)
    turn_sign()


def scores_of(piece_list, places, tables, shifts, x, images, groups=2):
    pieces = len(piece_list)
    rows, width = piece_list[0].shape
    held = pieces * rows
    rotated = pltpu.VMEM((shifts * held, groups * PAIR), jnp.bfloat16)
    return pl.pallas_call(
        functools.partial(score_kernel, places, shifts),
        in_specs=whole_in_vmem(pieces + 7),
        out_specs=tuple(whole_in_vmem(2)),
        out_shape=(
            jax.ShapeDtypeStruct((shifts * held, images), jnp.float32),
            jax.ShapeDtypeStruct((held, LANES), jnp.float32),
        ),
        scratch_shapes=[rotated, rotated],
        compiler_params=PARAMS,
        cost_estimate=pl.CostEstimate(
            flops=2 * shifts * held * images * width,
            bytes_accessed=2 * images * width + 8 * shifts * held * images,
            transcendentals=0,
        ),
    )(*piece_list, *tables[0], *tables[1], x)


def weight_kernel(layout, shifts, piece_rows, *refs):
    blocks = len(layout)
    score_refs, norm_refs = refs[:blocks], refs[blocks : 2 * blocks]
    prec_ref, x_ref = refs[2 * blocks : 2 * blocks + 2]
    outs, raised_refs = refs[2 * blocks + 2 : 2 * blocks + 8], refs[2 * blocks + 8 :]
    images = prec_ref.shape[1]
    span = shifts * piece_rows
    peak = jnp.max(x_ref[images:, :LANES].astype(jnp.float32)) * math.sqrt(2.0)
    prec = prec_ref[...][None]

    def cube(value):
        return value.reshape(-1, piece_rows, value.shape[-1])

    top = None
    for places, score_ref, norm_ref, raised_ref in zip(
        layout, score_refs, norm_refs, raised_refs
    ):
        norm = 0.5 * jnp.sum(norm_ref[...], axis=1, keepdims=True)
        for i in range(len(places)):
            row = slice(i * span, (i + 1) * span)
            bias = norm[i * piece_rows : (i + 1) * piece_rows][None]
            value = prec * (cube(score_ref[row, :]) - bias)
            raised_ref[row, :] = value.reshape(span, images)
            best = jnp.max(jnp.max(value, axis=0), axis=0, keepdims=True)
            top = best if top is None else jnp.maximum(top, best)
    norm = None
    for places, raised_ref in zip(layout, raised_refs):
        for i in range(len(places)):
            row = slice(i * span, (i + 1) * span)
            raised = jnp.exp(raised_ref[row, :] - top)
            raised_ref[row, :] = raised
            part = jnp.sum(jnp.sum(cube(raised), axis=0), axis=0, keepdims=True)
            norm = part if norm is None else norm + part
    inverse = 1.0 / norm
    for places, raised_ref in zip(layout, raised_refs):
        for i, (side, place) in enumerate(places):
            weight = (raised_ref[i * span : (i + 1) * span, :] * inverse).astype(jnp.bfloat16)
            outs[side][place * span : (place + 1) * span, :] = weight
            total = jnp.sum(cube(weight.astype(jnp.float32)), axis=0)
            total = jnp.sum(total, axis=1, keepdims=True)
            total = jnp.broadcast_to(total, (piece_rows, LANES))
            here = slice(place * piece_rows, (place + 1) * piece_rows)
            outs[2 + side][here, :] = total
            outs[4 + side][here, :] = total * peak


def weights_of(scores, layout, precision, x, shifts, held, piece_rows):
    images = precision.shape[0]
    weight = jax.ShapeDtypeStruct((shifts * held, images), jnp.bfloat16)
    total = jax.ShapeDtypeStruct((held, LANES), jnp.float32)
    rows = 2 * shifts * held
    own_w, other_w, own_t, other_t, own_b, other_b = pl.pallas_call(
        functools.partial(weight_kernel, layout, shifts, piece_rows),
        in_specs=whole_in_vmem(2 * len(layout) + 2),
        out_specs=tuple(whole_in_vmem(6)),
        out_shape=(weight, weight, total, total, total, total),
        scratch_shapes=[pltpu.VMEM(value.shape, jnp.float32) for value, _ in scores],
        compiler_params=PARAMS,
        cost_estimate=pl.CostEstimate(
            flops=20 * rows * images,
            bytes_accessed=12 * rows * images,
            transcendentals=2 * rows * images,
        ),
    )(
        *[value for value, _ in scores],
        *[value for _, value in scores],
        precision.reshape(1, images),
        x,
    )
    return (own_w, own_t[:, :1], own_b[:, :1]), (other_w, other_t[:, :1], other_b[:, :1])


def back_kernel(first, pieces, shifts, w_ref, cos_ref, sin_ref, sign_ref, x_ref, *refs):
    out_ref, turned_ref, mix_a, mix_b = refs
    rows, images = turned_ref.shape
    span = rows // pieces
    piece_rows = span // shifts
    count = cos_ref.shape[0]
    first = first * span
    used = slice(first, first + rows)
    for n in range(images // LANES):
        lanes = slice(n * LANES, (n + 1) * LANES)
        wide = w_ref[used, lanes].astype(jnp.float32) * sign_ref[used, :]
        turned_ref[:, lanes] = wide.astype(jnp.bfloat16)

    def mix(index, mix_ref):
        index = jnp.minimum(index, count - 1)
        for second in range(2):
            weight = turned_ref[...] if second else w_ref[used, :]
            base = pl.multiple_of((second * count + index) * PAIR, PAIR)
            mix_ref[:, second * PAIR : (second + 1) * PAIR] = jnp.dot(
                weight, x_ref[0:images, pl.ds(base, PAIR)], preferred_element_type=jnp.float32
            )

    def turn(index, mix_ref):
        for i in range(pieces):
            for t in range(0, piece_rows, 8):
                total = [None] * 4
                for j in range(shifts):
                    start = i * span + j * piece_rows + t
                    row = slice(start, start + 8)
                    at_row = slice(first + start, first + start + 8)
                    c, s = cos_ref[index, at_row, :], sin_ref[index, at_row, :]
                    terms = []
                    for second in range(2):
                        at = second * PAIR
                        real = mix_ref[row, at : at + LANES]
                        imag = mix_ref[row, at + LANES : at + PAIR]
                        terms += [real * c - imag * s, imag * c + real * s]
                    total = [b if a is None else a + b for a, b in zip(total, terms)]
                here = slice(i * piece_rows + t, i * piece_rows + t + 8)
                for part in range(4):
                    base = (part // 2 * count + index) * PAIR + part % 2 * LANES
                    out_ref[here, pl.ds(pl.multiple_of(base, LANES), LANES)] = total[part]

    mix(jnp.int32(0), mix_a)

    def step(i, carry):
        for at in range(0, UNROLL, 2):
            index = i * UNROLL + at
            mix(index + 1, mix_b)
            turn(index, mix_a)
            mix(index + 2, mix_a)
            turn(index + 1, mix_b)
        return carry

    lax.fori_loop(0, count // UNROLL, step, 0)


def back_of(weight, x, phases, shifts, first, pieces, piece_rows):
    images = weight.shape[1]
    rows = pieces * shifts * piece_rows
    width = x.shape[1]
    mixed = pltpu.VMEM((rows, 2 * PAIR), jnp.float32)
    return pl.pallas_call(
        functools.partial(back_kernel, first, pieces, shifts),
        in_specs=whole_in_vmem(5),
        out_specs=whole_in_vmem(1)[0],
        out_shape=jax.ShapeDtypeStruct((pieces * piece_rows, width), jnp.float32),
        scratch_shapes=[pltpu.VMEM((rows, images), jnp.bfloat16), mixed, mixed],
        compiler_params=PARAMS,
        cost_estimate=pl.CostEstimate(
            flops=2 * rows * images * width,
            bytes_accessed=2 * images * width + 2 * rows * images + 4 * pieces * width,
            transcendentals=0,
        ),
    )(weight, *phases, x)


def exchange(value, axis, size, bit):
    return lax.ppermute(value, axis, [(i, i ^ bit) for i in range(size)])


def body(images, precision, templates, template_id, shift_table):
    image_count, parts, coeffs = images.shape
    local = templates.shape[0]
    shifts = shift_table.shape[1]
    rows, cols = lax.axis_size("row"), lax.axis_size("col")
    quads = cols // 2
    groups = coeffs // LANES
    width = parts * coeffs
    held = local * rows * quads

    mine = lay(templates)
    row_set = [mine]
    row_set += [exchange(mine, "row", rows, d) for d in range(1, rows)]
    own_set = [jnp.concatenate(row_set, axis=0)]
    for d in range(1, quads):
        low, high = d & -d, 1 << (d.bit_length() - 1)
        if low == high:
            own_set.append(exchange(own_set[0], "col", cols, 2 * d))
            continue
        first = exchange(own_set[d ^ low][:, : width // 2], "col", cols, 2 * low)
        second = exchange(own_set[d ^ high][:, width // 2 :], "col", cols, 2 * high)
        own_set.append(jnp.concatenate([first, second], axis=1))
    other_set = []
    for d in range(quads):
        other_set.append(exchange(own_set[d], "col", cols, 1))

    x = relay(images)

    piece_rows = local * rows

    number = jnp.arange(SHIFT_SIDE * SHIFT_SIDE, dtype=jnp.int32)[:, None]
    step_x = number // SHIFT_SIDE - SHIFT_SIDE // 2
    step_y = number % SHIFT_SIDE - SHIFT_SIDE // 2
    lane = jnp.arange(LANES, dtype=jnp.int32)[None, :]
    freq_x = lane // GRID - GRID // 2
    freq_y = lane % GRID - GRID // 2
    first = (step_x * freq_x + step_y * freq_y) % GRID
    stride = jnp.broadcast_to(step_x * (LANES // GRID) % GRID, first.shape)
    angle = jnp.concatenate([first, stride], axis=1).astype(jnp.float32)
    angle = angle * (2.0 * math.pi / GRID)
    table = [jnp.cos(angle), jnp.sin(angle)]
    table = [part[:, at : at + LANES] for at in (0, LANES) for part in table]
    table = jnp.concatenate(table, axis=1)
    tables = phases_of(template_id, shift_table, table, groups // 2, local, quads)

    layout = [
        tuple((0, (d - 1) % quads) for d in range(quads - 1)),
        tuple((1, (d - 1) % quads) for d in range(quads - 1)),
        ((0, quads - 2), (1, quads - 2)),
    ]
    piece_lists = [own_set[:-1], other_set[:-1], [own_set[-1], other_set[-1]]]
    scores = []
    for number, (piece_list, places) in enumerate(zip(piece_lists, layout)):
        scores.append(scores_of(piece_list, places, tables, shifts, x, image_count))
    own, other = weights_of(scores, layout, precision, x, shifts, held, piece_rows)

    def pack(held_rows):
        value, total, bound = held_rows
        power = jnp.ceil(jnp.log2(jnp.maximum(bound, 1e-30))) - 15.0
        at = jnp.arange(LANES, dtype=jnp.int32)[None, :]
        extra = jnp.where(at == 0, total, jnp.where(at == 1, power, 0.0))
        return jnp.concatenate([value * jnp.exp2(-power), extra], axis=1).astype(WIRE)

    def unpack(payload):
        got = payload.astype(jnp.float32)
        total, power = got[:, width : width + 1], got[:, width + 1 : width + 2]
        return got[:, :width] * jnp.exp2(power), total, jnp.exp2(power + 15.0)

    def send(held_rows, axis, size, bit):
        return unpack(exchange(pack(held_rows), axis, size, bit))

    def add(first, *others):
        for other in others:
            first = tuple(a + b for a, b in zip(first, other))
        return first

    def cut(held_rows, at, count):
        return tuple(value[at * count : (at + 1) * count] for value in held_rows)

    other_back = back_of(other[0], x, tables[1], shifts, 0, quads, piece_rows)
    got = send((other_back,) + other[1:], "col", cols, 1)
    per_set = quads // 2
    set_rows = per_set * piece_rows
    own_weight = own[0]
    sums, received = [], []
    for number in range(2):
        back = back_of(
            own_weight, x, tables[0], shifts, number * per_set, per_set, piece_rows
        )
        whole = add((back,) + cut(own[1:], number, set_rows), cut(got, number, set_rows))
        pieces = [cut(whole, place, piece_rows) for place in range(per_set)]
        if number:
            sums.append(pieces.pop())
        pieces = [pack(piece) for piece in pieces]
        if not number:
            *pieces, own_weight = lax.optimization_barrier((*pieces, own_weight))
        for place, piece in enumerate(pieces):
            d = number * per_set + place + 1
            received.append(unpack(exchange(piece, "col", cols, 2 * d)))
    whole = add(sums[0], *received)
    got = []
    for d in range(1, rows):
        got.append(send(cut(whole, d, local), "row", rows, d))
    summed, totals, _ = add(cut(whole, 0, local), *got)
    prior = mine.astype(jnp.float32)
    out = (summed + PRIOR_WEIGHT * prior) / (totals + PRIOR_WEIGHT)
    return unlay(out, parts)


def solution(mesh):
    return jax.shard_map(
        body,
        mesh=mesh,
        in_specs=(
            P(("row", "col"), None, None),
            P(("row", "col")),
            P(("row", "col"), None, None),
            P(),
            P(),
        ),
        out_specs=P(("row", "col"), None, None),
        check_vma=False,
    )
```

```python
import functools
import math

import jax
import jax.numpy as jnp
from jax import lax
from jax.experimental import pallas as pl
from jax.experimental.pallas import tpu as pltpu
from jax.sharding import PartitionSpec as P


GRID = 64
SHIFT_SIDE = 8
PRIOR_WEIGHT = 4.0
LANES = 128
PAIR = 2 * LANES
UNROLL = 8
BACK_UNROLL = 16
WIRE = jnp.float16
VMEM_LIMIT = 8 << 20
RELAY_LIMIT = 14 << 20

PARAMS = pltpu.CompilerParams(vmem_limit_bytes=VMEM_LIMIT)


def whole_in_vmem(count):
    return [pl.BlockSpec(memory_space=pltpu.VMEM)] * count


def relay_kernel(in_ref, out_ref, taken_ref, wide_ref, peak_ref, sems):
    blocks, some, per, _ = taken_ref.shape
    rows = peak_ref.shape[0]
    count = blocks * some
    last = out_ref.shape[0]
    pitch = rows + 1

    def fetch(block):
        return pltpu.make_async_copy(
            in_ref.at[pl.ds(block * some, some)], taken_ref.at[block], sems.at[block]
        )

    for block in range(blocks):
        fetch(block).start()
    peak_ref[...] = jnp.zeros_like(peak_ref)

    def step(block, carry):
        fetch(block).wait()
        base = pl.multiple_of(block * some, some)
        peak = peak_ref[...]
        for n in range(0, some, 16):
            for r in range(0, per, rows):
                start = (n // 16 * (per // rows) + r // rows) * 16 * pitch
                for m in range(16):
                    wide = taken_ref[block, n + m, r : r + rows, :].astype(jnp.float32)
                    peak = jnp.maximum(peak, jnp.abs(wide))
                    at = start + m * pitch
                    wide_ref[at : at + rows, :] = wide
                for k in range(rows):
                    picked = wide_ref[pl.ds(start + k, 16, stride=pitch), :]
                    at = (r + k) * LANES
                    out_ref[pl.ds(base + n, 16), at : at + LANES] = picked.astype(jnp.bfloat16)
        peak_ref[...] = peak
        return carry

    lax.fori_loop(0, blocks, step, 0)
    peak = jnp.max(peak_ref[...], axis=0, keepdims=True)
    out_ref[count:last, :LANES] = jnp.broadcast_to(peak, (last - count, LANES)).astype(
        jnp.bfloat16
    )


def flat_rows(value, lead):
    count, parts, coeffs = value.shape
    groups = coeffs // LANES
    value = value.reshape(count, parts, groups, LANES)
    return value.transpose(0, 2, 1, 3).reshape(lead + (LANES,))


def relay(images, rows=8, spare=16):
    count, parts, coeffs = images.shape
    per = parts * (coeffs // LANES)
    some = min(count, 64)
    flat = pltpu.with_memory_space_constraint(flat_rows(images, (count, per)), pltpu.HBM)
    return pl.pallas_call(
        relay_kernel,
        in_specs=[pl.BlockSpec(memory_space=pltpu.HBM)],
        out_specs=pl.BlockSpec(memory_space=pltpu.VMEM),
        out_shape=jax.ShapeDtypeStruct((count + spare, per * LANES), jnp.bfloat16),
        scratch_shapes=[
            pltpu.VMEM((count // some, some, per, LANES), jnp.bfloat16),
            pltpu.VMEM((some * per // rows * (rows + 1), LANES), jnp.float32),
            pltpu.VMEM((rows, LANES), jnp.float32),
            pltpu.SemaphoreType.DMA((count // some,)),
        ],
        compiler_params=pltpu.CompilerParams(vmem_limit_bytes=RELAY_LIMIT),
        cost_estimate=pl.CostEstimate(
            flops=count * per * LANES,
            bytes_accessed=4 * count * per * LANES,
            transcendentals=0,
        ),
    )(flat)


def lay_kernel(in_ref, out_ref, wide_ref):
    local, width = out_ref.shape
    per = width // LANES
    wide_ref[...] = in_ref[...].astype(jnp.float32)
    for r in range(per):
        picked = wide_ref[pl.ds(r, local, stride=per), :]
        out_ref[:, r * LANES : (r + 1) * LANES] = picked.astype(out_ref.dtype)


def unlay_kernel(in_ref, out_ref):
    local, width = in_ref.shape
    per = width // LANES
    for r in range(per):
        out_ref[pl.ds(r, local, stride=per), :] = in_ref[:, r * LANES : (r + 1) * LANES]


def lay(templates):
    local, parts, coeffs = templates.shape
    width = parts * coeffs
    rows = local * width // LANES
    return pl.pallas_call(
        lay_kernel,
        in_specs=whole_in_vmem(1),
        out_specs=whole_in_vmem(1)[0],
        out_shape=jax.ShapeDtypeStruct((local, width), templates.dtype),
        scratch_shapes=[pltpu.VMEM((rows, LANES), jnp.float32)],
        compiler_params=PARAMS,
    )(flat_rows(templates, (rows,)))


def unlay(value, parts):
    local, width = value.shape
    groups = width // parts // LANES
    flat = pl.pallas_call(
        unlay_kernel,
        in_specs=whole_in_vmem(1),
        out_specs=whole_in_vmem(1)[0],
        out_shape=jax.ShapeDtypeStruct((local * width // LANES, LANES), value.dtype),
        compiler_params=PARAMS,
    )(value)
    flat = flat.reshape(local, groups, parts, LANES).transpose(0, 2, 1, 3)
    return flat.reshape(local, parts, width // parts)


def phase_kernel(local, quads, id_ref, shifts_ref, table_ref, *refs):
    outs, first_ref, chosen_ref = refs[:6], refs[6], refs[7]
    count, rows, _ = outs[0].shape
    number = table_ref.shape[0]
    shifts, templates = shifts_ref.shape
    held = templates // 2
    piece_rows = held // quads
    in_row = piece_rows // local

    position = lax.broadcasted_iota(jnp.int32, (templates, templates), 0)
    lane = lax.broadcasted_iota(jnp.int32, (templates, templates), 1)
    at_local = lax.rem(position, local)
    at_row = lax.rem(lax.div(position, local), in_row) ^ lax.axis_index("row")
    at_quad = lax.rem(lax.div(position, piece_rows) + 1, quads)
    at_col = (2 * at_quad + lax.div(position, held)) ^ lax.axis_index("col")
    slots = (at_row * (2 * quads) + at_col) * local + at_local
    names = jnp.where(slots == lane, id_ref[...].astype(jnp.float32), 0.0)
    names = jnp.sum(names, axis=1, keepdims=True)
    named = jnp.where(names == lane.astype(jnp.float32), 1.0, 0.0).astype(jnp.bfloat16)
    shift = lax.dot_general(
        named,
        shifts_ref[...].astype(jnp.float32).astype(jnp.bfloat16),
        (((1,), (1,)), ((), ())),
        preferred_element_type=jnp.float32,
    )

    rest, parts = table_ref[...], []
    for _ in range(3):
        part = rest.astype(jnp.bfloat16)
        parts.append(part)
        rest = rest - part.astype(jnp.float32)
    parts = jnp.concatenate(parts, axis=0)
    numbers = lax.broadcasted_iota(jnp.int32, (piece_rows, 3 * number), 1)
    numbers = lax.rem(numbers, number).astype(jnp.float32)
    for half in range(2):
        cos_ref, sin_ref, sign_ref = outs[3 * half : 3 * half + 3]
        for place in range(quads):
            at = half * held + place * piece_rows
            for j in range(shifts):
                hit = shift[at : at + piece_rows, j : j + 1] == numbers
                to = (place * shifts + j) * piece_rows
                chosen_ref[to : to + piece_rows, :] = jnp.where(hit, 1.0, 0.0).astype(
                    jnp.bfloat16
                )
        first_ref[...] = jnp.dot(
            chosen_ref[...], parts, preferred_element_type=jnp.float32
        )

        def step(i, carry, cos_ref=cos_ref, sin_ref=sin_ref, sign_ref=sign_ref):
            here = pl.ds(pl.multiple_of(i * 32, 32), 32)
            c, s = first_ref[here, :LANES], first_ref[here, LANES:PAIR]
            dc, ds = first_ref[here, PAIR : PAIR + LANES], first_ref[here, PAIR + LANES :]
            cos_ref[0, here, :] = c
            sin_ref[0, here, :] = s
            for k in range(1, count):
                c, s = c * dc - s * ds, s * dc + c * ds
                cos_ref[k, here, :] = c
                sin_ref[k, here, :] = s
            c, s = c * dc - s * ds, s * dc + c * ds
            same = c * first_ref[here, :LANES] + s * first_ref[here, LANES:PAIR]
            sign_ref[here, :] = jnp.where(same > 0.0, 1.0, -1.0)
            return carry

        lax.fori_loop(0, rows // 32, step, 0)


def phases_of(template_id, shift_table, table, count, local, quads):
    templates, shifts = shift_table.shape
    rows = templates // 2 * shifts
    held = jax.ShapeDtypeStruct((count, rows, LANES), jnp.float32)
    sign = jax.ShapeDtypeStruct((rows, LANES), jnp.float32)
    out = pl.pallas_call(
        functools.partial(phase_kernel, local, quads),
        in_specs=whole_in_vmem(3),
        out_specs=tuple(whole_in_vmem(6)),
        out_shape=(held, held, sign) * 2,
        scratch_shapes=[
            pltpu.VMEM((rows, table.shape[1]), jnp.float32),
            pltpu.VMEM((rows, 3 * table.shape[0]), jnp.bfloat16),
        ],
        compiler_params=PARAMS,
        cost_estimate=pl.CostEstimate(
            flops=12 * count * rows * LANES,
            bytes_accessed=16 * count * rows * LANES,
            transcendentals=0,
        ),
    )(template_id.reshape(1, templates), shift_table.T, table)
    return out[:3], out[3:]


def score_kernel(places, shifts, *refs):
    pieces = len(places)
    piece_refs = refs[:pieces]
    tables = (refs[pieces : pieces + 3], refs[pieces + 3 : pieces + 6])
    x_ref, out_ref, norm_ref, rot_a, rot_b = refs[pieces + 6 :]
    images = out_ref.shape[1]
    piece_rows = piece_refs[0].shape[0]
    span = shifts * piece_rows
    block = rot_a.shape[1]
    per = block // PAIR
    half = tables[0][0].shape[0] // per

    norm_ref[...] = jnp.zeros_like(norm_ref)
    out_ref[...] = jnp.zeros_like(out_ref)

    def rotate(index, rot_ref):
        live = index < 2 * half
        index = jnp.minimum(index, 2 * half - 1)
        base = pl.multiple_of(index * block, block)
        phase = lax.rem(index, half) * per
        for g in range(per):
            at = g * PAIR
            for i, (side, place) in enumerate(places):
                cos_ref, sin_ref, _ = tables[side]
                here = slice(i * piece_rows, (i + 1) * piece_rows)
                real = piece_refs[i][:, pl.ds(base + at, LANES)].astype(jnp.float32)
                imag = piece_refs[i][:, pl.ds(base + at + LANES, LANES)].astype(jnp.float32)
                power = real * real + imag * imag
                norm_ref[here, :] += jnp.where(live, power, 0.0)
                for j in range(shifts):
                    start = place * span + j * piece_rows
                    row = slice(start, start + piece_rows)
                    c, s = cos_ref[phase + g, row, :], sin_ref[phase + g, row, :]
                    start = i * span + j * piece_rows
                    row = slice(start, start + piece_rows)
                    rot_ref[row, at : at + LANES] = (real * c + imag * s).astype(jnp.bfloat16)
                    rot_ref[row, at + LANES : at + PAIR] = (imag * c - real * s).astype(
                        jnp.bfloat16
                    )

    def gather_scores(index, rot_ref):
        base = pl.multiple_of(index * block, block)
        out_ref[...] += lax.dot_general(
            rot_ref[...],
            x_ref[0:images, pl.ds(base, block)],
            (((1,), (1,)), ((), ())),
            preferred_element_type=jnp.float32,
        )

    def turn_sign():
        for n in range(images // LANES):
            lanes = slice(n * LANES, (n + 1) * LANES)
            for i, (side, place) in enumerate(places):
                sign = tables[side][2][place * span : (place + 1) * span, :]
                row = slice(i * span, (i + 1) * span)
                out_ref[row, lanes] = out_ref[row, lanes] * sign

    rotate(jnp.int32(0), rot_a)

    def step(i, carry):
        for at in range(0, UNROLL, 2):
            index = i * UNROLL + at
            gather_scores(index, rot_a)
            rotate(index + 1, rot_b)
            gather_scores(index + 1, rot_b)
            rotate(index + 2, rot_a)
        return carry

    lax.fori_loop(0, half // UNROLL, step, 0)
    turn_sign()
    lax.fori_loop(half // UNROLL, 2 * half // UNROLL, step, 0)
    turn_sign()


def scores_of(piece_list, places, tables, shifts, x, images, groups=2):
    pieces = len(piece_list)
    rows, width = piece_list[0].shape
    held = pieces * rows
    rotated = pltpu.VMEM((shifts * held, groups * PAIR), jnp.bfloat16)
    return pl.pallas_call(
        functools.partial(score_kernel, places, shifts),
        in_specs=whole_in_vmem(pieces + 7),
        out_specs=tuple(whole_in_vmem(2)),
        out_shape=(
            jax.ShapeDtypeStruct((shifts * held, images), jnp.float32),
            jax.ShapeDtypeStruct((held, LANES), jnp.float32),
        ),
        scratch_shapes=[rotated, rotated],
        compiler_params=PARAMS,
        cost_estimate=pl.CostEstimate(
            flops=2 * shifts * held * images * width,
            bytes_accessed=2 * images * width + 8 * shifts * held * images,
            transcendentals=0,
        ),
    )(*piece_list, *tables[0], *tables[1], x)


def weight_kernel(layout, shifts, piece_rows, *refs):
    blocks = len(layout)
    score_refs, norm_refs = refs[:blocks], refs[blocks : 2 * blocks]
    prec_ref, x_ref = refs[2 * blocks : 2 * blocks + 2]
    outs, raised_refs = refs[2 * blocks + 2 : 2 * blocks + 8], refs[2 * blocks + 8 :]
    images = prec_ref.shape[1]
    span = shifts * piece_rows
    peak = jnp.max(x_ref[images:, :LANES].astype(jnp.float32)) * math.sqrt(2.0)
    prec = prec_ref[...][None]

    def cube(value):
        return value.reshape(-1, piece_rows, value.shape[-1])

    top = None
    for places, score_ref, norm_ref, raised_ref in zip(
        layout, score_refs, norm_refs, raised_refs
    ):
        norm = 0.5 * jnp.sum(norm_ref[...], axis=1, keepdims=True)
        for i in range(len(places)):
            row = slice(i * span, (i + 1) * span)
            bias = norm[i * piece_rows : (i + 1) * piece_rows][None]
            value = prec * (cube(score_ref[row, :]) - bias)
            raised_ref[row, :] = value.reshape(span, images)
            best = jnp.max(jnp.max(value, axis=0), axis=0, keepdims=True)
            top = best if top is None else jnp.maximum(top, best)
    norm = None
    for places, raised_ref in zip(layout, raised_refs):
        for i in range(len(places)):
            row = slice(i * span, (i + 1) * span)
            raised = jnp.exp(raised_ref[row, :] - top)
            raised_ref[row, :] = raised
            part = jnp.sum(jnp.sum(cube(raised), axis=0), axis=0, keepdims=True)
            norm = part if norm is None else norm + part
    inverse = 1.0 / norm
    for places, raised_ref in zip(layout, raised_refs):
        for i, (side, place) in enumerate(places):
            weight = (raised_ref[i * span : (i + 1) * span, :] * inverse).astype(jnp.bfloat16)
            outs[side][place * span : (place + 1) * span, :] = weight
            total = jnp.sum(cube(weight.astype(jnp.float32)), axis=0)
            total = jnp.sum(total, axis=1, keepdims=True)
            total = jnp.broadcast_to(total, (piece_rows, LANES))
            here = slice(place * piece_rows, (place + 1) * piece_rows)
            outs[2 + side][here, :] = total
            outs[4 + side][here, :] = total * peak


def weights_of(scores, layout, precision, x, shifts, held, piece_rows):
    images = precision.shape[0]
    weight = jax.ShapeDtypeStruct((shifts * held, images), jnp.bfloat16)
    total = jax.ShapeDtypeStruct((held, LANES), jnp.float32)
    rows = 2 * shifts * held
    own_w, other_w, own_t, other_t, own_b, other_b = pl.pallas_call(
        functools.partial(weight_kernel, layout, shifts, piece_rows),
        in_specs=whole_in_vmem(2 * len(layout) + 2),
        out_specs=tuple(whole_in_vmem(6)),
        out_shape=(weight, weight, total, total, total, total),
        scratch_shapes=[pltpu.VMEM(value.shape, jnp.float32) for value, _ in scores],
        compiler_params=PARAMS,
        cost_estimate=pl.CostEstimate(
            flops=20 * rows * images,
            bytes_accessed=12 * rows * images,
            transcendentals=2 * rows * images,
        ),
    )(
        *[value for value, _ in scores],
        *[value for _, value in scores],
        precision.reshape(1, images),
        x,
    )
    return (own_w, own_t[:, :1], own_b[:, :1]), (other_w, other_t[:, :1], other_b[:, :1])


def back_kernel(first, pieces, shifts, w_ref, cos_ref, sin_ref, sign_ref, x_ref, *refs):
    out_ref, turned_ref, mix_a, mix_b = refs
    rows, images = turned_ref.shape
    span = rows // pieces
    piece_rows = span // shifts
    count = cos_ref.shape[0]
    first = first * span
    used = slice(first, first + rows)
    for n in range(images // LANES):
        lanes = slice(n * LANES, (n + 1) * LANES)
        wide = w_ref[used, lanes].astype(jnp.float32) * sign_ref[used, :]
        turned_ref[:, lanes] = wide.astype(jnp.bfloat16)

    def mix(index, mix_ref):
        index = jnp.minimum(index, count - 1)
        for second in range(2):
            weight = turned_ref[...] if second else w_ref[used, :]
            base = pl.multiple_of((second * count + index) * PAIR, PAIR)
            mix_ref[:, second * PAIR : (second + 1) * PAIR] = jnp.dot(
                weight, x_ref[0:images, pl.ds(base, PAIR)], preferred_element_type=jnp.float32
            )

    def turn(index, mix_ref):
        for i in range(pieces):
            for t in range(0, piece_rows, 8):
                total = [None] * 4
                for j in range(shifts):
                    start = i * span + j * piece_rows + t
                    row = slice(start, start + 8)
                    at_row = slice(first + start, first + start + 8)
                    c, s = cos_ref[index, at_row, :], sin_ref[index, at_row, :]
                    terms = []
                    for second in range(2):
                        at = second * PAIR
                        real = mix_ref[row, at : at + LANES]
                        imag = mix_ref[row, at + LANES : at + PAIR]
                        terms += [real * c - imag * s, imag * c + real * s]
                    total = [b if a is None else a + b for a, b in zip(total, terms)]
                here = slice(i * piece_rows + t, i * piece_rows + t + 8)
                for part in range(4):
                    base = (part // 2 * count + index) * PAIR + part % 2 * LANES
                    out_ref[here, pl.ds(pl.multiple_of(base, LANES), LANES)] = total[part]

    mix(jnp.int32(0), mix_a)

    def step(i, carry):
        for at in range(0, BACK_UNROLL, 2):
            index = i * BACK_UNROLL + at
            mix(index + 1, mix_b)
            turn(index, mix_a)
            mix(index + 2, mix_a)
            turn(index + 1, mix_b)
        return carry

    lax.fori_loop(0, count // BACK_UNROLL, step, 0)


def back_of(weight, x, phases, shifts, first, pieces, piece_rows):
    images = weight.shape[1]
    rows = pieces * shifts * piece_rows
    width = x.shape[1]
    mixed = pltpu.VMEM((rows, 2 * PAIR), jnp.float32)
    return pl.pallas_call(
        functools.partial(back_kernel, first, pieces, shifts),
        in_specs=whole_in_vmem(5),
        out_specs=whole_in_vmem(1)[0],
        out_shape=jax.ShapeDtypeStruct((pieces * piece_rows, width), jnp.float32),
        scratch_shapes=[pltpu.VMEM((rows, images), jnp.bfloat16), mixed, mixed],
        compiler_params=PARAMS,
        cost_estimate=pl.CostEstimate(
            flops=2 * rows * images * width,
            bytes_accessed=2 * images * width + 2 * rows * images + 4 * pieces * width,
            transcendentals=0,
        ),
    )(weight, *phases, x)


def exchange(value, axis, size, bit):
    return lax.ppermute(value, axis, [(i, i ^ bit) for i in range(size)])


def body(images, precision, templates, template_id, shift_table):
    image_count, parts, coeffs = images.shape
    local = templates.shape[0]
    shifts = shift_table.shape[1]
    rows, cols = lax.axis_size("row"), lax.axis_size("col")
    quads = cols // 2
    groups = coeffs // LANES
    width = parts * coeffs
    held = local * rows * quads

    mine = lay(templates)
    row_set = [mine]
    row_set += [exchange(mine, "row", rows, d) for d in range(1, rows)]
    own_set = [jnp.concatenate(row_set, axis=0)]
    for d in range(1, quads):
        low, high = d & -d, 1 << (d.bit_length() - 1)
        if low == high:
            own_set.append(exchange(own_set[0], "col", cols, 2 * d))
            continue
        first = exchange(own_set[d ^ low][:, : width // 2], "col", cols, 2 * low)
        second = exchange(own_set[d ^ high][:, width // 2 :], "col", cols, 2 * high)
        own_set.append(jnp.concatenate([first, second], axis=1))
    other_set = []
    for d in range(quads):
        other_set.append(exchange(own_set[d], "col", cols, 1))

    x = relay(images)

    piece_rows = local * rows

    number = jnp.arange(SHIFT_SIDE * SHIFT_SIDE, dtype=jnp.int32)[:, None]
    step_x = number // SHIFT_SIDE - SHIFT_SIDE // 2
    step_y = number % SHIFT_SIDE - SHIFT_SIDE // 2
    lane = jnp.arange(LANES, dtype=jnp.int32)[None, :]
    freq_x = lane // GRID - GRID // 2
    freq_y = lane % GRID - GRID // 2
    first = (step_x * freq_x + step_y * freq_y) % GRID
    stride = jnp.broadcast_to(step_x * (LANES // GRID) % GRID, first.shape)
    angle = jnp.concatenate([first, stride], axis=1).astype(jnp.float32)
    angle = angle * (2.0 * math.pi / GRID)
    table = [jnp.cos(angle), jnp.sin(angle)]
    table = [part[:, at : at + LANES] for at in (0, LANES) for part in table]
    table = jnp.concatenate(table, axis=1)
    tables = phases_of(template_id, shift_table, table, groups // 2, local, quads)

    layout = [
        tuple((0, (d - 1) % quads) for d in range(quads - 1)),
        tuple((1, (d - 1) % quads) for d in range(quads - 1)),
        ((0, quads - 2), (1, quads - 2)),
    ]
    piece_lists = [own_set[:-1], other_set[:-1], [own_set[-1], other_set[-1]]]
    scores = []
    for number, (piece_list, places) in enumerate(zip(piece_lists, layout)):
        scores.append(scores_of(piece_list, places, tables, shifts, x, image_count))
    own, other = weights_of(scores, layout, precision, x, shifts, held, piece_rows)

    def pack(held_rows):
        value, total, bound = held_rows
        power = jnp.ceil(jnp.log2(jnp.maximum(bound, 1e-30))) - 15.0
        at = jnp.arange(LANES, dtype=jnp.int32)[None, :]
        extra = jnp.where(at == 0, total, jnp.where(at == 1, power, 0.0))
        return jnp.concatenate([value * jnp.exp2(-power), extra], axis=1).astype(WIRE)

    def unpack(payload):
        got = payload.astype(jnp.float32)
        total, power = got[:, width : width + 1], got[:, width + 1 : width + 2]
        return got[:, :width] * jnp.exp2(power), total, jnp.exp2(power + 15.0)

    def send(held_rows, axis, size, bit):
        return unpack(exchange(pack(held_rows), axis, size, bit))

    def add(first, *others):
        for other in others:
            first = tuple(a + b for a, b in zip(first, other))
        return first

    def cut(held_rows, at, count):
        return tuple(value[at * count : (at + 1) * count] for value in held_rows)

    other_back = back_of(other[0], x, tables[1], shifts, 0, quads, piece_rows)
    got = send((other_back,) + other[1:], "col", cols, 1)
    per_set = quads // 2
    set_rows = per_set * piece_rows
    own_weight = own[0]
    sums, received = [], []
    for number in range(2):
        back = back_of(
            own_weight, x, tables[0], shifts, number * per_set, per_set, piece_rows
        )
        whole = add((back,) + cut(own[1:], number, set_rows), cut(got, number, set_rows))
        pieces = [cut(whole, place, piece_rows) for place in range(per_set)]
        if number:
            sums.append(pieces.pop())
        pieces = [pack(piece) for piece in pieces]
        if not number:
            *pieces, own_weight = lax.optimization_barrier((*pieces, own_weight))
        for place, piece in enumerate(pieces):
            d = number * per_set + place + 1
            received.append(unpack(exchange(piece, "col", cols, 2 * d)))
    whole = add(sums[0], *received)
    got = []
    for d in range(1, rows):
        got.append(send(cut(whole, d, local), "row", rows, d))
    summed, totals, _ = add(cut(whole, 0, local), *got)
    prior = mine.astype(jnp.float32)
    out = (summed + PRIOR_WEIGHT * prior) / (totals + PRIOR_WEIGHT)
    return unlay(out, parts)


def solution(mesh):
    return jax.shard_map(
        body,
        mesh=mesh,
        in_specs=(
            P(("row", "col"), None, None),
            P(("row", "col")),
            P(("row", "col"), None, None),
            P(),
            P(),
        ),
        out_specs=P(("row", "col"), None, None),
        check_vma=False,
    )
```
